32 devices in a mesh: ctx: 8 (over z, x), mp: 4 (over y, core).
Axes of the slice: x: 2, y: 2, z: 4, core: 2. Of those that a mesh axis runs over, the one named last changes fastest.
Arguments:
- queries: bfloat16 [2048, 3072], P('ctx', 'mp'), may hold values from -8 to 8
- keys: bfloat16 [2048, 3072], P('ctx', 'mp'), may hold values from -8 to 8
- values: bfloat16 [2048, 3072], P('ctx', 'mp'), may hold values from -6 to 6
- out_grad: bfloat16 [2048, 6144], P('ctx', 'mp'), may hold values from -6 to 6
- out_weight: bfloat16 [3072, 6144], P('mp'), may hold values from -0.078125 to 0.078125
Outputs:
- query_grad: bfloat16 [2048, 3072], P('ctx', 'mp')
- key_grad: bfloat16 [2048, 3072], P('ctx', 'mp')
- value_grad: bfloat16 [2048, 3072], P('ctx', 'mp')
The draws below stay inside these ranges and needn't reach their ends.
All inputs are finite; a program needn't handle non-finite values.
Results may differ from the reference program's by a relative error of at most 0.0076.
Values may be sent and summed in bfloat16 or wider, within the bound.
No kernel may reach another device: no remote copies, remote signals or barrier semaphores. Data moves between devices by JAX's collectives and lax.ppermute only.
A program may use at most 128 MiB of HBM per device.

```python
import jax
import jax.numpy as jnp
from jax import lax

D = 6144
HD = 128
HEADS = 24
REACH = 2
WIN = 5
TOK_DEV = 256
TOKENS = 2048


def draw_queries(key, part):
    drawn = jnp.clip(jax.random.normal(jax.random.fold_in(key, 1), (TOKENS, HEADS * HD), jnp.float32), -6.0, 6.0)
    return drawn.astype(jnp.bfloat16)


def draw_keys(key, part):
    drawn = jnp.clip(jax.random.normal(jax.random.fold_in(key, 2), (TOKENS, HEADS * HD), jnp.float32), -6.0, 6.0)
    return drawn.astype(jnp.bfloat16)


def block_scale(own_key, extent, pieces, low, top_value):
    def one(position, parts):
        heights = jax.random.uniform(jax.random.fold_in(jax.random.fold_in(own_key, 6), position), (parts,), jnp.float32, low / len(pieces), top_value / len(pieces))
        return jnp.repeat(jnp.exp(heights), extent[position] // parts).reshape((-1,) + (1,) * (len(extent) - position - 1))

    loudness = one(*pieces[0])
    for cut in pieces[1:]:
        loudness = loudness * one(*cut)
    return loudness


def scatter_about(rng, dims, spread, limit, cuts=(), held_as=jnp.bfloat16):
    values = jax.random.normal(rng, dims, jnp.float32) * spread
    if len(cuts) > 0:
        values = block_scale(rng, dims, cuts, -0.22, 0.18) * values
    return jnp.clip(values, min=-limit, max=limit).astype(held_as)


def setup_inputs(seed: int = 0) -> dict:
    key_of = jax.random.split(jax.random.key(seed), 6)
    queries = draw_queries(jax.random.fold_in(key_of[5], 71), 0)
    keys = draw_keys(jax.random.fold_in(key_of[5], 71), 0)
    values = scatter_about(key_of[2], (TOKENS, HEADS * HD), 1.0, 6.0, ((0, 8), (1, 4)))
    out_grad = scatter_about(key_of[3], (TOKENS, D), 1.0, 6.0, ((0, 8), (1, 4)))
    out_weight = scatter_about(key_of[4], (HEADS * HD, D), D ** -0.5, 0.078125, ((0, 4),))
    return {"queries": queries, "keys": keys, "values": values, "out_grad": out_grad, "out_weight": out_weight}


def banded(column, blocks):
    filler = jnp.zeros((REACH, TOK_DEV, HD), column.dtype)
    padded = jnp.concatenate([filler, column, filler], 0)
    return jnp.concatenate([padded[slot_index: slot_index + blocks] for slot_index in range(WIN)], 1)


def reference(queries, keys, values, out_grad, out_weight):
    head_grad = jnp.dot(out_grad, out_weight.T, preferred_element_type=jnp.float32).astype(jnp.bfloat16)
    blocks = TOKENS // TOK_DEV
    scaling = HD ** -0.5
    slot = jnp.arange(WIN * TOK_DEV).astype(jnp.int32) // TOK_DEV
    target = jnp.arange(blocks).astype(jnp.int32)[:, None] + slot[None, :] - REACH
    allowed = (target >= 0) & (target < blocks)
    mask = allowed[:, None, :]

    def per_head(head):
        first = (head * HD).astype(jnp.int32)

        def take(array):
            return lax.dynamic_slice_in_dim(array, first, HD, 1).reshape(blocks, TOK_DEV, HD).astype(jnp.float32)

        query_rows = take(queries)
        key_rows = take(keys)
        value_rows = take(values)
        grad_rows = take(head_grad)
        window_keys = banded(key_rows, blocks)
        window_values = banded(value_rows, blocks)
        scores = jnp.einsum('btd,bud->btu', query_rows, window_keys) * scaling
        masked = jnp.where(mask, scores, -jnp.inf)
        largest = jnp.max(masked, -1, keepdims=True)
        log_total = largest + jnp.log(jnp.sum(jnp.exp(masked - largest), -1, keepdims=True))
        probs = jnp.where(mask, jnp.exp(scores - log_total), jnp.float32(0.0))
        prob_grad = jnp.einsum('btd,bud->btu', grad_rows, window_values)
        delta_rows = jnp.sum(probs * prob_grad, -1, keepdims=True)
        score_low = lax.optimization_barrier((probs * (prob_grad - delta_rows) * scaling).astype(jnp.bfloat16))
        probs_low = lax.optimization_barrier(probs.astype(jnp.bfloat16))
        score_grad = score_low.astype(jnp.float32)
        probs_back = probs_low.astype(jnp.float32)
        query_grad = jnp.einsum('btu,bud->btd', score_grad, window_keys)
        key_parts = jnp.einsum('btu,btd->bud', score_grad, query_rows).reshape(blocks, WIN, TOK_DEV, HD)
        value_parts = jnp.einsum('btu,btd->bud', probs_back, grad_rows).reshape(blocks, WIN, TOK_DEV, HD)
        key_total = jnp.zeros((blocks, TOK_DEV, HD), jnp.float32)
        value_total = jnp.zeros((blocks, TOK_DEV, HD), jnp.float32)
        filler = jnp.zeros((REACH, TOK_DEV, HD), jnp.float32)
        for slot_index in range(WIN):
            key_term = key_parts[:, slot_index]
            value_term = value_parts[:, slot_index]
            if slot_index != REACH:
                key_term = lax.optimization_barrier(key_term.astype(jnp.bfloat16)).astype(jnp.float32)
                value_term = lax.optimization_barrier(value_term.astype(jnp.bfloat16)).astype(jnp.float32)
            key_padded = jnp.concatenate([filler, key_term, filler], 0)
            value_padded = jnp.concatenate([filler, value_term, filler], 0)
            begin = 2 * REACH - slot_index
            key_total = key_total + key_padded[begin: begin + blocks]
            value_total = value_total + value_padded[begin: begin + blocks]
        return jnp.stack([query_grad, key_total, value_total], 0).astype(jnp.bfloat16)

    results = lax.map(per_head, jnp.arange(HEADS).astype(jnp.int32))
    arranged = results.transpose(1, 2, 3, 0, 4).reshape(3, TOKENS, HEADS * HD)
    return arranged[0], arranged[1], arranged[2]
```

```python
import functools
import math

import jax
import jax.numpy as jnp
from jax import lax
from jax.experimental import pallas as pl
from jax.experimental.pallas import tpu as pltpu
from jax.sharding import PartitionSpec as P

HD = 128
BF16 = jnp.bfloat16
F32 = jnp.float32
BIG = 1e30
ANY = pl.BlockSpec(memory_space=pl.ANY)
VM = pl.BlockSpec(memory_space=pltpu.VMEM)


def params(mib=40):
    return pltpu.CompilerParams(vmem_limit_bytes=mib << 20)


def nt(a, b):
    return lax.dot_general(a, b, (((1,), (1,)), ((), ())), preferred_element_type=F32)


def nn(a, b):
    return lax.dot_general(a, b, (((1,), (0,)), ((), ())), preferred_element_type=F32)


def cost(flops, moved, exps=0):
    return pl.CostEstimate(flops=int(flops), bytes_accessed=int(moved), transcendentals=int(exps))


def all_of(copies):
    for copy in copies:
        copy.start()
    for copy in copies:
        copy.wait()


def pack_kernel(q, k, v, og, keep, send, og0, og1, sem):
    half = q.shape[1] // 2
    wide = og.shape[1] // 2
    x = lax.rem(lax.axis_index("ctx"), 2)
    mine = pl.ds(pl.multiple_of(x * half, half), half)
    theirs = pl.ds(pl.multiple_of((1 - x) * half, half), half)
    copies = []
    for i, ref in enumerate((q, k, v)):
        copies.append(pltpu.make_async_copy(ref.at[:, mine], keep.at[i], sem.at[i]))
        copies.append(pltpu.make_async_copy(ref.at[:, theirs], send.at[i], sem.at[3 + i]))
    copies.append(pltpu.make_async_copy(og.at[:, :wide], og0, sem.at[6]))
    copies.append(pltpu.make_async_copy(og.at[:, wide:], og1, sem.at[7]))
    all_of(copies)


def pack(q, k, v, og):
    rows, cols = q.shape
    part = jax.ShapeDtypeStruct((3, rows, cols // 2), BF16)
    piece = jax.ShapeDtypeStruct((rows, og.shape[1] // 2), BF16)
    return pl.pallas_call(
        pack_kernel,
        out_shape=(part, part, piece, piece),
        in_specs=[ANY] * 4,
        out_specs=(ANY,) * 4,
        scratch_shapes=[pltpu.SemaphoreType.DMA((8,))],
        cost_estimate=cost(0, 8e6),
        name="pack",
    )(q, k, v, og)


def grad_kernel(width, flips, offset, has_acc, last, *refs):
    refs = list(refs)
    acc = refs.pop(0) if has_acc else None
    pieces = [refs.pop(0), refs.pop(0)]
    w = refs.pop(0)
    outs = [refs.pop(0) for _ in range(2 if last else 1)]
    wbuf, sem = refs.pop(0), refs.pop(0)
    me = lax.axis_index("mp")
    size = pieces[0].shape[1]
    copies = []
    for i, flip in enumerate(flips):
        first = jnp.bitwise_xor(me, flip) * width + offset
        columns = pl.ds(pl.multiple_of(first, size), size)
        copies.append(pltpu.make_async_copy(w.at[:, columns], wbuf.at[i], sem.at[i]))
    for copy in copies:
        copy.start()
    copies[0].wait()
    total = nt(pieces[0][...], wbuf[0])
    copies[1].wait()
    total = total + nt(pieces[1][...], wbuf[1])
    if has_acc:
        total = total + acc[...]
    if not last:
        outs[0][...] = total
        return
    half = total.shape[1] // 2
    x = lax.rem(lax.axis_index("ctx"), 2)
    low = total[:, :half].astype(BF16)
    high = total[:, half:].astype(BF16)

    @pl.when(x == 0)
    def _():
        outs[0][...] = low
        outs[1][...] = high

    @pl.when(x != 0)
    def _():
        outs[0][...] = high
        outs[1][...] = low


def grad_piece(acc, first, second, w, width, flips, offset, last):
    rows, size = first.shape
    heads = w.shape[0]
    if last:
        shape = (jax.ShapeDtypeStruct((rows, heads // 2), BF16),) * 2
        spec = (VM, VM)
    else:
        shape = jax.ShapeDtypeStruct((rows, heads), F32)
        spec = VM
    operands = ([] if acc is None else [acc]) + [first, second, w]
    return pl.pallas_call(
        functools.partial(grad_kernel, width, flips, offset, acc is not None, last),
        out_shape=shape,
        in_specs=[VM] * (len(operands) - 1) + [ANY],
        out_specs=spec,
        scratch_shapes=[pltpu.VMEM((2, heads, size), BF16), pltpu.SemaphoreType.DMA((2,))],
        compiler_params=params(),
        cost_estimate=cost(4 * rows * size * heads, 4 * heads * size + 4 * rows * size),
        name="head_grad",
    )(*operands)


def place():
    position = lax.axis_index("ctx")
    x = lax.rem(position, 2)
    block = position // 2
    odd = lax.rem(block, 2)
    return x, block, odd


def query_kernel(scale, keep, xr, e0, e1, o0, o1, dkeep, dxr, dq_keep, dq_send, stats, qs, ks, vs, ds, marks, sem):
    rows = keep.shape[1]
    heads = keep.shape[2] // HD
    both = 2 * rows
    x, block, odd = place()
    blocks = lax.axis_size("ctx") // 2
    mine = x * rows
    theirs = (1 - x) * rows
    even_at = (1 - odd) * (2 * both)
    odd_at = odd * (2 * both)

    def at(first):
        return pl.ds(pl.multiple_of(first, rows), rows)

    copies = [
        (keep.at[0], qs.at[at(mine)]),
        (xr.at[0], qs.at[at(theirs)]),
        (dkeep, ds.at[at(mine)]),
        (dxr, ds.at[at(theirs)]),
    ]
    for i, buffer in ((1, ks), (2, vs)):
        copies.append((keep.at[i], buffer.at[at(both + mine)]))
        copies.append((xr.at[i], buffer.at[at(both + theirs)]))
        copies.append((e0.at[i], buffer.at[at(even_at + mine)]))
        copies.append((e1.at[i], buffer.at[at(even_at + theirs)]))
        copies.append((o0.at[i], buffer.at[at(odd_at + mine)]))
        copies.append((o1.at[i], buffer.at[at(odd_at + theirs)]))
    all_of([pltpu.make_async_copy(a, b, sem.at[i]) for i, (a, b) in enumerate(copies)])

    log2e = math.log2(math.e)
    c = scale * log2e
    low_off = jnp.where(block > 0, 0.0, BIG).astype(F32)
    high_off = jnp.where(block < blocks - 1, 0.0, BIG).astype(F32)
    lane = lax.broadcasted_iota(jnp.int32, (rows, HD), 1)
    for half in range(2):
        if half == 0:
            runs = ((0, both, low_off), (both, 2 * both, None), (2 * both, 2 * both + rows, high_off))
        else:
            runs = ((rows, both, low_off), (both, 2 * both, None), (2 * both, 3 * both, high_off))
        mark = jnp.zeros((rows, HD), F32)
        here = slice(half * rows, (half + 1) * rows)
        for head in range(heads):
            cols = slice(head * HD, (head + 1) * HD)
            query = qs[here, cols]
            grad = ds[here, cols]
            scores = [nt(query, ks[a:b, cols]) for a, b, _ in runs]
            top = None
            for s, (_, _, off) in zip(scores, runs):
                m = jnp.max(s, -1, keepdims=True)
                m = m if off is None else m - off
                top = m if top is None else jnp.maximum(top, m)
            top = top * c
            weights = [
                jnp.exp2(s * c - (top if off is None else top + off))
                for s, (_, _, off) in zip(scores, runs)
            ]
            total = sum(jnp.sum(w, -1, keepdims=True) for w in weights)
            grads = [nt(grad, vs[a:b, cols]) for a, b, _ in runs]
            inverse = 1.0 / total
            delta = sum(jnp.sum(w * g, -1, keepdims=True) for w, g in zip(weights, grads)) * inverse
            result = sum(
                nn((w * (g - delta)).astype(BF16), ks[a:b, cols])
                for w, g, (a, b, _) in zip(weights, grads, runs)
            )
            result = (result * (inverse * scale)).astype(BF16)

            @pl.when(x == half)
            def _():
                dq_keep[:, cols] = result

            @pl.when(x != half)
            def _():
                dq_send[:, cols] = result

            mark = jnp.where(lane == 2 * head, top + jnp.log2(total), mark)
            mark = jnp.where(lane == 2 * head + 1, delta, mark)
        stats[:, half * rows : (half + 1) * rows] = jnp.transpose(mark)[: stats.shape[0], :]


def query_pass(keep, xr, e0, e1, o0, o1, dkeep, dxr):
    _, rows, cols = keep.shape
    heads = cols // HD
    both = 2 * rows
    pairs = both * 5 * rows * heads
    part = jax.ShapeDtypeStruct((rows, cols), BF16)
    return pl.pallas_call(
        functools.partial(query_kernel, HD ** -0.5),
        out_shape=(part, part, jax.ShapeDtypeStruct((8, both), F32)),
        in_specs=[ANY] * 8,
        out_specs=(VM, VM, VM),
        scratch_shapes=[
            pltpu.VMEM((both, cols), BF16),
            pltpu.VMEM((3 * both, cols), BF16),
            pltpu.VMEM((3 * both, cols), BF16),
            pltpu.VMEM((both, cols), BF16),
            pltpu.VMEM((rows, HD), F32),
            pltpu.SemaphoreType.DMA((16,)),
        ],
        compiler_params=params(),
        cost_estimate=cost(6 * HD * pairs, 20 * rows * cols * 2, pairs),
        name="query_pass",
    )(keep, xr, e0, e1, o0, o1, dkeep, dxr)


def key_kernel(scale, keep, xr, e0, e1, o0, o1, dkeep, dxr, de0, de1, do0, do1, stats, se, so,
               out_keep, out_send, ks, vs, qs, ds, marks, sem):
    rows = keep.shape[1]
    heads = keep.shape[2] // HD
    both = 2 * rows
    x, block, odd = place()
    blocks = lax.axis_size("ctx") // 2
    mine = x * rows
    theirs = (1 - x) * rows
    even_at = (1 - odd) * (2 * both)
    odd_at = odd * (2 * both)

    def at(first):
        return pl.ds(pl.multiple_of(first, rows), rows)

    copies = []
    for i, buffer in ((1, ks), (2, vs)):
        copies.append((keep.at[i], buffer.at[at(mine)]))
        copies.append((xr.at[i], buffer.at[at(theirs)]))
    for buffer, own0, own1, a0, a1, b0, b1 in (
        (qs, keep.at[0], xr.at[0], e0.at[0], e1.at[0], o0.at[0], o1.at[0]),
        (ds, dkeep, dxr, de0, de1, do0, do1),
    ):
        copies.append((own0, buffer.at[at(both + mine)]))
        copies.append((own1, buffer.at[at(both + theirs)]))
        copies.append((a0, buffer.at[at(even_at + mine)]))
        copies.append((a1, buffer.at[at(even_at + theirs)]))
        copies.append((b0, buffer.at[at(odd_at + mine)]))
        copies.append((b1, buffer.at[at(odd_at + theirs)]))
    all_of([pltpu.make_async_copy(a, b, sem.at[i]) for i, (a, b) in enumerate(copies)])

    c = scale * math.log2(math.e)
    low_ok = block > 0
    high_ok = block < blocks - 1
    is_even = odd == 0
    low = jnp.where(is_even, so[...], se[...])
    high = jnp.where(is_even, se[...], so[...])
    row = lax.broadcasted_iota(jnp.int32, low.shape, 0)
    nothing = jnp.where(lax.rem(row, 2) == 0, jnp.float32(BIG), jnp.float32(0.0))
    marks[:, :both] = jnp.where(low_ok, low, nothing)
    marks[:, both : 2 * both] = stats[...]
    marks[:, 2 * both :] = jnp.where(high_ok, high, nothing)

    for half in range(2):
        here = slice(half * rows, (half + 1) * rows)
        for head in range(heads):
            cols = slice(head * HD, (head + 1) * HD)
            key = ks[here, cols]
            value = vs[here, cols]
            key_sum = None
            value_sum = None
            for step in range(5):
                span = slice((half + step) * rows, (half + step + 1) * rows)
                query = qs[span, cols]
                grad = ds[span, cols]
                weight = jnp.exp2(nt(key, query) * c - marks[2 * head : 2 * head + 1, span])
                change = weight * (nt(value, grad) - marks[2 * head + 1 : 2 * head + 2, span])
                v = nn(weight.astype(BF16), grad)
                k = nn(change.astype(BF16), query)
                value_sum = v if value_sum is None else value_sum + v
                key_sum = k if key_sum is None else key_sum + k
            key_out = (key_sum * scale).astype(BF16)
            value_out = value_sum.astype(BF16)

            @pl.when(x == half)
            def _():
                out_keep[0, :, cols] = key_out
                out_keep[1, :, cols] = value_out

            @pl.when(x != half)
            def _():
                out_send[0, :, cols] = key_out
                out_send[1, :, cols] = value_out


def key_pass(*operands):
    _, rows, cols = operands[0].shape
    heads = cols // HD
    both = 2 * rows
    pairs = both * 5 * rows * heads
    part = jax.ShapeDtypeStruct((2, rows, cols), BF16)
    return pl.pallas_call(
        functools.partial(key_kernel, HD ** -0.5),
        out_shape=(part, part),
        in_specs=[ANY] * 12 + [VM] * 3,
        out_specs=(VM, VM),
        scratch_shapes=[
            pltpu.VMEM((both, cols), BF16),
            pltpu.VMEM((both, cols), BF16),
            pltpu.VMEM((3 * both, cols), BF16),
            pltpu.VMEM((3 * both, cols), BF16),
            pltpu.VMEM((8, 3 * both), F32),
            pltpu.SemaphoreType.DMA((16,)),
        ],
        compiler_params=params(),
        cost_estimate=cost(8 * HD * pairs, 20 * rows * cols * 2, pairs),
        name="key_pass",
    )(*operands)


def unpack_kernel(q_keep, q_got, kv_keep, kv_got, dq, dk, dv, sem):
    half = q_keep.shape[1]
    x = lax.rem(lax.axis_index("ctx"), 2)
    mine = pl.ds(pl.multiple_of(x * half, half), half)
    theirs = pl.ds(pl.multiple_of((1 - x) * half, half), half)
    pairs = [
        (q_keep, dq.at[:, mine]),
        (q_got, dq.at[:, theirs]),
        (kv_keep.at[0], dk.at[:, mine]),
        (kv_got.at[0], dk.at[:, theirs]),
        (kv_keep.at[1], dv.at[:, mine]),
        (kv_got.at[1], dv.at[:, theirs]),
    ]
    all_of([pltpu.make_async_copy(a, b, sem.at[i]) for i, (a, b) in enumerate(pairs)])


def unpack(q_keep, q_got, kv_keep, kv_got):
    rows, half = q_keep.shape
    whole = jax.ShapeDtypeStruct((rows, 2 * half), BF16)
    return pl.pallas_call(
        unpack_kernel,
        out_shape=(whole,) * 3,
        in_specs=[ANY] * 4,
        out_specs=(ANY,) * 3,
        scratch_shapes=[pltpu.SemaphoreType.DMA((6,))],
        cost_estimate=cost(0, 3 * rows * half * 8),
        name="unpack",
    )(q_keep, q_got, kv_keep, kv_got)


def body(queries, keys, values, out_grad, out_weight):
    length = lax.axis_size("ctx")
    lanes = lax.axis_size("mp")
    blocks = length // 2
    width = out_grad.shape[1]

    def over_mp(array, flip):
        return lax.ppermute(array, "mp", [(i, i ^ flip) for i in range(lanes)])

    def over_x(array):
        return lax.ppermute(array, "ctx", [(i, i ^ 1) for i in range(length)])

    def over_z(array, first):
        pairs = []
        for position in range(length):
            block = position // 2
            other = ((block - first) ^ 1) + first
            for lane in range(lanes):
                source = position * lanes + lane
                if block >= first and other < blocks:
                    target = (2 * other + position % 2) * lanes + lane
                else:
                    target = position * lanes + (lane ^ 1)
                pairs.append((source, target))
        return lax.ppermute(array, ("ctx", "mp"), pairs)

    keep, send, og0, og1 = pack(queries, keys, values, out_grad)
    e0, o0 = over_z(keep, 0), over_z(keep, 1)
    y0 = over_mp(og0, 2)
    xr = over_x(send)
    y1 = over_mp(og1, 2)
    near = over_mp(out_grad, 1)
    acc = grad_piece(None, out_grad, near, out_weight, width, (0, 1), 0, False)
    e1, o1 = over_z(xr, 0), over_z(xr, 1)
    far0 = over_mp(y0, 1)
    acc = grad_piece(acc, y0, far0, out_weight, width, (2, 3), 0, False)
    far1 = over_mp(y1, 1)
    dkeep, dsend = grad_piece(acc, y1, far1, out_weight, width, (2, 3), width // 2, True)
    dxr = over_x(dsend)
    de0, do0 = over_z(dkeep, 0), over_z(dkeep, 1)
    dq_keep, dq_send, stats = query_pass(keep, xr, e0, e1, o0, o1, dkeep, dxr)
    de1, do1 = over_z(dxr, 0), over_z(dxr, 1)
    se, so = over_z(stats, 0), over_z(stats, 1)
    dq_got = over_x(dq_send)
    kv_keep, kv_send = key_pass(
        keep, xr, e0, e1, o0, o1, dkeep, dxr, de0, de1, do0, do1, stats, se, so
    )
    kv_got = over_x(kv_send)
    return tuple(unpack(dq_keep, dq_got, kv_keep, kv_got))


def solution(mesh):
    placed = (P("ctx", "mp"), P("ctx", "mp"), P("ctx", "mp"), P("ctx", "mp"), P("mp", None))
    return jax.shard_map(
        body,
        mesh=mesh,
        in_specs=placed,
        out_specs=(P("ctx", "mp"), P("ctx", "mp"), P("ctx", "mp")),
        check_vma=False,
    )
```

```python
import functools
import math

import jax
import jax.numpy as jnp
from jax import lax
from jax.experimental import pallas as pl
from jax.experimental.pallas import tpu as pltpu
from jax.sharding import PartitionSpec as P

HD = 128
BF16 = jnp.bfloat16
F32 = jnp.float32
BIG = 1e30
ANY = pl.BlockSpec(memory_space=pl.ANY)
VM = pl.BlockSpec(memory_space=pltpu.VMEM)
HBM = pl.BlockSpec(memory_space=pltpu.HBM)


def params(mib=40):
    return pltpu.CompilerParams(vmem_limit_bytes=mib << 20)


def nt(a, b):
    return lax.dot_general(a, b, (((1,), (1,)), ((), ())), preferred_element_type=F32)


def nn(a, b):
    return lax.dot_general(a, b, (((1,), (0,)), ((), ())), preferred_element_type=F32)


def cost(flops, moved, exps=0):
    return pl.CostEstimate(flops=int(flops), bytes_accessed=int(moved), transcendentals=int(exps))


def all_of(copies):
    for copy in copies:
        copy.start()
    for copy in copies:
        copy.wait()


def pack_kernel(q, k, v, og, keep, send, og0, og1, sem):
    half = q.shape[1] // 2
    wide = og.shape[1] // 2
    x = lax.rem(lax.axis_index("ctx"), 2)
    mine = pl.ds(pl.multiple_of(x * half, half), half)
    theirs = pl.ds(pl.multiple_of((1 - x) * half, half), half)
    copies = []
    for i, ref in enumerate((q, k, v)):
        copies.append(pltpu.make_async_copy(ref.at[:, mine], keep.at[i], sem.at[i]))
        copies.append(pltpu.make_async_copy(ref.at[:, theirs], send.at[i], sem.at[3 + i]))
    copies.append(pltpu.make_async_copy(og.at[:, :wide], og0, sem.at[6]))
    copies.append(pltpu.make_async_copy(og.at[:, wide:], og1, sem.at[7]))
    all_of(copies)


def pack(q, k, v, og):
    rows, cols = q.shape
    part = jax.ShapeDtypeStruct((3, rows, cols // 2), BF16)
    piece = jax.ShapeDtypeStruct((rows, og.shape[1] // 2), BF16)
    return pl.pallas_call(
        pack_kernel,
        out_shape=(part, part, piece, piece),
        in_specs=[ANY] * 4,
        out_specs=(VM,) * 4,
        scratch_shapes=[pltpu.SemaphoreType.DMA((8,))],
        cost_estimate=cost(0, 8e6),
        name="pack",
    )(q, k, v, og)


def grad_kernel(width, flips, offset, has_acc, last, *refs):
    refs = list(refs)
    acc = refs.pop(0) if has_acc else None
    pieces = [refs.pop(0), refs.pop(0)]
    w = refs.pop(0)
    outs = [refs.pop(0) for _ in range(2 if last else 1)]
    wbuf, sem = refs.pop(0), refs.pop(0)
    me = lax.axis_index("mp")
    size = pieces[0].shape[1]
    copies = []
    for i, flip in enumerate(flips):
        first = jnp.bitwise_xor(me, flip) * width + offset
        columns = pl.ds(pl.multiple_of(first, size), size)
        copies.append(pltpu.make_async_copy(w.at[:, columns], wbuf.at[i], sem.at[i]))
    for copy in copies:
        copy.start()
    copies[0].wait()
    total = nt(pieces[0][...], wbuf[0])
    copies[1].wait()
    total = total + nt(pieces[1][...], wbuf[1])
    if has_acc:
        total = total + acc[...]
    if not last:
        outs[0][...] = total
        return
    half = total.shape[1] // 2
    x = lax.rem(lax.axis_index("ctx"), 2)
    low = total[:, :half].astype(BF16)
    high = total[:, half:].astype(BF16)

    @pl.when(x == 0)
    def _():
        outs[0][...] = low
        outs[1][...] = high

    @pl.when(x != 0)
    def _():
        outs[0][...] = high
        outs[1][...] = low


def grad_piece(acc, first, second, w, width, flips, offset, last):
    rows, size = first.shape
    heads = w.shape[0]
    if last:
        shape = (jax.ShapeDtypeStruct((rows, heads // 2), BF16),) * 2
        spec = (VM, VM)
    else:
        shape = jax.ShapeDtypeStruct((rows, heads), F32)
        spec = VM
    operands = ([] if acc is None else [acc]) + [first, second, w]
    return pl.pallas_call(
        functools.partial(grad_kernel, width, flips, offset, acc is not None, last),
        out_shape=shape,
        in_specs=[VM] * (len(operands) - 1) + [HBM],
        out_specs=spec,
        scratch_shapes=[pltpu.VMEM((2, heads, size), BF16), pltpu.SemaphoreType.DMA((2,))],
        compiler_params=params(),
        cost_estimate=cost(4 * rows * size * heads, 4 * heads * size + 4 * rows * size),
        name="head_grad",
    )(*operands)


def place():
    position = lax.axis_index("ctx")
    x = lax.rem(position, 2)
    block = position // 2
    odd = lax.rem(block, 2)
    return x, block, odd


def query_kernel(scale, keep, xr, e0, e1, o0, o1, dkeep, dxr, dq_keep, dq_send, stats, qs, ks, vs, ds, marks, sem):
    rows = keep.shape[1]
    heads = keep.shape[2] // HD
    both = 2 * rows
    x, block, odd = place()
    blocks = lax.axis_size("ctx") // 2
    mine = x * rows
    theirs = (1 - x) * rows
    even_at = (1 - odd) * (2 * both)
    odd_at = odd * (2 * both)

    def at(first):
        return pl.ds(pl.multiple_of(first, rows), rows)

    copies = [
        (keep.at[0], qs.at[at(mine)]),
        (xr.at[0], qs.at[at(theirs)]),
        (dkeep, ds.at[at(mine)]),
        (dxr, ds.at[at(theirs)]),
    ]
    for i, buffer in ((1, ks), (2, vs)):
        copies.append((keep.at[i], buffer.at[at(both + mine)]))
        copies.append((xr.at[i], buffer.at[at(both + theirs)]))
        copies.append((e0.at[i], buffer.at[at(even_at + mine)]))
        copies.append((e1.at[i], buffer.at[at(even_at + theirs)]))
        copies.append((o0.at[i], buffer.at[at(odd_at + mine)]))
        copies.append((o1.at[i], buffer.at[at(odd_at + theirs)]))
    all_of([pltpu.make_async_copy(a, b, sem.at[i]) for i, (a, b) in enumerate(copies)])

    log2e = math.log2(math.e)
    c = scale * log2e
    low_off = jnp.where(block > 0, 0.0, BIG).astype(F32)
    high_off = jnp.where(block < blocks - 1, 0.0, BIG).astype(F32)
    lane = lax.broadcasted_iota(jnp.int32, (rows, HD), 1)
    for half in range(2):
        if half == 0:
            runs = ((0, both, low_off), (both, 2 * both, None), (2 * both, 2 * both + rows, high_off))
        else:
            runs = ((rows, both, low_off), (both, 2 * both, None), (2 * both, 3 * both, high_off))
        mark = jnp.zeros((rows, HD), F32)
        here = slice(half * rows, (half + 1) * rows)
        for head in range(heads):
            cols = slice(head * HD, (head + 1) * HD)
            query = qs[here, cols]
            grad = ds[here, cols]
            scores = [nt(query, ks[a:b, cols]) for a, b, _ in runs]
            top = None
            for s, (_, _, off) in zip(scores, runs):
                m = jnp.max(s, -1, keepdims=True)
                m = m if off is None else m - off
                top = m if top is None else jnp.maximum(top, m)
            top = top * c
            weights = [
                jnp.exp2(s * c - (top if off is None else top + off))
                for s, (_, _, off) in zip(scores, runs)
            ]
            total = sum(jnp.sum(w, -1, keepdims=True) for w in weights)
            grads = [nt(grad, vs[a:b, cols]) for a, b, _ in runs]
            inverse = 1.0 / total
            delta = sum(jnp.sum(w * g, -1, keepdims=True) for w, g in zip(weights, grads)) * inverse
            result = sum(
                nn((w * (g - delta)).astype(BF16), ks[a:b, cols])
                for w, g, (a, b, _) in zip(weights, grads, runs)
            )
            result = (result * (inverse * scale)).astype(BF16)

            @pl.when(x == half)
            def _():
                dq_keep[:, cols] = result

            @pl.when(x != half)
            def _():
                dq_send[:, cols] = result

            mark = jnp.where(lane == 2 * head, top + jnp.log2(total), mark)
            mark = jnp.where(lane == 2 * head + 1, delta, mark)
        stats[:, half * rows : (half + 1) * rows] = jnp.transpose(mark)[: stats.shape[0], :]


def query_pass(keep, xr, e0, e1, o0, o1, dkeep, dxr):
    _, rows, cols = keep.shape
    heads = cols // HD
    both = 2 * rows
    pairs = both * 5 * rows * heads
    part = jax.ShapeDtypeStruct((rows, cols), BF16)
    return pl.pallas_call(
        functools.partial(query_kernel, HD ** -0.5),
        out_shape=(part, part, jax.ShapeDtypeStruct((8, both), F32)),
        in_specs=[ANY] * 8,
        out_specs=(VM, VM, VM),
        scratch_shapes=[
            pltpu.VMEM((both, cols), BF16),
            pltpu.VMEM((3 * both, cols), BF16),
            pltpu.VMEM((3 * both, cols), BF16),
            pltpu.VMEM((both, cols), BF16),
            pltpu.VMEM((rows, HD), F32),
            pltpu.SemaphoreType.DMA((16,)),
        ],
        compiler_params=params(),
        cost_estimate=cost(6 * HD * pairs, 20 * rows * cols * 2, pairs),
        name="query_pass",
    )(keep, xr, e0, e1, o0, o1, dkeep, dxr)


def key_kernel(scale, keep, xr, e0, e1, o0, o1, dkeep, dxr, de0, de1, do0, do1, stats, se, so,
               out_keep, out_send, ks, vs, qs, ds, marks, sem):
    rows = keep.shape[1]
    heads = keep.shape[2] // HD
    both = 2 * rows
    x, block, odd = place()
    blocks = lax.axis_size("ctx") // 2
    mine = x * rows
    theirs = (1 - x) * rows
    even_at = (1 - odd) * (2 * both)
    odd_at = odd * (2 * both)

    def at(first):
        return pl.ds(pl.multiple_of(first, rows), rows)

    copies = []
    for i, buffer in ((1, ks), (2, vs)):
        copies.append((keep.at[i], buffer.at[at(mine)]))
        copies.append((xr.at[i], buffer.at[at(theirs)]))
    for buffer, own0, own1, a0, a1, b0, b1 in (
        (qs, keep.at[0], xr.at[0], e0.at[0], e1.at[0], o0.at[0], o1.at[0]),
        (ds, dkeep, dxr, de0, de1, do0, do1),
    ):
        copies.append((own0, buffer.at[at(both + mine)]))
        copies.append((own1, buffer.at[at(both + theirs)]))
        copies.append((a0, buffer.at[at(even_at + mine)]))
        copies.append((a1, buffer.at[at(even_at + theirs)]))
        copies.append((b0, buffer.at[at(odd_at + mine)]))
        copies.append((b1, buffer.at[at(odd_at + theirs)]))
    all_of([pltpu.make_async_copy(a, b, sem.at[i]) for i, (a, b) in enumerate(copies)])

    c = scale * math.log2(math.e)
    low_ok = block > 0
    high_ok = block < blocks - 1
    is_even = odd == 0
    low = jnp.where(is_even, so[...], se[...])
    high = jnp.where(is_even, se[...], so[...])
    row = lax.broadcasted_iota(jnp.int32, low.shape, 0)
    nothing = jnp.where(lax.rem(row, 2) == 0, jnp.float32(BIG), jnp.float32(0.0))
    marks[:, :both] = jnp.where(low_ok, low, nothing)
    marks[:, both : 2 * both] = stats[...]
    marks[:, 2 * both :] = jnp.where(high_ok, high, nothing)

    for half in range(2):
        here = slice(half * rows, (half + 1) * rows)
        for head in range(heads):
            cols = slice(head * HD, (head + 1) * HD)
            key = ks[here, cols]
            value = vs[here, cols]
            key_sum = None
            value_sum = None
            for step in range(5):
                span = slice((half + step) * rows, (half + step + 1) * rows)
                query = qs[span, cols]
                grad = ds[span, cols]
                weight = jnp.exp2(nt(key, query) * c - marks[2 * head : 2 * head + 1, span])
                change = weight * (nt(value, grad) - marks[2 * head + 1 : 2 * head + 2, span])
                v = nn(weight.astype(BF16), grad)
                k = nn(change.astype(BF16), query)
                value_sum = v if value_sum is None else value_sum + v
                key_sum = k if key_sum is None else key_sum + k
            key_out = (key_sum * scale).astype(BF16)
            value_out = value_sum.astype(BF16)

            @pl.when(x == half)
            def _():
                out_keep[0, :, cols] = key_out
                out_keep[1, :, cols] = value_out

            @pl.when(x != half)
            def _():
                out_send[0, :, cols] = key_out
                out_send[1, :, cols] = value_out


def key_pass(*operands):
    _, rows, cols = operands[0].shape
    heads = cols // HD
    both = 2 * rows
    pairs = both * 5 * rows * heads
    part = jax.ShapeDtypeStruct((2, rows, cols), BF16)
    return pl.pallas_call(
        functools.partial(key_kernel, HD ** -0.5),
        out_shape=(part, part),
        in_specs=[ANY] * 12 + [VM] * 3,
        out_specs=(VM, VM),
        scratch_shapes=[
            pltpu.VMEM((both, cols), BF16),
            pltpu.VMEM((both, cols), BF16),
            pltpu.VMEM((3 * both, cols), BF16),
            pltpu.VMEM((3 * both, cols), BF16),
            pltpu.VMEM((8, 3 * both), F32),
            pltpu.SemaphoreType.DMA((16,)),
        ],
        compiler_params=params(),
        cost_estimate=cost(8 * HD * pairs, 20 * rows * cols * 2, pairs),
        name="key_pass",
    )(*operands)


def unpack_kernel(q_keep, q_got, kv_keep, kv_got, dq, dk, dv, sem):
    half = q_keep.shape[1]
    x = lax.rem(lax.axis_index("ctx"), 2)
    mine = pl.ds(pl.multiple_of(x * half, half), half)
    theirs = pl.ds(pl.multiple_of((1 - x) * half, half), half)
    pairs = [
        (q_keep, dq.at[:, mine]),
        (q_got, dq.at[:, theirs]),
        (kv_keep.at[0], dk.at[:, mine]),
        (kv_got.at[0], dk.at[:, theirs]),
        (kv_keep.at[1], dv.at[:, mine]),
        (kv_got.at[1], dv.at[:, theirs]),
    ]
    all_of([pltpu.make_async_copy(a, b, sem.at[i]) for i, (a, b) in enumerate(pairs)])


def unpack(q_keep, q_got, kv_keep, kv_got):
    rows, half = q_keep.shape
    whole = jax.ShapeDtypeStruct((rows, 2 * half), BF16)
    return pl.pallas_call(
        unpack_kernel,
        out_shape=(whole,) * 3,
        in_specs=[ANY] * 4,
        out_specs=(VM,) * 3,
        scratch_shapes=[pltpu.SemaphoreType.DMA((6,))],
        cost_estimate=cost(0, 3 * rows * half * 8),
        name="unpack",
    )(q_keep, q_got, kv_keep, kv_got)


def body(queries, keys, values, out_grad, out_weight):
    length = lax.axis_size("ctx")
    lanes = lax.axis_size("mp")
    blocks = length // 2
    width = out_grad.shape[1]

    def over_mp(array, flip):
        return lax.ppermute(array, "mp", [(i, i ^ flip) for i in range(lanes)])

    def over_x(array):
        return lax.ppermute(array, "ctx", [(i, i ^ 1) for i in range(length)])

    def over_z(array, first):
        pairs = []
        for position in range(length):
            block = position // 2
            other = ((block - first) ^ 1) + first
            for lane in range(lanes):
                source = position * lanes + lane
                if block >= first and other < blocks:
                    target = (2 * other + position % 2) * lanes + lane
                else:
                    target = position * lanes + (lane ^ 1)
                pairs.append((source, target))
        return lax.ppermute(array, ("ctx", "mp"), pairs)

    keep, send, og0, og1 = pack(queries, keys, values, out_grad)
    e0, o0 = over_z(keep, 0), over_z(keep, 1)
    y0 = over_mp(og0, 2)
    xr = over_x(send)
    y1 = over_mp(og1, 2)
    near = over_mp(out_grad, 1)
    acc = grad_piece(None, out_grad, near, out_weight, width, (0, 1), 0, False)
    e1, o1 = over_z(xr, 0), over_z(xr, 1)
    far0 = over_mp(y0, 1)
    acc = grad_piece(acc, y0, far0, out_weight, width, (2, 3), 0, False)
    far1 = over_mp(y1, 1)
    dkeep, dsend = grad_piece(acc, y1, far1, out_weight, width, (2, 3), width // 2, True)
    dxr = over_x(dsend)
    de0, do0 = over_z(dkeep, 0), over_z(dkeep, 1)
    dq_keep, dq_send, stats = query_pass(keep, xr, e0, e1, o0, o1, dkeep, dxr)
    de1, do1 = over_z(dxr, 0), over_z(dxr, 1)
    se, so = over_z(stats, 0), over_z(stats, 1)
    dq_got = over_x(dq_send)
    kv_keep, kv_send = key_pass(
        keep, xr, e0, e1, o0, o1, dkeep, dxr, de0, de1, do0, do1, stats, se, so
    )
    kv_got = over_x(kv_send)
    return tuple(unpack(dq_keep, dq_got, kv_keep, kv_got))


def solution(mesh):
    placed = (P("ctx", "mp"), P("ctx", "mp"), P("ctx", "mp"), P("ctx", "mp"), P("mp", None))
    return jax.shard_map(
        body,
        mesh=mesh,
        in_specs=placed,
        out_specs=(P("ctx", "mp"), P("ctx", "mp"), P("ctx", "mp")),
        check_vma=False,
    )
```

```python
import functools
import math

import jax
import jax.numpy as jnp
from jax import lax
from jax.experimental import pallas as pl
from jax.experimental.pallas import tpu as pltpu
from jax.sharding import PartitionSpec as P

HD = 128
BF16 = jnp.bfloat16
F32 = jnp.float32
BIG = 1e30
ANY = pl.BlockSpec(memory_space=pl.ANY)
VM = pl.BlockSpec(memory_space=pltpu.VMEM)
HBM = pl.BlockSpec(memory_space=pltpu.HBM)


def params(mib=40):
    return pltpu.CompilerParams(vmem_limit_bytes=mib << 20)


def nt(a, b):
    return lax.dot_general(a, b, (((1,), (1,)), ((), ())), preferred_element_type=F32)


def nn(a, b):
    return lax.dot_general(a, b, (((1,), (0,)), ((), ())), preferred_element_type=F32)


def cost():
    return pl.CostEstimate(flops=1, bytes_accessed=1, transcendentals=0)


def all_of(copies):
    for copy in copies:
        copy.start()
    for copy in copies:
        copy.wait()


def pack_kernel(q, k, v, og, keep, send, og0, og1, sem):
    half = q.shape[1] // 2
    wide = og.shape[1] // 2
    x = lax.rem(lax.axis_index("ctx"), 2)
    mine = pl.ds(pl.multiple_of(x * half, half), half)
    theirs = pl.ds(pl.multiple_of((1 - x) * half, half), half)
    copies = []
    for i, ref in enumerate((q, k, v)):
        copies.append(pltpu.make_async_copy(ref.at[:, mine], keep.at[i], sem.at[i]))
        copies.append(pltpu.make_async_copy(ref.at[:, theirs], send.at[i], sem.at[3 + i]))
    copies.append(pltpu.make_async_copy(og.at[:, :wide], og0, sem.at[6]))
    copies.append(pltpu.make_async_copy(og.at[:, wide:], og1, sem.at[7]))
    all_of(copies)


def pack(q, k, v, og):
    rows, cols = q.shape
    part = jax.ShapeDtypeStruct((3, rows, cols // 2), BF16)
    piece = jax.ShapeDtypeStruct((rows, og.shape[1] // 2), BF16)
    return pl.pallas_call(
        pack_kernel,
        out_shape=(part, part, piece, piece),
        in_specs=[ANY] * 4,
        out_specs=(VM,) * 4,
        scratch_shapes=[pltpu.SemaphoreType.DMA((8,))],
        compiler_params=params(16),
        cost_estimate=cost(),
        name="pack",
    )(q, k, v, og)


def grad_kernel(width, flips, offset, has_acc, last, *refs):
    refs = list(refs)
    acc = refs.pop(0) if has_acc else None
    pieces = [refs.pop(0), refs.pop(0)]
    w = refs.pop(0)
    outs = [refs.pop(0) for _ in range(2 if last else 1)]
    wbuf, sem = refs.pop(0), refs.pop(0)
    me = lax.axis_index("mp")
    size = pieces[0].shape[1]
    copies = []
    for i, flip in enumerate(flips):
        first = jnp.bitwise_xor(me, flip) * width + offset
        columns = pl.ds(pl.multiple_of(first, size), size)
        copies.append(pltpu.make_async_copy(w.at[:, columns], wbuf.at[i], sem.at[i]))
    for copy in copies:
        copy.start()
    copies[0].wait()
    total = nt(pieces[0][...], wbuf[0])
    copies[1].wait()
    total = total + nt(pieces[1][...], wbuf[1])
    if has_acc:
        total = total + acc[...]
    if not last:
        outs[0][...] = total
        return
    half = total.shape[1] // 2
    x = lax.rem(lax.axis_index("ctx"), 2)
    low = total[:, :half].astype(BF16)
    high = total[:, half:].astype(BF16)

    @pl.when(x == 0)
    def _():
        outs[0][...] = low
        outs[1][...] = high

    @pl.when(x != 0)
    def _():
        outs[0][...] = high
        outs[1][...] = low


def grad_piece(acc, first, second, w, width, flips, offset, last):
    rows, size = first.shape
    heads = w.shape[0]
    if last:
        shape = (jax.ShapeDtypeStruct((rows, heads // 2), BF16),) * 2
        spec = (VM, VM)
    else:
        shape = jax.ShapeDtypeStruct((rows, heads), F32)
        spec = VM
    operands = ([] if acc is None else [acc]) + [first, second, w]
    return pl.pallas_call(
        functools.partial(grad_kernel, width, flips, offset, acc is not None, last),
        out_shape=shape,
        in_specs=[VM] * (len(operands) - 1) + [HBM],
        out_specs=spec,
        scratch_shapes=[pltpu.VMEM((2, heads, size), BF16), pltpu.SemaphoreType.DMA((2,))],
        compiler_params=params(50),
        cost_estimate=cost(),
        name="head_grad",
    )(*operands)


def place():
    position = lax.axis_index("ctx")
    x = lax.rem(position, 2)
    block = position // 2
    odd = lax.rem(block, 2)
    return x, block, odd


def query_kernel(scale, keep, xr, e0, e1, o0, o1, dkeep, dxr, dq_keep, dq_send, stats, qs, ks, vs, ds, marks, sem):
    rows = keep.shape[1]
    heads = keep.shape[2] // HD
    both = 2 * rows
    x, block, odd = place()
    blocks = lax.axis_size("ctx") // 2
    mine = x * rows
    theirs = (1 - x) * rows
    even_at = (1 - odd) * (2 * both)
    odd_at = odd * (2 * both)

    def at(first):
        return pl.ds(pl.multiple_of(first, rows), rows)

    copies = [
        (keep.at[0], qs.at[at(mine)]),
        (xr.at[0], qs.at[at(theirs)]),
        (dkeep, ds.at[at(mine)]),
        (dxr, ds.at[at(theirs)]),
    ]
    for i, buffer in ((1, ks), (2, vs)):
        copies.append((keep.at[i], buffer.at[at(both + mine)]))
        copies.append((xr.at[i], buffer.at[at(both + theirs)]))
        copies.append((e0.at[i], buffer.at[at(even_at + mine)]))
        copies.append((e1.at[i], buffer.at[at(even_at + theirs)]))
        copies.append((o0.at[i], buffer.at[at(odd_at + mine)]))
        copies.append((o1.at[i], buffer.at[at(odd_at + theirs)]))
    all_of([pltpu.make_async_copy(a, b, sem.at[i]) for i, (a, b) in enumerate(copies)])

    log2e = math.log2(math.e)
    c = scale * log2e
    low_off = jnp.where(block > 0, 0.0, BIG).astype(F32)
    high_off = jnp.where(block < blocks - 1, 0.0, BIG).astype(F32)
    lane = lax.broadcasted_iota(jnp.int32, (rows, HD), 1)
    for half in range(2):
        if half == 0:
            runs = ((0, both, low_off), (both, 2 * both, None), (2 * both, 2 * both + rows, high_off))
        else:
            runs = ((rows, both, low_off), (both, 2 * both, None), (2 * both, 3 * both, high_off))
        mark = jnp.zeros((rows, HD), F32)
        here = slice(half * rows, (half + 1) * rows)
        for head in range(heads):
            cols = slice(head * HD, (head + 1) * HD)
            query = qs[here, cols]
            grad = ds[here, cols]
            scores = [nt(query, ks[a:b, cols]) for a, b, _ in runs]
            top = None
            for s, (_, _, off) in zip(scores, runs):
                m = jnp.max(s, -1, keepdims=True)
                m = m if off is None else m - off
                top = m if top is None else jnp.maximum(top, m)
            top = top * c
            weights = [
                jnp.exp2(s * c - (top if off is None else top + off))
                for s, (_, _, off) in zip(scores, runs)
            ]
            total = sum(jnp.sum(w, -1, keepdims=True) for w in weights)
            grads = [nt(grad, vs[a:b, cols]) for a, b, _ in runs]
            inverse = 1.0 / total
            delta = sum(jnp.sum(w * g, -1, keepdims=True) for w, g in zip(weights, grads)) * inverse
            result = sum(
                nn((w * (g - delta)).astype(BF16), ks[a:b, cols])
                for w, g, (a, b, _) in zip(weights, grads, runs)
            )
            result = (result * (inverse * scale)).astype(BF16)

            @pl.when(x == half)
            def _():
                dq_keep[:, cols] = result

            @pl.when(x != half)
            def _():
                dq_send[:, cols] = result

            mark = jnp.where(lane == 2 * head, top + jnp.log2(total), mark)
            mark = jnp.where(lane == 2 * head + 1, delta, mark)
        stats[:, half * rows : (half + 1) * rows] = jnp.transpose(mark)[: stats.shape[0], :]


def query_pass(keep, xr, e0, e1, o0, o1, dkeep, dxr):
    _, rows, cols = keep.shape
    heads = cols // HD
    both = 2 * rows
    pairs = both * 5 * rows * heads
    part = jax.ShapeDtypeStruct((rows, cols), BF16)
    return pl.pallas_call(
        functools.partial(query_kernel, HD ** -0.5),
        out_shape=(part, part, jax.ShapeDtypeStruct((8, both), F32)),
        in_specs=[ANY] * 8,
        out_specs=(VM, VM, VM),
        scratch_shapes=[
            pltpu.VMEM((both, cols), BF16),
            pltpu.VMEM((3 * both, cols), BF16),
            pltpu.VMEM((3 * both, cols), BF16),
            pltpu.VMEM((both, cols), BF16),
            pltpu.VMEM((rows, HD), F32),
            pltpu.SemaphoreType.DMA((16,)),
        ],
        compiler_params=params(),
        cost_estimate=cost(),
        name="query_pass",
    )(keep, xr, e0, e1, o0, o1, dkeep, dxr)


def key_kernel(scale, keep, xr, e0, e1, o0, o1, dkeep, dxr, de0, de1, do0, do1, stats, se, so,
               out_keep, out_send, ks, vs, qs, ds, marks, sem):
    rows = keep.shape[1]
    heads = keep.shape[2] // HD
    both = 2 * rows
    x, block, odd = place()
    blocks = lax.axis_size("ctx") // 2
    mine = x * rows
    theirs = (1 - x) * rows
    even_at = (1 - odd) * (2 * both)
    odd_at = odd * (2 * both)

    def at(first):
        return pl.ds(pl.multiple_of(first, rows), rows)

    copies = []
    for i, buffer in ((1, ks), (2, vs)):
        copies.append((keep.at[i], buffer.at[at(mine)]))
        copies.append((xr.at[i], buffer.at[at(theirs)]))
    for buffer, own0, own1, a0, a1, b0, b1 in (
        (qs, keep.at[0], xr.at[0], e0.at[0], e1.at[0], o0.at[0], o1.at[0]),
        (ds, dkeep, dxr, de0, de1, do0, do1),
    ):
        copies.append((own0, buffer.at[at(both + mine)]))
        copies.append((own1, buffer.at[at(both + theirs)]))
        copies.append((a0, buffer.at[at(even_at + mine)]))
        copies.append((a1, buffer.at[at(even_at + theirs)]))
        copies.append((b0, buffer.at[at(odd_at + mine)]))
        copies.append((b1, buffer.at[at(odd_at + theirs)]))
    all_of([pltpu.make_async_copy(a, b, sem.at[i]) for i, (a, b) in enumerate(copies)])

    c = scale * math.log2(math.e)
    low_ok = block > 0
    high_ok = block < blocks - 1
    is_even = odd == 0
    low = jnp.where(is_even, so[...], se[...])
    high = jnp.where(is_even, se[...], so[...])
    row = lax.broadcasted_iota(jnp.int32, low.shape, 0)
    nothing = jnp.where(lax.rem(row, 2) == 0, jnp.float32(BIG), jnp.float32(0.0))
    marks[:, :both] = jnp.where(low_ok, low, nothing)
    marks[:, both : 2 * both] = stats[...]
    marks[:, 2 * both :] = jnp.where(high_ok, high, nothing)

    for half in range(2):
        here = slice(half * rows, (half + 1) * rows)
        for head in range(heads):
            cols = slice(head * HD, (head + 1) * HD)
            key = ks[here, cols]
            value = vs[here, cols]
            key_sum = None
            value_sum = None
            for step in range(5):
                span = slice((half + step) * rows, (half + step + 1) * rows)
                query = qs[span, cols]
                grad = ds[span, cols]
                weight = jnp.exp2(nt(key, query) * c - marks[2 * head : 2 * head + 1, span])
                change = weight * (nt(value, grad) - marks[2 * head + 1 : 2 * head + 2, span])
                v = nn(weight.astype(BF16), grad)
                k = nn(change.astype(BF16), query)
                value_sum = v if value_sum is None else value_sum + v
                key_sum = k if key_sum is None else key_sum + k
            key_out = (key_sum * scale).astype(BF16)
            value_out = value_sum.astype(BF16)

            @pl.when(x == half)
            def _():
                out_keep[0, :, cols] = key_out
                out_keep[1, :, cols] = value_out

            @pl.when(x != half)
            def _():
                out_send[0, :, cols] = key_out
                out_send[1, :, cols] = value_out


def key_pass(*operands):
    _, rows, cols = operands[0].shape
    heads = cols // HD
    both = 2 * rows
    pairs = both * 5 * rows * heads
    part = jax.ShapeDtypeStruct((2, rows, cols), BF16)
    return pl.pallas_call(
        functools.partial(key_kernel, HD ** -0.5),
        out_shape=(part, part),
        in_specs=[ANY] * 12 + [VM] * 3,
        out_specs=(VM, VM),
        scratch_shapes=[
            pltpu.VMEM((both, cols), BF16),
            pltpu.VMEM((both, cols), BF16),
            pltpu.VMEM((3 * both, cols), BF16),
            pltpu.VMEM((3 * both, cols), BF16),
            pltpu.VMEM((8, 3 * both), F32),
            pltpu.SemaphoreType.DMA((16,)),
        ],
        compiler_params=params(),
        cost_estimate=cost(),
        name="key_pass",
    )(*operands)


def unpack_kernel(q_keep, q_got, kv_keep, kv_got, dq, dk, dv):
    half = q_keep.shape[1]
    x = lax.rem(lax.axis_index("ctx"), 2)
    mine = pl.ds(pl.multiple_of(x * half, half), half)
    theirs = pl.ds(pl.multiple_of((1 - x) * half, half), half)
    for out, kept, got in (
        (dq, q_keep, q_got),
        (dk, kv_keep.at[0], kv_got.at[0]),
        (dv, kv_keep.at[1], kv_got.at[1]),
    ):
        out[:, mine] = kept[...]
        out[:, theirs] = got[...]


def unpack(q_keep, q_got, kv_keep, kv_got):
    rows, half = q_keep.shape
    whole = jax.ShapeDtypeStruct((rows, 2 * half), BF16)
    return pl.pallas_call(
        unpack_kernel,
        out_shape=(whole,) * 3,
        in_specs=[VM] * 4,
        out_specs=(VM,) * 3,
        compiler_params=params(16),
        cost_estimate=cost(),
        name="unpack",
    )(q_keep, q_got, kv_keep, kv_got)


def body(queries, keys, values, out_grad, out_weight):
    length = lax.axis_size("ctx")
    lanes = lax.axis_size("mp")
    blocks = length // 2
    width = out_grad.shape[1]

    def over_mp(array, flip):
        return lax.ppermute(array, "mp", [(i, i ^ flip) for i in range(lanes)])

    def over_x(array):
        return lax.ppermute(array, "ctx", [(i, i ^ 1) for i in range(length)])

    def over_z(array, first):
        pairs = []
        for position in range(length):
            block = position // 2
            other = ((block - first) ^ 1) + first
            for lane in range(lanes):
                source = position * lanes + lane
                if block >= first and other < blocks:
                    target = (2 * other + position % 2) * lanes + lane
                else:
                    target = position * lanes + (lane ^ 1)
                pairs.append((source, target))
        return lax.ppermute(array, ("ctx", "mp"), pairs)

    keep, send, og0, og1 = pack(queries, keys, values, out_grad)
    e0, o0 = over_z(keep, 0), over_z(keep, 1)
    y0 = over_mp(og0, 2)
    xr = over_x(send)
    y1 = over_mp(og1, 2)
    near = over_mp(out_grad, 1)
    acc = grad_piece(None, out_grad, near, out_weight, width, (0, 1), 0, False)
    e1, o1 = over_z(xr, 0), over_z(xr, 1)
    far0 = over_mp(y0, 1)
    acc = grad_piece(acc, y0, far0, out_weight, width, (2, 3), 0, False)
    y1, e0, o0 = lax.optimization_barrier((y1, e0, o0))
    far1 = over_mp(y1, 1)
    dkeep, dsend = grad_piece(acc, y1, far1, out_weight, width, (2, 3), width // 2, True)
    dxr = over_x(dsend)
    de0, do0 = over_z(dkeep, 0), over_z(dkeep, 1)
    dq_keep, dq_send, stats = query_pass(keep, xr, e0, e1, o0, o1, dkeep, dxr)
    de1, do1 = over_z(dxr, 0), over_z(dxr, 1)
    se, so = over_z(stats, 0), over_z(stats, 1)
    dq_got = over_x(dq_send)
    kv_keep, kv_send = key_pass(
        keep, xr, e0, e1, o0, o1, dkeep, dxr, de0, de1, do0, do1, stats, se, so
    )
    kv_got = over_x(kv_send)
    return tuple(unpack(dq_keep, dq_got, kv_keep, kv_got))


def solution(mesh):
    placed = (P("ctx", "mp"), P("ctx", "mp"), P("ctx", "mp"), P("ctx", "mp"), P("mp", None))
    return jax.shard_map(
        body,
        mesh=mesh,
        in_specs=placed,
        out_specs=(P("ctx", "mp"), P("ctx", "mp"), P("ctx", "mp")),
        check_vma=False,
    )
```

```python
import functools
import math

import jax
import jax.numpy as jnp
from jax import lax
from jax.experimental import pallas as pl
from jax.experimental.pallas import tpu as pltpu
from jax.sharding import PartitionSpec as P

HD = 128
BF16 = jnp.bfloat16
F32 = jnp.float32
BIG = 1e30
ANY = pl.BlockSpec(memory_space=pl.ANY)
VM = pl.BlockSpec(memory_space=pltpu.VMEM)
HBM = pl.BlockSpec(memory_space=pltpu.HBM)


def params(mib=40):
    return pltpu.CompilerParams(vmem_limit_bytes=mib << 20)


def nt(a, b):
    return lax.dot_general(a, b, (((1,), (1,)), ((), ())), preferred_element_type=F32)


def nn(a, b):
    return lax.dot_general(a, b, (((1,), (0,)), ((), ())), preferred_element_type=F32)


def cost(flops=1):
    return pl.CostEstimate(flops=int(flops), bytes_accessed=1, transcendentals=0)


def pack_kernel(q, k, v, keep, send, sem):
    half = q.shape[1] // 2
    x = lax.rem(lax.axis_index("ctx"), 2)
    mine = pl.ds(pl.multiple_of(x * half, half), half)
    theirs = pl.ds(pl.multiple_of((1 - x) * half, half), half)
    copies = []
    for i, ref in enumerate((q, k, v)):
        copies.append(pltpu.make_async_copy(ref.at[:, mine], keep.at[i], sem.at[i]))
        copies.append(pltpu.make_async_copy(ref.at[:, theirs], send.at[i], sem.at[3 + i]))
    for copy in copies:
        copy.start()
    for copy in copies:
        copy.wait()


def pack(q, k, v):
    rows, cols = q.shape
    part = jax.ShapeDtypeStruct((3, rows, cols // 2), BF16)
    return pl.pallas_call(
        pack_kernel,
        out_shape=(part, part),
        in_specs=[ANY] * 3,
        out_specs=(VM,) * 2,
        scratch_shapes=[pltpu.SemaphoreType.DMA((6,))],
        compiler_params=params(60),
        cost_estimate=cost(),
        name="pack",
    )(q, k, v)


def first_kernel(og, near, w, acc, wy, wf, wbuf, sem):
    width = og.shape[1]
    me = lax.axis_index("mp")
    copies = []
    for flip, target in enumerate((wbuf.at[0], wbuf.at[1], wy, wf)):
        first = pl.multiple_of(jnp.bitwise_xor(me, flip) * width, width)
        copies.append(pltpu.make_async_copy(w.at[:, pl.ds(first, width)], target, sem.at[flip]))
    for copy in copies:
        copy.start()
    copies[0].wait()
    acc[...] = nt(og[...], wbuf[0])
    copies[1].wait()
    acc[...] += nt(near[...], wbuf[1])
    copies[2].wait()
    copies[3].wait()


def first_piece(og, near, w):
    rows, width = og.shape
    heads = w.shape[0]
    part = jax.ShapeDtypeStruct((heads, width), BF16)
    return pl.pallas_call(
        first_kernel,
        out_shape=(jax.ShapeDtypeStruct((rows, heads), F32), part, part),
        in_specs=[VM, VM, ANY],
        out_specs=(VM, VM, VM),
        scratch_shapes=[pltpu.VMEM((2, heads, width), BF16), pltpu.SemaphoreType.DMA((4,))],
        compiler_params=params(46),
        cost_estimate=cost(),
        name="head_grad_first",
    )(og, near, w)


def next_kernel(acc, piece, w, out):
    out[...] = acc[...] + nt(piece[...], w[...])


def last_kernel(acc, piece, w, keep, send):
    total = acc[...] + nt(piece[...], w[...])
    half = total.shape[1] // 2
    x = lax.rem(lax.axis_index("ctx"), 2)
    low = total[:, :half].astype(BF16)
    high = total[:, half:].astype(BF16)

    @pl.when(x == 0)
    def _():
        keep[...] = low
        send[...] = high

    @pl.when(x != 0)
    def _():
        keep[...] = high
        send[...] = low


def grad_piece(acc, piece, w, last):
    rows, heads = acc.shape
    half = jax.ShapeDtypeStruct((rows, heads // 2), BF16)
    return pl.pallas_call(
        last_kernel if last else next_kernel,
        out_shape=(half, half) if last else jax.ShapeDtypeStruct((rows, heads), F32),
        in_specs=[VM] * 3,
        out_specs=(VM, VM) if last else VM,
        compiler_params=params(30),
        cost_estimate=cost(),
        name="head_grad",
    )(acc, piece, w)


def place():
    position = lax.axis_index("ctx")
    block = position // 2
    low_ok = block > 0
    high_ok = block < lax.axis_size("ctx") // 2 - 1
    odd = lax.rem(block, 2) == 1
    even_ok = jnp.logical_or(jnp.logical_and(odd, low_ok), jnp.logical_and(jnp.logical_not(odd), high_ok))
    odd_ok = jnp.logical_or(jnp.logical_and(odd, high_ok), jnp.logical_and(jnp.logical_not(odd), low_ok))
    turned = lax.rem(position + block, 2) == 1
    return even_ok, odd_ok, turned


def off(ok):
    return jnp.where(ok, 0.0, BIG).astype(F32)


def query_kernel(scale, keep, xr, e0, e1, o0, o1, dkeep, dxr, dq_keep, dq_send, stats, fifth):
    rows = keep.shape[1]
    heads = keep.shape[2] // HD
    even_ok, odd_ok, turned = place()

    @pl.when(turned)
    def _():
        fifth[0] = e1[1:3]
        fifth[1] = o0[1:3]

    @pl.when(jnp.logical_not(turned))
    def _():
        fifth[0] = o1[1:3]
        fifth[1] = e0[1:3]

    c = scale * math.log2(math.e)
    even_off, odd_off = off(even_ok), off(odd_ok)
    lane = lax.broadcasted_iota(jnp.int32, (rows, HD), 1)
    fifth_off = (
        jnp.where(turned, even_off, odd_off),
        jnp.where(turned, odd_off, even_off),
    )
    for mine, (q, d, e, o, out) in enumerate(
        ((keep, dkeep, e0, o0, dq_keep), (xr, dxr, e1, o1, dq_send))
    ):
        runs = (
            (keep, 1, None),
            (xr, 1, None),
            (e, 1, even_off),
            (o, 1, odd_off),
            (fifth.at[mine], 0, fifth_off[mine]),
        )
        mark = jnp.zeros((rows, HD), F32)
        for head in range(heads):
            cols = slice(head * HD, (head + 1) * HD)
            query = q[0, :, cols]
            grad = d[:, cols]
            scores = [nt(query, ref[k, :, cols]) for ref, k, _ in runs]
            top = None
            for s, (_, _, gone) in zip(scores, runs):
                m = jnp.max(s, -1, keepdims=True)
                m = m if gone is None else m - gone
                top = m if top is None else jnp.maximum(top, m)
            top = top * c
            weights = [
                jnp.exp2(s * c - (top if gone is None else top + gone))
                for s, (_, _, gone) in zip(scores, runs)
            ]
            total = jnp.sum(sum(weights), -1, keepdims=True)
            grads = [nt(grad, ref[k + 1, :, cols]) for ref, k, _ in runs]
            inverse = 1.0 / total
            delta = jnp.sum(sum(w * g for w, g in zip(weights, grads)), -1, keepdims=True) * inverse
            result = sum(
                nn((w * (g - delta)).astype(BF16), ref[k, :, cols])
                for w, g, (ref, k, _) in zip(weights, grads, runs)
            )
            out[:, cols] = (result * (inverse * scale)).astype(BF16)
            mark = jnp.where(lane == 2 * head, top + jnp.log2(total), mark)
            mark = jnp.where(lane == 2 * head + 1, delta, mark)
        stats[:, mine * rows : (mine + 1) * rows] = jnp.transpose(mark)[: stats.shape[0], :]


def query_pass(keep, xr, e0, e1, o0, o1, dkeep, dxr):
    _, rows, cols = keep.shape
    part = jax.ShapeDtypeStruct((rows, cols), BF16)
    return pl.pallas_call(
        functools.partial(query_kernel, HD ** -0.5),
        out_shape=(part, part, jax.ShapeDtypeStruct((8, 2 * rows), F32)),
        in_specs=[VM] * 8,
        out_specs=(VM, VM, VM),
        scratch_shapes=[pltpu.VMEM((2, 2, rows, cols), BF16)],
        compiler_params=params(30),
        cost_estimate=cost(2e10),
        name="query_pass",
    )(keep, xr, e0, e1, o0, o1, dkeep, dxr)


def key_step(scale, key, value, steps):
    c = scale * math.log2(math.e)
    key_sum = None
    value_sum = None
    for query, grad, total, delta in steps:
        weight = jnp.exp2(nt(key, query) * c - total)
        change = weight * (nt(value, grad) - delta)
        v = nn(weight.astype(BF16), grad)
        k = nn(change.astype(BF16), query)
        value_sum = v if value_sum is None else value_sum + v
        key_sum = k if key_sum is None else key_sum + k
    return key_sum, value_sum


def own_kernel(scale, keep, xr, dkeep, dxr, stats, sums):
    rows = keep.shape[1]
    heads = keep.shape[2] // HD
    for mine, keys in enumerate((keep, xr)):
        for head in range(heads):
            cols = slice(head * HD, (head + 1) * HD)
            steps = []
            for i, (q, d) in enumerate(((keep, dkeep), (xr, dxr))):
                span = slice(i * rows, (i + 1) * rows)
                steps.append((
                    q[0, :, cols],
                    d[:, cols],
                    stats[2 * head : 2 * head + 1, span],
                    stats[2 * head + 1 : 2 * head + 2, span],
                ))
            k, v = key_step(scale, keys[1, :, cols], keys[2, :, cols], steps)
            sums[mine, 0, :, cols] = k
            sums[mine, 1, :, cols] = v


def own_pass(keep, xr, dkeep, dxr, stats):
    _, rows, cols = keep.shape
    return pl.pallas_call(
        functools.partial(own_kernel, HD ** -0.5),
        out_shape=jax.ShapeDtypeStruct((2, 2, rows, cols), F32),
        in_specs=[VM] * 5,
        out_specs=VM,
        compiler_params=params(30),
        cost_estimate=cost(),
        name="own_pass",
    )(keep, xr, dkeep, dxr, stats)


def key_kernel(scale, head, keep, xr, e0, e1, o0, o1, de0, de1, do0, do1, se, so, sums, out_keep, out_send, fifth, marks):
    rows = keep.shape[1]
    even_ok, odd_ok, turned = place()
    cols = slice(head * HD, (head + 1) * HD)

    @pl.when(turned)
    def _():
        fifth[0, 0] = e1[0, :, cols]
        fifth[0, 1] = de1[:, cols]
        fifth[1, 0] = o0[0, :, cols]
        fifth[1, 1] = do0[:, cols]

    @pl.when(jnp.logical_not(turned))
    def _():
        fifth[0, 0] = o1[0, :, cols]
        fifth[0, 1] = do1[:, cols]
        fifth[1, 0] = e0[0, :, cols]
        fifth[1, 1] = de0[:, cols]

    even = se[2 * head : 2 * head + 2, :]
    odd = so[2 * head : 2 * head + 2, :]
    row = lax.broadcasted_iota(jnp.int32, even.shape, 0)
    nothing = jnp.where(row == 0, jnp.float32(BIG), jnp.float32(0.0))
    even = jnp.where(even_ok, even, nothing)
    odd = jnp.where(odd_ok, odd, nothing)
    fifths = (
        jnp.where(turned, even[:, rows:], odd[:, rows:]),
        jnp.where(turned, odd[:, :rows], even[:, :rows]),
    )
    for mine, (keys, e, o, de, do, out) in enumerate(
        ((keep, e0, o0, de0, do0, out_keep), (xr, e1, o1, de1, do1, out_send))
    ):
        span = slice(mine * rows, (mine + 1) * rows)
        steps = (
            (e[0, :, cols], de[:, cols], even[0:1, span], even[1:2, span]),
            (o[0, :, cols], do[:, cols], odd[0:1, span], odd[1:2, span]),
            (fifth[mine, 0], fifth[mine, 1], fifths[mine][0:1], fifths[mine][1:2]),
        )
        k, v = key_step(scale, keys[1, :, cols], keys[2, :, cols], steps)
        out[0] = ((k + sums[mine, 0, :, cols]) * scale).astype(BF16)
        out[1] = (v + sums[mine, 1, :, cols]).astype(BF16)


def key_pass(head, *operands):
    _, rows, cols = operands[0].shape
    part = jax.ShapeDtypeStruct((2, rows, HD), BF16)
    return pl.pallas_call(
        functools.partial(key_kernel, HD ** -0.5, head),
        out_shape=(part, part),
        in_specs=[VM] * 13,
        out_specs=(VM, VM),
        scratch_shapes=[pltpu.VMEM((2, 2, rows, HD), BF16), pltpu.VMEM((8, 2 * rows), F32)],
        compiler_params=params(30),
        cost_estimate=cost(),
        name="key_pass",
    )(*operands)


def unpack_kernel(q_keep, q_got, *refs):
    heads = q_keep.shape[1] // HD
    kept, got, (dq, dk, dv) = refs[:heads], refs[heads : 2 * heads], refs[2 * heads :]
    half = q_keep.shape[1]
    x = lax.rem(lax.axis_index("ctx"), 2)
    mine = pl.multiple_of(x * half, half)
    theirs = pl.multiple_of((1 - x) * half, half)
    dq[:, pl.ds(mine, half)] = q_keep[...]
    dq[:, pl.ds(theirs, half)] = q_got[...]
    for head in range(heads):
        for i, out in enumerate((dk, dv)):
            out[:, pl.ds(mine + head * HD, HD)] = kept[head][i]
            out[:, pl.ds(theirs + head * HD, HD)] = got[head][i]


def unpack(q_keep, q_got, kept, got):
    rows, half = q_keep.shape
    whole = jax.ShapeDtypeStruct((rows, 2 * half), BF16)
    return pl.pallas_call(
        unpack_kernel,
        out_shape=(whole,) * 3,
        in_specs=[VM] * (2 + 2 * len(kept)),
        out_specs=(VM,) * 3,
        compiler_params=params(16),
        cost_estimate=cost(),
        name="unpack",
    )(q_keep, q_got, *kept, *got)


def body(queries, keys, values, out_grad, out_weight):
    length = lax.axis_size("ctx")
    lanes = lax.axis_size("mp")
    blocks = length // 2
    width = out_grad.shape[1]

    def over_mp(array, flip):
        return lax.ppermute(array, "mp", [(i, i ^ flip) for i in range(lanes)])

    def over_x(array):
        return lax.ppermute(array, "ctx", [(i, i ^ 1) for i in range(length)])

    def over_z(array, first):
        pairs = []
        for position in range(length):
            block = position // 2
            other = ((block - first) ^ 1) + first
            for lane in range(lanes):
                source = position * lanes + lane
                if block >= first and other < blocks:
                    target = (2 * other + position % 2) * lanes + lane
                else:
                    target = position * lanes + (lane ^ 1)
                pairs.append((source, target))
        return lax.ppermute(array, ("ctx", "mp"), pairs)

    y = over_mp(out_grad, 2)
    near = over_mp(out_grad, 1)
    keep, send = pack(queries, keys, values)
    e0, o0 = over_z(keep, 0), over_z(keep, 1)
    xr = over_x(send)
    acc, wy, wf = first_piece(out_grad, near, out_weight)
    y, e0, o0, acc = lax.optimization_barrier((y, e0, o0, acc))
    e1, o1 = over_z(xr, 0), over_z(xr, 1)
    far = over_mp(y, 1)
    acc = grad_piece(acc, y, wy, False)
    dkeep, dsend = grad_piece(acc, far, wf, True)
    dxr = over_x(dsend)
    de0, do0 = over_z(dkeep, 0), over_z(dkeep, 1)
    dq_keep, dq_send, stats = query_pass(keep, xr, e0, e1, o0, o1, dkeep, dxr)
    de1, do1 = over_z(dxr, 0), over_z(dxr, 1)
    stats, de0, do0 = lax.optimization_barrier((stats, de0, do0))
    se, so = over_z(stats, 0), over_z(stats, 1)
    dq_got = over_x(dq_send)
    sums = own_pass(keep, xr, dkeep, dxr, stats)
    kept, got = [], []
    for head in range(dkeep.shape[1] // HD):
        if head == 1:
            sums, dq_got = lax.optimization_barrier((sums, dq_got))
        kv_keep, kv_send = key_pass(
            head, keep, xr, e0, e1, o0, o1, de0, de1, do0, do1, se, so, sums
        )
        kept.append(kv_keep)
        got.append(over_x(kv_send))
    return tuple(unpack(dq_keep, dq_got, kept, got))


def solution(mesh):
    placed = (P("ctx", "mp"), P("ctx", "mp"), P("ctx", "mp"), P("ctx", "mp"), P("mp", None))
    return jax.shard_map(
        body,
        mesh=mesh,
        in_specs=placed,
        out_specs=(P("ctx", "mp"), P("ctx", "mp"), P("ctx", "mp")),
        check_vma=False,
    )
```

```python
import functools
import math

import jax
import jax.numpy as jnp
from jax import lax
from jax.experimental import pallas as pl
from jax.experimental.pallas import tpu as pltpu
from jax.sharding import PartitionSpec as P

HD = 128
BF16 = jnp.bfloat16
F32 = jnp.float32
BIG = 1e30
ANY = pl.BlockSpec(memory_space=pl.ANY)
VM = pl.BlockSpec(memory_space=pltpu.VMEM)
HBM = pl.BlockSpec(memory_space=pltpu.HBM)


def params(mib=40):
    return pltpu.CompilerParams(vmem_limit_bytes=mib << 20)


def nt(a, b):
    return lax.dot_general(a, b, (((1,), (1,)), ((), ())), preferred_element_type=F32)


def nn(a, b):
    return lax.dot_general(a, b, (((1,), (0,)), ((), ())), preferred_element_type=F32)


def cost(flops=1):
    return pl.CostEstimate(flops=int(flops), bytes_accessed=1, transcendentals=0)


def pack_kernel(q, k, v, keep, send_kv, send_q, sem):
    half = q.shape[1] // 2
    x = lax.rem(lax.axis_index("ctx"), 2)
    mine = pl.ds(pl.multiple_of(x * half, half), half)
    theirs = pl.ds(pl.multiple_of((1 - x) * half, half), half)
    pairs = (
        (k.at[:, theirs], send_kv.at[0]),
        (v.at[:, theirs], send_kv.at[1]),
        (k.at[:, mine], keep.at[0]),
        (v.at[:, mine], keep.at[1]),
        (q.at[:, mine], keep.at[2]),
        (q.at[:, theirs], send_q.at[0]),
    )
    copies = [pltpu.make_async_copy(a, b, sem.at[i]) for i, (a, b) in enumerate(pairs)]
    for copy in copies:
        copy.start()
    for copy in copies:
        copy.wait()


def pack(q, k, v):
    rows, cols = q.shape
    three, two, one = (jax.ShapeDtypeStruct((n, rows, cols // 2), BF16) for n in (3, 2, 1))
    return pl.pallas_call(
        pack_kernel,
        out_shape=(three, two, one),
        in_specs=[ANY] * 3,
        out_specs=(VM,) * 3,
        scratch_shapes=[pltpu.SemaphoreType.DMA((6,))],
        compiler_params=params(60),
        cost_estimate=cost(),
        name="pack",
    )(q, k, v)


def join_kernel(mine, theirs, out):
    out[0] = mine[...]
    out[1] = theirs[...]


def join(mine, theirs):
    return pl.pallas_call(
        join_kernel,
        out_shape=jax.ShapeDtypeStruct((2, *mine.shape), BF16),
        in_specs=[VM] * 2,
        out_specs=VM,
        compiler_params=params(16),
        cost_estimate=cost(),
        name="join",
    )(mine, theirs)


def first_kernel(og, near, w, acc, wy, wf, wbuf, sem):
    width = og.shape[1]
    me = lax.axis_index("mp")
    copies = []
    for flip, target in enumerate((wbuf.at[0], wbuf.at[1], wy, wf)):
        first = pl.multiple_of(jnp.bitwise_xor(me, flip) * width, width)
        copies.append(pltpu.make_async_copy(w.at[:, pl.ds(first, width)], target, sem.at[flip]))
    for copy in copies:
        copy.start()
    copies[0].wait()
    acc[...] = nt(og[...], wbuf[0])
    copies[1].wait()
    acc[...] += nt(near[...], wbuf[1])
    copies[2].wait()
    copies[3].wait()


def first_piece(og, near, w):
    rows, width = og.shape
    heads = w.shape[0]
    part = jax.ShapeDtypeStruct((heads, width), BF16)
    return pl.pallas_call(
        first_kernel,
        out_shape=(jax.ShapeDtypeStruct((rows, heads), F32), part, part),
        in_specs=[VM, VM, ANY],
        out_specs=(VM, VM, VM),
        scratch_shapes=[pltpu.VMEM((2, heads, width), BF16), pltpu.SemaphoreType.DMA((4,))],
        compiler_params=params(46),
        cost_estimate=cost(),
        name="head_grad_first",
    )(og, near, w)


def next_kernel(acc, piece, w, out):
    out[...] = acc[...] + nt(piece[...], w[...])


def last_kernel(acc, piece, w, keep, send):
    total = acc[...] + nt(piece[...], w[...])
    half = total.shape[1] // 2
    x = lax.rem(lax.axis_index("ctx"), 2)
    low = total[:, :half].astype(BF16)
    high = total[:, half:].astype(BF16)

    @pl.when(x == 0)
    def _():
        keep[...] = low
        send[...] = high

    @pl.when(x != 0)
    def _():
        keep[...] = high
        send[...] = low


def grad_piece(acc, piece, w, last):
    rows, heads = acc.shape
    half = jax.ShapeDtypeStruct((rows, heads // 2), BF16)
    return pl.pallas_call(
        last_kernel if last else next_kernel,
        out_shape=(half, half) if last else jax.ShapeDtypeStruct((rows, heads), F32),
        in_specs=[VM] * 3,
        out_specs=(VM, VM) if last else VM,
        compiler_params=params(30),
        cost_estimate=cost(),
        name="head_grad",
    )(acc, piece, w)


def place():
    position = lax.axis_index("ctx")
    block = position // 2
    low_ok = block > 0
    high_ok = block < lax.axis_size("ctx") // 2 - 1
    odd = lax.rem(block, 2) == 1
    even_ok = jnp.logical_or(jnp.logical_and(odd, low_ok), jnp.logical_and(jnp.logical_not(odd), high_ok))
    odd_ok = jnp.logical_or(jnp.logical_and(odd, high_ok), jnp.logical_and(jnp.logical_not(odd), low_ok))
    turned = lax.rem(position + block, 2) == 1
    return even_ok, odd_ok, turned


def off(ok):
    return jnp.where(ok, 0.0, BIG).astype(F32)


def query_kernel(scale, own, has_marks, *refs):
    refs = list(refs)
    q, d, keep, xr, e, o, e_other, o_other = refs[:8]
    q = q.at[q.shape[0] - 1]
    before = refs[8] if has_marks else None
    out, stats, fifth = refs[-3:]
    rows = q.shape[0]
    heads = q.shape[1] // HD
    even_ok, odd_ok, turned = place()
    from_even = turned if own else jnp.logical_not(turned)

    @pl.when(from_even)
    def _():
        fifth[...] = e_other[0:2]

    @pl.when(jnp.logical_not(from_even))
    def _():
        fifth[...] = o_other[0:2]

    c = scale * math.log2(math.e)
    even_off, odd_off = off(even_ok), off(odd_ok)
    lane = lax.broadcasted_iota(jnp.int32, (rows, HD), 1)
    runs = (
        (keep, None),
        (xr, None),
        (e, even_off),
        (o, odd_off),
        (fifth, jnp.where(from_even, even_off, odd_off)),
    )
    mark = jnp.zeros((rows, HD), F32)
    for head in range(heads):
        cols = slice(head * HD, (head + 1) * HD)
        query = q[:, cols]
        grad = d[:, cols]
        scores = [nt(query, ref[0, :, cols]) for ref, _ in runs]
        top = None
        for s, (_, gone) in zip(scores, runs):
            m = jnp.max(s, -1, keepdims=True)
            m = m if gone is None else m - gone
            top = m if top is None else jnp.maximum(top, m)
        top = top * c
        weights = [
            jnp.exp2(s * c - (top if gone is None else top + gone))
            for s, (_, gone) in zip(scores, runs)
        ]
        total = jnp.sum(sum(weights), -1, keepdims=True)
        grads = [nt(grad, ref[1, :, cols]) for ref, _ in runs]
        inverse = 1.0 / total
        delta = jnp.sum(sum(w * g for w, g in zip(weights, grads)), -1, keepdims=True) * inverse
        result = sum(
            nn((w * (g - delta)).astype(BF16), ref[0, :, cols])
            for w, g, (ref, _) in zip(weights, grads, runs)
        )
        out[:, cols] = (result * (inverse * scale)).astype(BF16)
        mark = jnp.where(lane == 2 * head, top + jnp.log2(total), mark)
        mark = jnp.where(lane == 2 * head + 1, delta, mark)
    marks = jnp.transpose(mark)[: stats.shape[0], :]
    if has_marks:
        stats[:, :rows] = before[...]
        stats[:, rows:] = marks
    else:
        stats[...] = marks


def query_pass(own, q, d, keep, xr, e, o, e_other, o_other, before=None):
    rows, cols = d.shape
    operands = [q, d, keep, xr, e, o, e_other, o_other]
    if before is not None:
        operands.append(before)
    return pl.pallas_call(
        functools.partial(query_kernel, HD ** -0.5, own, before is not None),
        out_shape=(
            jax.ShapeDtypeStruct((rows, cols), BF16),
            jax.ShapeDtypeStruct((8, rows if before is None else 2 * rows), F32),
        ),
        in_specs=[VM] * len(operands),
        out_specs=(VM, VM),
        scratch_shapes=[pltpu.VMEM((2, rows, cols), BF16)],
        compiler_params=params(30),
        cost_estimate=cost(6e9),
        name="query_pass",
    )(*operands)


def key_step(scale, key, value, steps):
    c = scale * math.log2(math.e)
    key_sum = None
    value_sum = None
    for query, grad, total, delta in steps:
        weight = jnp.exp2(nt(key, query) * c - total)
        change = weight * (nt(value, grad) - delta)
        v = nn(weight.astype(BF16), grad)
        k = nn(change.astype(BF16), query)
        value_sum = v if value_sum is None else value_sum + v
        key_sum = k if key_sum is None else key_sum + k
    return key_sum, value_sum


def own_kernel(scale, keep, xkv, xq, dkeep, dxr, stats, sums):
    rows = keep.shape[1]
    heads = keep.shape[2] // HD
    for mine, keys in enumerate((keep, xkv)):
        for head in range(heads):
            cols = slice(head * HD, (head + 1) * HD)
            steps = []
            for i, (q, d) in enumerate(((keep.at[2], dkeep), (xq.at[0], dxr))):
                span = slice(i * rows, (i + 1) * rows)
                steps.append((
                    q[:, cols],
                    d[:, cols],
                    stats[2 * head : 2 * head + 1, span],
                    stats[2 * head + 1 : 2 * head + 2, span],
                ))
            k, v = key_step(scale, keys[0, :, cols], keys[1, :, cols], steps)
            sums[mine, 0, :, cols] = k
            sums[mine, 1, :, cols] = v


def own_pass(*operands):
    _, rows, cols = operands[0].shape
    return pl.pallas_call(
        functools.partial(own_kernel, HD ** -0.5),
        out_shape=jax.ShapeDtypeStruct((2, 2, rows, cols), F32),
        in_specs=[VM] * 6,
        out_specs=VM,
        compiler_params=params(30),
        cost_estimate=cost(),
        name="own_pass",
    )(*operands)


def key_kernel(scale, own, heads, kv, e0, o0, e1, o1, de, do, se, so, sums, out, fifth_q, fifth_d):
    rows = kv.shape[1]
    even_ok, odd_ok, turned = place()
    from_even = turned if own else jnp.logical_not(turned)
    even_q = (e0.at[e0.shape[0] - 1], e1.at[e1.shape[0] - 1])
    odd_q = (o0.at[o0.shape[0] - 1], o1.at[o1.shape[0] - 1])
    same, other = (0, 1) if own else (1, 0)
    wanted = slice(heads[0] * HD, (heads[-1] + 1) * HD)

    @pl.when(from_even)
    def _():
        fifth_q[...] = even_q[other][:, wanted]
        fifth_d[...] = de[other, :, wanted]

    @pl.when(jnp.logical_not(from_even))
    def _():
        fifth_q[...] = odd_q[other][:, wanted]
        fifth_d[...] = do[other, :, wanted]

    row = lax.broadcasted_iota(jnp.int32, se.shape, 0)
    nothing = jnp.where(lax.rem(row, 2) == 0, jnp.float32(BIG), jnp.float32(0.0))
    even = jnp.where(even_ok, se[...], nothing)
    odd = jnp.where(odd_ok, so[...], nothing)
    span = slice(same * rows, (same + 1) * rows)
    across = slice(other * rows, (other + 1) * rows)
    fifth = jnp.where(from_even, even[:, across], odd[:, across])
    for i, head in enumerate(heads):
        cols = slice(head * HD, (head + 1) * HD)
        to = slice(i * HD, (i + 1) * HD)
        a, b = 2 * head, 2 * head + 1
        steps = (
            (even_q[same][:, cols], de[same, :, cols], even[a : a + 1, span], even[b : b + 1, span]),
            (odd_q[same][:, cols], do[same, :, cols], odd[a : a + 1, span], odd[b : b + 1, span]),
            (fifth_q[:, to], fifth_d[:, to], fifth[a : a + 1], fifth[b : b + 1]),
        )
        k, v = key_step(scale, kv[0, :, cols], kv[1, :, cols], steps)
        out[0, :, to] = ((k + sums[same, 0, :, cols]) * scale).astype(BF16)
        out[1, :, to] = (v + sums[same, 1, :, cols]).astype(BF16)


def key_pass(own, heads, kv, *operands):
    _, rows, _ = kv.shape
    wide = HD * len(heads)
    return pl.pallas_call(
        functools.partial(key_kernel, HD ** -0.5, own, heads),
        out_shape=jax.ShapeDtypeStruct((2, rows, wide), BF16),
        in_specs=[VM] * (1 + len(operands)),
        out_specs=VM,
        scratch_shapes=[pltpu.VMEM((rows, wide), BF16)] * 2,
        compiler_params=params(30),
        cost_estimate=cost(),
        name="key_pass",
    )(kv, *operands)


def unpack_kernel(q_keep, q_got, kv_keep, *refs):
    got, (dq, dk, dv) = refs[:-3], refs[-3:]
    half = q_keep.shape[1]
    x = lax.rem(lax.axis_index("ctx"), 2)
    mine = pl.multiple_of(x * half, half)
    theirs = pl.multiple_of((1 - x) * half, half)
    dq[:, pl.ds(mine, half)] = q_keep[...]
    dq[:, pl.ds(theirs, half)] = q_got[...]
    for i, out in enumerate((dk, dv)):
        out[:, pl.ds(mine, half)] = kv_keep[i]
        first = 0
        for piece in got:
            width = piece.shape[2]
            out[:, pl.ds(theirs + first, width)] = piece[i]
            first += width


def unpack(q_keep, q_got, kv_keep, *got):
    rows, half = q_keep.shape
    whole = jax.ShapeDtypeStruct((rows, 2 * half), BF16)
    return pl.pallas_call(
        unpack_kernel,
        out_shape=(whole,) * 3,
        in_specs=[VM] * (3 + len(got)),
        out_specs=(VM,) * 3,
        compiler_params=params(16),
        cost_estimate=cost(),
        name="unpack",
    )(q_keep, q_got, kv_keep, *got)


def body(queries, keys, values, out_grad, out_weight):
    length = lax.axis_size("ctx")
    lanes = lax.axis_size("mp")
    blocks = length // 2
    width = out_grad.shape[1]

    def over_mp(array, flip):
        return lax.ppermute(array, "mp", [(i, i ^ flip) for i in range(lanes)])

    def over_x(array):
        return lax.ppermute(array, "ctx", [(i, i ^ 1) for i in range(length)])

    def over_z(array, first):
        pairs = []
        for position in range(length):
            block = position // 2
            other = ((block - first) ^ 1) + first
            for lane in range(lanes):
                source = position * lanes + lane
                if block >= first and other < blocks:
                    target = (2 * other + position % 2) * lanes + lane
                else:
                    target = position * lanes + (lane ^ 1)
                pairs.append((source, target))
        return lax.ppermute(array, ("ctx", "mp"), pairs)

    y = over_mp(out_grad, 2)
    near = over_mp(out_grad, 1)
    keep, send_kv, send_q = pack(queries, keys, values)
    xkv = over_x(send_kv)
    e0, o0 = over_z(keep, 0), over_z(keep, 1)
    xq = over_x(send_q)
    acc, wy, wf = first_piece(out_grad, near, out_weight)
    e1, o1 = over_z(xkv, 0), over_z(xkv, 1)
    qe1, qo1 = over_z(xq, 0), over_z(xq, 1)
    y, e0, o0, xkv, xq, acc = lax.optimization_barrier((y, e0, o0, xkv, xq, acc))
    far = over_mp(y, 1)
    acc = grad_piece(acc, y, wy, False)
    dkeep, dsend = grad_piece(acc, far, wf, True)
    dxr = over_x(dsend)

    both_d = join(dkeep, dxr)
    de, do = over_z(both_d, 0), over_z(both_d, 1)
    dq_keep, stats = query_pass(True, keep, dkeep, keep, xkv, e0, o0, e1, o1)
    stats, qe1, qo1 = lax.optimization_barrier((stats, qe1, qo1))
    dq_send, stats = query_pass(False, xq, dxr, keep, xkv, e1, o1, e0, o0, stats)
    se, so = over_z(stats, 0), over_z(stats, 1)
    dq_got = over_x(dq_send)
    sums = own_pass(keep, xkv, xq, dkeep, dxr, stats)
    sums, dq_got = lax.optimization_barrier((sums, dq_got))
    heads = dkeep.shape[1] // HD
    got = [
        over_x(key_pass(False, (head,), xkv, e0, o0, qe1, qo1, de, do, se, so, sums))
        for head in range(heads)
    ]
    kv_keep = key_pass(True, tuple(range(heads)), keep, e0, o0, qe1, qo1, de, do, se, so, sums)
    return tuple(unpack(dq_keep, dq_got, kv_keep, *got))


def solution(mesh):
    placed = (P("ctx", "mp"), P("ctx", "mp"), P("ctx", "mp"), P("ctx", "mp"), P("mp", None))
    return jax.shard_map(
        body,
        mesh=mesh,
        in_specs=placed,
        out_specs=(P("ctx", "mp"), P("ctx", "mp"), P("ctx", "mp")),
        check_vma=False,
    )
```

```python
import functools
import math

import jax
import jax.numpy as jnp
from jax import lax
from jax.experimental import pallas as pl
from jax.experimental.pallas import tpu as pltpu
from jax.sharding import PartitionSpec as P

HD = 128
BF16 = jnp.bfloat16
F32 = jnp.float32
BIG = 1e30
ANY = pl.BlockSpec(memory_space=pl.ANY)
VM = pl.BlockSpec(memory_space=pltpu.VMEM)
HBM = pl.BlockSpec(memory_space=pltpu.HBM)


def params(mib=40):
    return pltpu.CompilerParams(vmem_limit_bytes=mib << 20)


def nt(a, b):
    return lax.dot_general(a, b, (((1,), (1,)), ((), ())), preferred_element_type=F32)


def nn(a, b):
    return lax.dot_general(a, b, (((1,), (0,)), ((), ())), preferred_element_type=F32)


def cost(flops=1):
    return pl.CostEstimate(flops=int(flops), bytes_accessed=1, transcendentals=0)


def pack_kernel(q, k, v, keep, send_kv, send_q, sem):
    half = q.shape[1] // 2
    x = lax.rem(lax.axis_index("ctx"), 2)
    mine = pl.ds(pl.multiple_of(x * half, half), half)
    theirs = pl.ds(pl.multiple_of((1 - x) * half, half), half)
    pairs = (
        (k.at[:, theirs], send_kv.at[0]),
        (v.at[:, theirs], send_kv.at[1]),
        (k.at[:, mine], keep.at[0]),
        (v.at[:, mine], keep.at[1]),
        (q.at[:, mine], keep.at[2]),
        (q.at[:, theirs], send_q.at[0]),
    )
    copies = [pltpu.make_async_copy(a, b, sem.at[i]) for i, (a, b) in enumerate(pairs)]
    for copy in copies:
        copy.start()
    for copy in copies:
        copy.wait()


def pack(q, k, v):
    rows, cols = q.shape
    three, two, one = (jax.ShapeDtypeStruct((n, rows, cols // 2), BF16) for n in (3, 2, 1))
    return pl.pallas_call(
        pack_kernel,
        out_shape=(three, two, one),
        in_specs=[ANY] * 3,
        out_specs=(VM,) * 3,
        scratch_shapes=[pltpu.SemaphoreType.DMA((6,))],
        compiler_params=params(60),
        cost_estimate=cost(),
        name="pack",
    )(q, k, v)


def join_kernel(mine, theirs, out):
    out[0] = mine[...]
    out[1] = theirs[...]


def join(mine, theirs):
    return pl.pallas_call(
        join_kernel,
        out_shape=jax.ShapeDtypeStruct((2, *mine.shape), BF16),
        in_specs=[VM] * 2,
        out_specs=VM,
        compiler_params=params(16),
        cost_estimate=cost(),
        name="join",
    )(mine, theirs)


def first_kernel(og, near, w, acc, wy, wf, wbuf, sem):
    width = og.shape[1]
    me = lax.axis_index("mp")
    copies = []
    for flip, target in enumerate((wbuf.at[0], wbuf.at[1], wy, wf)):
        first = pl.multiple_of(jnp.bitwise_xor(me, flip) * width, width)
        copies.append(pltpu.make_async_copy(w.at[:, pl.ds(first, width)], target, sem.at[flip]))
    for copy in copies:
        copy.start()
    copies[0].wait()
    acc[...] = nt(og[...], wbuf[0])
    copies[1].wait()
    acc[...] += nt(near[...], wbuf[1])
    copies[2].wait()
    copies[3].wait()


def first_piece(og, near, w):
    rows, width = og.shape
    heads = w.shape[0]
    part = jax.ShapeDtypeStruct((heads, width), BF16)
    return pl.pallas_call(
        first_kernel,
        out_shape=(jax.ShapeDtypeStruct((rows, heads), F32), part, part),
        in_specs=[VM, VM, ANY],
        out_specs=(VM, VM, VM),
        scratch_shapes=[pltpu.VMEM((2, heads, width), BF16), pltpu.SemaphoreType.DMA((4,))],
        compiler_params=params(46),
        cost_estimate=cost(),
        name="head_grad_first",
    )(og, near, w)


def next_kernel(acc, piece, w, out):
    out[...] = acc[...] + nt(piece[...], w[...])


def last_kernel(acc, piece, w, keep, send):
    total = acc[...] + nt(piece[...], w[...])
    half = total.shape[1] // 2
    x = lax.rem(lax.axis_index("ctx"), 2)
    low = total[:, :half].astype(BF16)
    high = total[:, half:].astype(BF16)

    @pl.when(x == 0)
    def _():
        keep[...] = low
        send[...] = high

    @pl.when(x != 0)
    def _():
        keep[...] = high
        send[...] = low


def grad_piece(acc, piece, w, last):
    rows, heads = acc.shape
    half = jax.ShapeDtypeStruct((rows, heads // 2), BF16)
    return pl.pallas_call(
        last_kernel if last else next_kernel,
        out_shape=(half, half) if last else jax.ShapeDtypeStruct((rows, heads), F32),
        in_specs=[VM] * 3,
        out_specs=(VM, VM) if last else VM,
        compiler_params=params(30),
        cost_estimate=cost(),
        name="head_grad",
    )(acc, piece, w)


def place():
    position = lax.axis_index("ctx")
    block = position // 2
    low_ok = block > 0
    high_ok = block < lax.axis_size("ctx") // 2 - 1
    odd = lax.rem(block, 2) == 1
    even_ok = jnp.logical_or(jnp.logical_and(odd, low_ok), jnp.logical_and(jnp.logical_not(odd), high_ok))
    odd_ok = jnp.logical_or(jnp.logical_and(odd, high_ok), jnp.logical_and(jnp.logical_not(odd), low_ok))
    turned = lax.rem(position + block, 2) == 1
    return even_ok, odd_ok, turned


def off(ok):
    return jnp.where(ok, 0.0, BIG).astype(F32)


def query_kernel(scale, own, has_marks, *refs):
    refs = list(refs)
    q, d, keep, xr, e, o, e_other, o_other = refs[:8]
    q = q.at[q.shape[0] - 1]
    before = refs[8] if has_marks else None
    out, stats, fifth = refs[-3:]
    rows = q.shape[0]
    heads = q.shape[1] // HD
    even_ok, odd_ok, turned = place()
    from_even = turned if own else jnp.logical_not(turned)

    @pl.when(from_even)
    def _():
        fifth[...] = e_other[0:2]

    @pl.when(jnp.logical_not(from_even))
    def _():
        fifth[...] = o_other[0:2]

    c = scale * math.log2(math.e)
    even_off, odd_off = off(even_ok), off(odd_ok)
    lane = lax.broadcasted_iota(jnp.int32, (rows, HD), 1)
    runs = (
        (keep, None),
        (xr, None),
        (e, even_off),
        (o, odd_off),
        (fifth, jnp.where(from_even, even_off, odd_off)),
    )
    mark = jnp.zeros((rows, HD), F32)
    for head in range(heads):
        cols = slice(head * HD, (head + 1) * HD)
        query = q[:, cols]
        grad = d[:, cols]
        scores = [nt(query, ref[0, :, cols]) for ref, _ in runs]
        top = None
        for s, (_, gone) in zip(scores, runs):
            m = jnp.max(s, -1, keepdims=True)
            m = m if gone is None else m - gone
            top = m if top is None else jnp.maximum(top, m)
        top = top * c
        weights = [
            jnp.exp2(s * c - (top if gone is None else top + gone))
            for s, (_, gone) in zip(scores, runs)
        ]
        total = jnp.sum(sum(weights), -1, keepdims=True)
        grads = [nt(grad, ref[1, :, cols]) for ref, _ in runs]
        inverse = 1.0 / total
        delta = jnp.sum(sum(w * g for w, g in zip(weights, grads)), -1, keepdims=True) * inverse
        result = sum(
            nn((w * (g - delta)).astype(BF16), ref[0, :, cols])
            for w, g, (ref, _) in zip(weights, grads, runs)
        )
        out[:, cols] = (result * (inverse * scale)).astype(BF16)
        mark = jnp.where(lane == 2 * head, top + jnp.log2(total), mark)
        mark = jnp.where(lane == 2 * head + 1, delta, mark)
    marks = jnp.transpose(mark)[: stats.shape[0], :]
    if has_marks:
        stats[:, :rows] = before[...]
        stats[:, rows:] = marks
    else:
        stats[...] = marks


def query_pass(own, q, d, keep, xr, e, o, e_other, o_other, before=None):
    rows, cols = d.shape
    operands = [q, d, keep, xr, e, o, e_other, o_other]
    if before is not None:
        operands.append(before)
    return pl.pallas_call(
        functools.partial(query_kernel, HD ** -0.5, own, before is not None),
        out_shape=(
            jax.ShapeDtypeStruct((rows, cols), BF16),
            jax.ShapeDtypeStruct((8, rows if before is None else 2 * rows), F32),
        ),
        in_specs=[VM] * len(operands),
        out_specs=(VM, VM),
        scratch_shapes=[pltpu.VMEM((2, rows, cols), BF16)],
        compiler_params=params(30),
        cost_estimate=cost(6e9 if own else 1),
        name="query_pass",
    )(*operands)


def key_step(scale, key, value, steps):
    c = scale * math.log2(math.e)
    key_sum = None
    value_sum = None
    for query, grad, total, delta in steps:
        weight = jnp.exp2(nt(key, query) * c - total)
        change = weight * (nt(value, grad) - delta)
        v = nn(weight.astype(BF16), grad)
        k = nn(change.astype(BF16), query)
        value_sum = v if value_sum is None else value_sum + v
        key_sum = k if key_sum is None else key_sum + k
    return key_sum, value_sum


def own_kernel(scale, keep, xkv, xq, dkeep, dxr, stats, sums):
    rows = keep.shape[1]
    heads = keep.shape[2] // HD
    for mine, keys in enumerate((keep, xkv)):
        for head in range(heads):
            cols = slice(head * HD, (head + 1) * HD)
            steps = []
            for i, (q, d) in enumerate(((keep.at[2], dkeep), (xq.at[0], dxr))):
                span = slice(i * rows, (i + 1) * rows)
                steps.append((
                    q[:, cols],
                    d[:, cols],
                    stats[2 * head : 2 * head + 1, span],
                    stats[2 * head + 1 : 2 * head + 2, span],
                ))
            k, v = key_step(scale, keys[0, :, cols], keys[1, :, cols], steps)
            sums[mine, 0, :, cols] = k
            sums[mine, 1, :, cols] = v


def own_pass(*operands):
    _, rows, cols = operands[0].shape
    return pl.pallas_call(
        functools.partial(own_kernel, HD ** -0.5),
        out_shape=jax.ShapeDtypeStruct((2, 2, rows, cols), F32),
        in_specs=[VM] * 6,
        out_specs=VM,
        compiler_params=params(30),
        cost_estimate=cost(),
        name="own_pass",
    )(*operands)


def key_kernel(scale, own, heads, kv, e0, o0, e1, o1, de, do, se, so, sums, out, fifth_q, fifth_d):
    rows = kv.shape[1]
    even_ok, odd_ok, turned = place()
    from_even = turned if own else jnp.logical_not(turned)
    even_q = (e0.at[e0.shape[0] - 1], e1.at[e1.shape[0] - 1])
    odd_q = (o0.at[o0.shape[0] - 1], o1.at[o1.shape[0] - 1])
    same, other = (0, 1) if own else (1, 0)
    wanted = slice(heads[0] * HD, (heads[-1] + 1) * HD)

    @pl.when(from_even)
    def _():
        fifth_q[...] = even_q[other][:, wanted]
        fifth_d[...] = de[other, :, wanted]

    @pl.when(jnp.logical_not(from_even))
    def _():
        fifth_q[...] = odd_q[other][:, wanted]
        fifth_d[...] = do[other, :, wanted]

    row = lax.broadcasted_iota(jnp.int32, se.shape, 0)
    nothing = jnp.where(lax.rem(row, 2) == 0, jnp.float32(BIG), jnp.float32(0.0))
    even = jnp.where(even_ok, se[...], nothing)
    odd = jnp.where(odd_ok, so[...], nothing)
    span = slice(same * rows, (same + 1) * rows)
    across = slice(other * rows, (other + 1) * rows)
    fifth = jnp.where(from_even, even[:, across], odd[:, across])
    for i, head in enumerate(heads):
        cols = slice(head * HD, (head + 1) * HD)
        to = slice(i * HD, (i + 1) * HD)
        a, b = 2 * head, 2 * head + 1
        steps = (
            (even_q[same][:, cols], de[same, :, cols], even[a : a + 1, span], even[b : b + 1, span]),
            (odd_q[same][:, cols], do[same, :, cols], odd[a : a + 1, span], odd[b : b + 1, span]),
            (fifth_q[:, to], fifth_d[:, to], fifth[a : a + 1], fifth[b : b + 1]),
        )
        k, v = key_step(scale, kv[0, :, cols], kv[1, :, cols], steps)
        out[0, :, to] = ((k + sums[same, 0, :, cols]) * scale).astype(BF16)
        out[1, :, to] = (v + sums[same, 1, :, cols]).astype(BF16)


def key_pass(own, heads, kv, *operands):
    _, rows, _ = kv.shape
    wide = HD * len(heads)
    return pl.pallas_call(
        functools.partial(key_kernel, HD ** -0.5, own, heads),
        out_shape=jax.ShapeDtypeStruct((2, rows, wide), BF16),
        in_specs=[VM] * (1 + len(operands)),
        out_specs=VM,
        scratch_shapes=[pltpu.VMEM((rows, wide), BF16)] * 2,
        compiler_params=params(30),
        cost_estimate=cost(),
        name="key_pass",
    )(kv, *operands)


def unpack_kernel(q_keep, q_got, kv_keep, *refs):
    got, (dq, dk, dv) = refs[:-3], refs[-3:]
    half = q_keep.shape[1]
    x = lax.rem(lax.axis_index("ctx"), 2)
    mine = pl.multiple_of(x * half, half)
    theirs = pl.multiple_of((1 - x) * half, half)
    dq[:, pl.ds(mine, half)] = q_keep[...]
    dq[:, pl.ds(theirs, half)] = q_got[...]
    for i, out in enumerate((dk, dv)):
        out[:, pl.ds(mine, half)] = kv_keep[i]
        first = 0
        for piece in got:
            width = piece.shape[2]
            out[:, pl.ds(theirs + first, width)] = piece[i]
            first += width


def unpack(q_keep, q_got, kv_keep, *got):
    rows, half = q_keep.shape
    whole = jax.ShapeDtypeStruct((rows, 2 * half), BF16)
    return pl.pallas_call(
        unpack_kernel,
        out_shape=(whole,) * 3,
        in_specs=[VM] * (3 + len(got)),
        out_specs=(VM,) * 3,
        compiler_params=params(16),
        cost_estimate=cost(),
        name="unpack",
    )(q_keep, q_got, kv_keep, *got)


def body(queries, keys, values, out_grad, out_weight):
    length = lax.axis_size("ctx")
    lanes = lax.axis_size("mp")
    blocks = length // 2
    width = out_grad.shape[1]

    def over_mp(array, flip):
        return lax.ppermute(array, "mp", [(i, i ^ flip) for i in range(lanes)])

    def over_x(array):
        return lax.ppermute(array, "ctx", [(i, i ^ 1) for i in range(length)])

    def over_z(array, first):
        pairs = []
        for position in range(length):
            block = position // 2
            other = ((block - first) ^ 1) + first
            for lane in range(lanes):
                source = position * lanes + lane
                if block >= first and other < blocks:
                    target = (2 * other + position % 2) * lanes + lane
                else:
                    target = position * lanes + (lane ^ 1)
                pairs.append((source, target))
        return lax.ppermute(array, ("ctx", "mp"), pairs)

    y = over_mp(out_grad, 2)
    near = over_mp(out_grad, 1)
    keep, send_kv, send_q = pack(queries, keys, values)
    xkv = over_x(send_kv)
    e0, o0 = over_z(keep, 0), over_z(keep, 1)
    xkv, send_q = lax.optimization_barrier((xkv, send_q))
    xq = over_x(send_q)
    acc, wy, wf = first_piece(out_grad, near, out_weight)
    e1, o1 = over_z(xkv, 0), over_z(xkv, 1)
    y, e0, o0, xq, acc = lax.optimization_barrier((y, e0, o0, xq, acc))
    xq, e1, o1 = lax.optimization_barrier((xq, e1, o1))
    qe1, qo1 = over_z(xq, 0), over_z(xq, 1)
    far = over_mp(y, 1)
    acc = grad_piece(acc, y, wy, False)
    dkeep, dsend = grad_piece(acc, far, wf, True)
    dxr = over_x(dsend)

    both_d = join(dkeep, dxr)
    de, do = over_z(both_d, 0), over_z(both_d, 1)
    dq_keep, stats = query_pass(True, keep, dkeep, keep, xkv, e0, o0, e1, o1)
    dq_send, stats = query_pass(False, xq, dxr, keep, xkv, e1, o1, e0, o0, stats)
    stats, qe1, qo1 = lax.optimization_barrier((stats, qe1, qo1))
    se, so = over_z(stats, 0), over_z(stats, 1)
    dq_got = over_x(dq_send)
    sums = own_pass(keep, xkv, xq, dkeep, dxr, stats)
    sums, dq_got = lax.optimization_barrier((sums, dq_got))
    heads = dkeep.shape[1] // HD
    got = [
        over_x(key_pass(False, (head,), xkv, e0, o0, qe1, qo1, de, do, se, so, sums))
        for head in range(heads)
    ]
    kv_keep = key_pass(True, tuple(range(heads)), keep, e0, o0, qe1, qo1, de, do, se, so, sums)
    return tuple(unpack(dq_keep, dq_got, kv_keep, *got))


def solution(mesh):
    placed = (P("ctx", "mp"), P("ctx", "mp"), P("ctx", "mp"), P("ctx", "mp"), P("mp", None))
    return jax.shard_map(
        body,
        mesh=mesh,
        in_specs=placed,
        out_specs=(P("ctx", "mp"), P("ctx", "mp"), P("ctx", "mp")),
        check_vma=False,
    )
```

```python
import functools
import math

import jax
import jax.numpy as jnp
from jax import lax
from jax.experimental import pallas as pl
from jax.experimental.pallas import tpu as pltpu
from jax.sharding import PartitionSpec as P

HD = 128
BF16 = jnp.bfloat16
F32 = jnp.float32
BIG = 1e30
ANY = pl.BlockSpec(memory_space=pl.ANY)
VM = pl.BlockSpec(memory_space=pltpu.VMEM)
HBM = pl.BlockSpec(memory_space=pltpu.HBM)


def params(mib=40):
    return pltpu.CompilerParams(vmem_limit_bytes=mib << 20)


def nt(a, b):
    return lax.dot_general(a, b, (((1,), (1,)), ((), ())), preferred_element_type=F32)


def nn(a, b):
    return lax.dot_general(a, b, (((1,), (0,)), ((), ())), preferred_element_type=F32)


def cost(flops=1):
    return pl.CostEstimate(flops=int(flops), bytes_accessed=1, transcendentals=0)


def pack_kernel(q, k, v, keep, send, sem):
    half = q.shape[1] // 2
    x = lax.rem(lax.axis_index("ctx"), 2)
    mine = pl.ds(pl.multiple_of(x * half, half), half)
    theirs = pl.ds(pl.multiple_of((1 - x) * half, half), half)
    pairs = (
        (k.at[:, theirs], send.at[0]),
        (v.at[:, theirs], send.at[1]),
        (k.at[:, mine], keep.at[0]),
        (v.at[:, mine], keep.at[1]),
        (q.at[:, mine], keep.at[2]),
        (q.at[:, theirs], send.at[2]),
    )
    copies = [pltpu.make_async_copy(a, b, sem.at[i]) for i, (a, b) in enumerate(pairs)]
    for copy in copies:
        copy.start()
    for copy in copies:
        copy.wait()


def pack(q, k, v):
    rows, cols = q.shape
    part = jax.ShapeDtypeStruct((3, rows, cols // 2), BF16)
    return pl.pallas_call(
        pack_kernel,
        out_shape=(part, part),
        in_specs=[ANY] * 3,
        out_specs=(VM,) * 2,
        scratch_shapes=[pltpu.SemaphoreType.DMA((6,))],
        compiler_params=params(60),
        cost_estimate=cost(),
        name="pack",
    )(q, k, v)


def join_kernel(mine, theirs, out):
    out[0] = mine[...]
    out[1] = theirs[...]


def join(mine, theirs):
    return pl.pallas_call(
        join_kernel,
        out_shape=jax.ShapeDtypeStruct((2, *mine.shape), BF16),
        in_specs=[VM] * 2,
        out_specs=VM,
        compiler_params=params(16),
        cost_estimate=cost(),
        name="join",
    )(mine, theirs)


def first_kernel(og, near, w, acc, wy, wf, wbuf, sem):
    width = og.shape[1]
    me = lax.axis_index("mp")
    copies = []
    for flip, target in enumerate((wbuf.at[0], wbuf.at[1], wy, wf)):
        first = pl.multiple_of(jnp.bitwise_xor(me, flip) * width, width)
        copies.append(pltpu.make_async_copy(w.at[:, pl.ds(first, width)], target, sem.at[flip]))
    for copy in copies:
        copy.start()
    copies[0].wait()
    acc[...] = nt(og[...], wbuf[0])
    copies[1].wait()
    acc[...] += nt(near[...], wbuf[1])
    copies[2].wait()
    copies[3].wait()


def first_piece(og, near, w):
    rows, width = og.shape
    heads = w.shape[0]
    part = jax.ShapeDtypeStruct((heads, width), BF16)
    return pl.pallas_call(
        first_kernel,
        out_shape=(jax.ShapeDtypeStruct((rows, heads), F32), part, part),
        in_specs=[VM, VM, ANY],
        out_specs=(VM, VM, VM),
        scratch_shapes=[pltpu.VMEM((2, heads, width), BF16), pltpu.SemaphoreType.DMA((4,))],
        compiler_params=params(46),
        cost_estimate=cost(),
        name="head_grad_first",
    )(og, near, w)


def next_kernel(acc, piece, w, out):
    out[...] = acc[...] + nt(piece[...], w[...])


def last_kernel(acc, piece, w, keep, send):
    total = acc[...] + nt(piece[...], w[...])
    half = total.shape[1] // 2
    x = lax.rem(lax.axis_index("ctx"), 2)
    low = total[:, :half].astype(BF16)
    high = total[:, half:].astype(BF16)

    @pl.when(x == 0)
    def _():
        keep[...] = low
        send[...] = high

    @pl.when(x != 0)
    def _():
        keep[...] = high
        send[...] = low


def grad_piece(acc, piece, w, last):
    rows, heads = acc.shape
    half = jax.ShapeDtypeStruct((rows, heads // 2), BF16)
    return pl.pallas_call(
        last_kernel if last else next_kernel,
        out_shape=(half, half) if last else jax.ShapeDtypeStruct((rows, heads), F32),
        in_specs=[VM] * 3,
        out_specs=(VM, VM) if last else VM,
        compiler_params=params(30),
        cost_estimate=cost(),
        name="head_grad",
    )(acc, piece, w)


def after_kernel(value, other, out):
    del value, other, out


def after(value, other):
    return pl.pallas_call(
        after_kernel,
        out_shape=jax.ShapeDtypeStruct(value.shape, value.dtype),
        in_specs=[ANY, ANY],
        out_specs=ANY,
        input_output_aliases={0: 0},
        compiler_params=params(16),
        cost_estimate=cost(1e8),
        name="after",
    )(value, other)


def place():
    position = lax.axis_index("ctx")
    block = position // 2
    low_ok = block > 0
    high_ok = block < lax.axis_size("ctx") // 2 - 1
    odd = lax.rem(block, 2) == 1
    even_ok = jnp.logical_or(jnp.logical_and(odd, low_ok), jnp.logical_and(jnp.logical_not(odd), high_ok))
    odd_ok = jnp.logical_or(jnp.logical_and(odd, high_ok), jnp.logical_and(jnp.logical_not(odd), low_ok))
    turned = lax.rem(position + block, 2) == 1
    return even_ok, odd_ok, turned


def off(ok):
    return jnp.where(ok, 0.0, BIG).astype(F32)


def query_kernel(scale, own, has_marks, *refs):
    refs = list(refs)
    q, d, keep, xr, e, o, e_other, o_other = refs[:8]
    q = q.at[q.shape[0] - 1]
    before = refs[8] if has_marks else None
    out, stats, fifth = refs[-3:]
    rows = q.shape[0]
    heads = q.shape[1] // HD
    even_ok, odd_ok, turned = place()
    from_even = turned if own else jnp.logical_not(turned)

    @pl.when(from_even)
    def _():
        fifth[...] = e_other[0:2]

    @pl.when(jnp.logical_not(from_even))
    def _():
        fifth[...] = o_other[0:2]

    c = scale * math.log2(math.e)
    even_off, odd_off = off(even_ok), off(odd_ok)
    lane = lax.broadcasted_iota(jnp.int32, (rows, HD), 1)
    runs = (
        (keep, None),
        (xr, None),
        (e, even_off),
        (o, odd_off),
        (fifth, jnp.where(from_even, even_off, odd_off)),
    )
    mark = jnp.zeros((rows, HD), F32)
    for head in range(heads):
        cols = slice(head * HD, (head + 1) * HD)
        query = q[:, cols]
        grad = d[:, cols]
        scores = [nt(query, ref[0, :, cols]) for ref, _ in runs]
        top = None
        for s, (_, gone) in zip(scores, runs):
            m = jnp.max(s, -1, keepdims=True)
            m = m if gone is None else m - gone
            top = m if top is None else jnp.maximum(top, m)
        top = top * c
        weights = [
            jnp.exp2(s * c - (top if gone is None else top + gone))
            for s, (_, gone) in zip(scores, runs)
        ]
        total = jnp.sum(sum(weights), -1, keepdims=True)
        grads = [nt(grad, ref[1, :, cols]) for ref, _ in runs]
        inverse = 1.0 / total
        delta = jnp.sum(sum(w * g for w, g in zip(weights, grads)), -1, keepdims=True) * inverse
        result = sum(
            nn((w * (g - delta)).astype(BF16), ref[0, :, cols])
            for w, g, (ref, _) in zip(weights, grads, runs)
        )
        out[:, cols] = (result * (inverse * scale)).astype(BF16)
        mark = jnp.where(lane == 2 * head, top + jnp.log2(total), mark)
        mark = jnp.where(lane == 2 * head + 1, delta, mark)
    marks = jnp.transpose(mark)[: stats.shape[0], :]
    if has_marks:
        stats[:, :rows] = before[...]
        stats[:, rows:] = marks
    else:
        stats[...] = marks


def query_pass(own, q, d, keep, xr, e, o, e_other, o_other, before=None):
    rows, cols = d.shape
    operands = [q, d, keep, xr, e, o, e_other, o_other]
    if before is not None:
        operands.append(before)
    return pl.pallas_call(
        functools.partial(query_kernel, HD ** -0.5, own, before is not None),
        out_shape=(
            jax.ShapeDtypeStruct((rows, cols), BF16),
            jax.ShapeDtypeStruct((8, rows if before is None else 2 * rows), F32),
        ),
        in_specs=[VM] * len(operands),
        out_specs=(VM, VM),
        scratch_shapes=[pltpu.VMEM((2, rows, cols), BF16)],
        compiler_params=params(30),
        cost_estimate=cost(6e9 if own else 1),
        name="query_pass",
    )(*operands)


def key_step(scale, key, value, steps):
    c = scale * math.log2(math.e)
    key_sum = None
    value_sum = None
    for query, grad, total, delta in steps:
        weight = jnp.exp2(nt(key, query) * c - total)
        change = weight * (nt(value, grad) - delta)
        v = nn(weight.astype(BF16), grad)
        k = nn(change.astype(BF16), query)
        value_sum = v if value_sum is None else value_sum + v
        key_sum = k if key_sum is None else key_sum + k
    return key_sum, value_sum


def own_kernel(scale, keep, xr, dkeep, dxr, stats, sums):
    rows = keep.shape[1]
    heads = keep.shape[2] // HD
    for mine, keys in enumerate((keep, xr)):
        for head in range(heads):
            cols = slice(head * HD, (head + 1) * HD)
            steps = []
            for i, (q, d) in enumerate(((keep.at[2], dkeep), (xr.at[2], dxr))):
                span = slice(i * rows, (i + 1) * rows)
                steps.append((
                    q[:, cols],
                    d[:, cols],
                    stats[2 * head : 2 * head + 1, span],
                    stats[2 * head + 1 : 2 * head + 2, span],
                ))
            k, v = key_step(scale, keys[0, :, cols], keys[1, :, cols], steps)
            sums[mine, 0, :, cols] = k
            sums[mine, 1, :, cols] = v


def own_pass(*operands):
    _, rows, cols = operands[0].shape
    return pl.pallas_call(
        functools.partial(own_kernel, HD ** -0.5),
        out_shape=jax.ShapeDtypeStruct((2, 2, rows, cols), F32),
        in_specs=[VM] * 5,
        out_specs=VM,
        compiler_params=params(30),
        cost_estimate=cost(),
        name="own_pass",
    )(*operands)


def key_kernel(scale, own, heads, kv, e0, o0, e1, o1, de, do, se, so, sums, out, fifth_q, fifth_d):
    rows = kv.shape[1]
    even_ok, odd_ok, turned = place()
    from_even = turned if own else jnp.logical_not(turned)
    even_q = (e0.at[e0.shape[0] - 1], e1.at[e1.shape[0] - 1])
    odd_q = (o0.at[o0.shape[0] - 1], o1.at[o1.shape[0] - 1])
    same, other = (0, 1) if own else (1, 0)
    wanted = slice(heads[0] * HD, (heads[-1] + 1) * HD)

    @pl.when(from_even)
    def _():
        fifth_q[...] = even_q[other][:, wanted]
        fifth_d[...] = de[other, :, wanted]

    @pl.when(jnp.logical_not(from_even))
    def _():
        fifth_q[...] = odd_q[other][:, wanted]
        fifth_d[...] = do[other, :, wanted]

    row = lax.broadcasted_iota(jnp.int32, se.shape, 0)
    nothing = jnp.where(lax.rem(row, 2) == 0, jnp.float32(BIG), jnp.float32(0.0))
    even = jnp.where(even_ok, se[...], nothing)
    odd = jnp.where(odd_ok, so[...], nothing)
    span = slice(same * rows, (same + 1) * rows)
    across = slice(other * rows, (other + 1) * rows)
    fifth = jnp.where(from_even, even[:, across], odd[:, across])
    for i, head in enumerate(heads):
        cols = slice(head * HD, (head + 1) * HD)
        to = slice(i * HD, (i + 1) * HD)
        a, b = 2 * head, 2 * head + 1
        steps = (
            (even_q[same][:, cols], de[same, :, cols], even[a : a + 1, span], even[b : b + 1, span]),
            (odd_q[same][:, cols], do[same, :, cols], odd[a : a + 1, span], odd[b : b + 1, span]),
            (fifth_q[:, to], fifth_d[:, to], fifth[a : a + 1], fifth[b : b + 1]),
        )
        k, v = key_step(scale, kv[0, :, cols], kv[1, :, cols], steps)
        out[0, :, to] = ((k + sums[same, 0, :, cols]) * scale).astype(BF16)
        out[1, :, to] = (v + sums[same, 1, :, cols]).astype(BF16)


def key_pass(own, heads, kv, *operands):
    _, rows, _ = kv.shape
    wide = HD * len(heads)
    return pl.pallas_call(
        functools.partial(key_kernel, HD ** -0.5, own, heads),
        out_shape=jax.ShapeDtypeStruct((2, rows, wide), BF16),
        in_specs=[VM] * (1 + len(operands)),
        out_specs=VM,
        scratch_shapes=[pltpu.VMEM((rows, wide), BF16)] * 2,
        compiler_params=params(30),
        cost_estimate=cost(),
        name="key_pass",
    )(kv, *operands)


def unpack_kernel(q_keep, q_got, kv_keep, *refs):
    got, (dq, dk, dv) = refs[:-3], refs[-3:]
    half = q_keep.shape[1]
    x = lax.rem(lax.axis_index("ctx"), 2)
    mine = pl.multiple_of(x * half, half)
    theirs = pl.multiple_of((1 - x) * half, half)
    dq[:, pl.ds(mine, half)] = q_keep[...]
    dq[:, pl.ds(theirs, half)] = q_got[...]
    for i, out in enumerate((dk, dv)):
        out[:, pl.ds(mine, half)] = kv_keep[i]
        first = 0
        for piece in got:
            width = piece.shape[2]
            out[:, pl.ds(theirs + first, width)] = piece[i]
            first += width


def unpack(q_keep, q_got, kv_keep, *got):
    rows, half = q_keep.shape
    whole = jax.ShapeDtypeStruct((rows, 2 * half), BF16)
    return pl.pallas_call(
        unpack_kernel,
        out_shape=(whole,) * 3,
        in_specs=[VM] * (3 + len(got)),
        out_specs=(VM,) * 3,
        compiler_params=params(16),
        cost_estimate=cost(),
        name="unpack",
    )(q_keep, q_got, kv_keep, *got)


def body(queries, keys, values, out_grad, out_weight):
    length = lax.axis_size("ctx")
    lanes = lax.axis_size("mp")
    blocks = length // 2
    width = out_grad.shape[1]

    def over_mp(array, flip):
        return lax.ppermute(array, "mp", [(i, i ^ flip) for i in range(lanes)])

    def over_x(array):
        return lax.ppermute(array, "ctx", [(i, i ^ 1) for i in range(length)])

    def over_z(array, first):
        pairs = []
        for position in range(length):
            block = position // 2
            other = ((block - first) ^ 1) + first
            for lane in range(lanes):
                source = position * lanes + lane
                if block >= first and other < blocks:
                    target = (2 * other + position % 2) * lanes + lane
                else:
                    target = position * lanes + (lane ^ 1)
                pairs.append((source, target))
        return lax.ppermute(array, ("ctx", "mp"), pairs)

    y = over_mp(out_grad, 2)
    near = over_mp(out_grad, 1)
    keep, send = pack(queries, keys, values)
    xr = over_x(send)
    e0, o0 = over_z(keep, 0), over_z(keep, 1)
    acc, wy, wf = first_piece(out_grad, near, out_weight)
    e1, o1 = over_z(xr, 0), over_z(xr, 1)
    acc = after(acc, xr)
    y, e0, o0, acc = lax.optimization_barrier((y, e0, o0, acc))
    far = over_mp(y, 1)
    acc = grad_piece(acc, y, wy, False)
    dkeep, dsend = grad_piece(acc, far, wf, True)
    dxr = over_x(dsend)

    both_d = join(dkeep, dxr)
    de, do = over_z(both_d, 0), over_z(both_d, 1)
    dq_keep, stats = query_pass(True, keep, dkeep, keep, xr, e0, o0, e1, o1)
    dq_send, stats = query_pass(False, xr, dxr, keep, xr, e1, o1, e0, o0, stats)
    se, so = over_z(stats, 0), over_z(stats, 1)
    dq_got = over_x(dq_send)
    sums = own_pass(keep, xr, dkeep, dxr, stats)
    sums, dq_got = lax.optimization_barrier((sums, dq_got))
    heads = dkeep.shape[1] // HD
    got = [
        over_x(key_pass(False, (head,), xr, e0, o0, e1, o1, de, do, se, so, sums))
        for head in range(heads)
    ]
    kv_keep = key_pass(True, tuple(range(heads)), keep, e0, o0, e1, o1, de, do, se, so, sums)
    return tuple(unpack(dq_keep, dq_got, kv_keep, *got))


def solution(mesh):
    placed = (P("ctx", "mp"), P("ctx", "mp"), P("ctx", "mp"), P("ctx", "mp"), P("mp", None))
    return jax.shard_map(
        body,
        mesh=mesh,
        in_specs=placed,
        out_specs=(P("ctx", "mp"), P("ctx", "mp"), P("ctx", "mp")),
        check_vma=False,
    )
```

```python
import functools
import math

import jax
import jax.numpy as jnp
from jax import lax
from jax.experimental import pallas as pl
from jax.experimental.pallas import tpu as pltpu
from jax.sharding import PartitionSpec as P

HD = 128
BF16 = jnp.bfloat16
F32 = jnp.float32
BIG = 1e30
ANY = pl.BlockSpec(memory_space=pl.ANY)
VM = pl.BlockSpec(memory_space=pltpu.VMEM)
HBM = pl.BlockSpec(memory_space=pltpu.HBM)


def params(mib=40):
    return pltpu.CompilerParams(vmem_limit_bytes=mib << 20)


def nt(a, b):
    return lax.dot_general(a, b, (((1,), (1,)), ((), ())), preferred_element_type=F32)


def nn(a, b):
    return lax.dot_general(a, b, (((1,), (0,)), ((), ())), preferred_element_type=F32)


def cost(flops=1):
    return pl.CostEstimate(flops=int(flops), bytes_accessed=1, transcendentals=0)


def pack_kernel(q, k, v, keep, send, sem):
    half = q.shape[1] // 2
    x = lax.rem(lax.axis_index("ctx"), 2)
    mine = pl.ds(pl.multiple_of(x * half, half), half)
    theirs = pl.ds(pl.multiple_of((1 - x) * half, half), half)
    pairs = (
        (k.at[:, theirs], send.at[0]),
        (v.at[:, theirs], send.at[1]),
        (k.at[:, mine], keep.at[0]),
        (v.at[:, mine], keep.at[1]),
        (q.at[:, mine], keep.at[2]),
        (q.at[:, theirs], send.at[2]),
    )
    copies = [pltpu.make_async_copy(a, b, sem.at[i]) for i, (a, b) in enumerate(pairs)]
    for copy in copies:
        copy.start()
    for copy in copies:
        copy.wait()


def pack(q, k, v):
    rows, cols = q.shape
    part = jax.ShapeDtypeStruct((3, rows, cols // 2), BF16)
    return pl.pallas_call(
        pack_kernel,
        out_shape=(part, part),
        in_specs=[ANY] * 3,
        out_specs=(VM,) * 2,
        scratch_shapes=[pltpu.SemaphoreType.DMA((6,))],
        compiler_params=params(60),
        cost_estimate=cost(),
        name="pack",
    )(q, k, v)


def join_kernel(mine, theirs, out):
    out[0] = mine[...]
    out[1] = theirs[...]


def join(mine, theirs):
    return pl.pallas_call(
        join_kernel,
        out_shape=jax.ShapeDtypeStruct((2, *mine.shape), BF16),
        in_specs=[VM] * 2,
        out_specs=VM,
        compiler_params=params(16),
        cost_estimate=cost(),
        name="join",
    )(mine, theirs)


def first_kernel(og, near, w, acc, wy, wf, wbuf, sem):
    width = og.shape[1]
    me = lax.axis_index("mp")
    copies = []
    for flip, target in enumerate((wbuf.at[0], wbuf.at[1], wy, wf)):
        first = pl.multiple_of(jnp.bitwise_xor(me, flip) * width, width)
        copies.append(pltpu.make_async_copy(w.at[:, pl.ds(first, width)], target, sem.at[flip]))
    for copy in copies:
        copy.start()
    copies[0].wait()
    acc[...] = nt(og[...], wbuf[0])
    copies[1].wait()
    acc[...] += nt(near[...], wbuf[1])
    copies[2].wait()
    copies[3].wait()


def first_piece(og, near, w):
    rows, width = og.shape
    heads = w.shape[0]
    part = jax.ShapeDtypeStruct((heads, width), BF16)
    return pl.pallas_call(
        first_kernel,
        out_shape=(jax.ShapeDtypeStruct((rows, heads), F32), part, part),
        in_specs=[VM, VM, ANY],
        out_specs=(VM, VM, VM),
        scratch_shapes=[pltpu.VMEM((2, heads, width), BF16), pltpu.SemaphoreType.DMA((4,))],
        compiler_params=params(46),
        cost_estimate=cost(),
        name="head_grad_first",
    )(og, near, w)


def next_kernel(acc, piece, w, out):
    out[...] = acc[...] + nt(piece[...], w[...])


def last_kernel(acc, piece, w, keep, send):
    total = acc[...] + nt(piece[...], w[...])
    half = total.shape[1] // 2
    x = lax.rem(lax.axis_index("ctx"), 2)
    low = total[:, :half].astype(BF16)
    high = total[:, half:].astype(BF16)

    @pl.when(x == 0)
    def _():
        keep[...] = low
        send[...] = high

    @pl.when(x != 0)
    def _():
        keep[...] = high
        send[...] = low


def grad_piece(acc, piece, w, last):
    rows, heads = acc.shape
    half = jax.ShapeDtypeStruct((rows, heads // 2), BF16)
    return pl.pallas_call(
        last_kernel if last else next_kernel,
        out_shape=(half, half) if last else jax.ShapeDtypeStruct((rows, heads), F32),
        in_specs=[VM] * 3,
        out_specs=(VM, VM) if last else VM,
        compiler_params=params(30),
        cost_estimate=cost(),
        name="head_grad",
    )(acc, piece, w)


def after(value, *others, flops):
    return pl.pallas_call(
        lambda *refs: None,
        out_shape=jax.ShapeDtypeStruct(value.shape, value.dtype),
        in_specs=[ANY] * (1 + len(others)),
        out_specs=ANY,
        input_output_aliases={0: 0},
        compiler_params=params(16),
        cost_estimate=cost(flops),
        name="after",
    )(value, *others)


def place():
    position = lax.axis_index("ctx")
    block = position // 2
    low_ok = block > 0
    high_ok = block < lax.axis_size("ctx") // 2 - 1
    odd = lax.rem(block, 2) == 1
    even_ok = jnp.logical_or(jnp.logical_and(odd, low_ok), jnp.logical_and(jnp.logical_not(odd), high_ok))
    odd_ok = jnp.logical_or(jnp.logical_and(odd, high_ok), jnp.logical_and(jnp.logical_not(odd), low_ok))
    turned = lax.rem(position + block, 2) == 1
    return even_ok, odd_ok, turned


def off(ok):
    return jnp.where(ok, 0.0, BIG).astype(F32)


def query_kernel(scale, own, has_marks, *refs):
    refs = list(refs)
    q, d, keep, xr, e, o, e_other, o_other = refs[:8]
    q = q.at[q.shape[0] - 1]
    before = refs[8] if has_marks else None
    out, stats, fifth = refs[-3:]
    rows = q.shape[0]
    heads = q.shape[1] // HD
    even_ok, odd_ok, turned = place()
    from_even = turned if own else jnp.logical_not(turned)

    @pl.when(from_even)
    def _():
        fifth[...] = e_other[0:2]

    @pl.when(jnp.logical_not(from_even))
    def _():
        fifth[...] = o_other[0:2]

    c = scale * math.log2(math.e)
    even_off, odd_off = off(even_ok), off(odd_ok)
    lane = lax.broadcasted_iota(jnp.int32, (rows, HD), 1)
    runs = (
        (keep, None),
        (xr, None),
        (e, even_off),
        (o, odd_off),
        (fifth, jnp.where(from_even, even_off, odd_off)),
    )
    mark = jnp.zeros((rows, HD), F32)
    for head in range(heads):
        cols = slice(head * HD, (head + 1) * HD)
        query = q[:, cols]
        grad = d[:, cols]
        scores = [nt(query, ref[0, :, cols]) for ref, _ in runs]
        top = None
        for s, (_, gone) in zip(scores, runs):
            m = jnp.max(s, -1, keepdims=True)
            m = m if gone is None else m - gone
            top = m if top is None else jnp.maximum(top, m)
        top = top * c
        weights = [
            jnp.exp2(s * c - (top if gone is None else top + gone))
            for s, (_, gone) in zip(scores, runs)
        ]
        total = jnp.sum(sum(weights), -1, keepdims=True)
        grads = [nt(grad, ref[1, :, cols]) for ref, _ in runs]
        inverse = 1.0 / total
        delta = jnp.sum(sum(w * g for w, g in zip(weights, grads)), -1, keepdims=True) * inverse
        result = sum(
            nn((w * (g - delta)).astype(BF16), ref[0, :, cols])
            for w, g, (ref, _) in zip(weights, grads, runs)
        )
        out[:, cols] = (result * (inverse * scale)).astype(BF16)
        mark = jnp.where(lane == 2 * head, top + jnp.log2(total), mark)
        mark = jnp.where(lane == 2 * head + 1, delta, mark)
    marks = jnp.transpose(mark)[: stats.shape[0], :]
    if has_marks:
        stats[:, :rows] = before[...]
        stats[:, rows:] = marks
    else:
        stats[...] = marks


def query_pass(own, q, d, keep, xr, e, o, e_other, o_other, before=None):
    rows, cols = d.shape
    operands = [q, d, keep, xr, e, o, e_other, o_other]
    if before is not None:
        operands.append(before)
    return pl.pallas_call(
        functools.partial(query_kernel, HD ** -0.5, own, before is not None),
        out_shape=(
            jax.ShapeDtypeStruct((rows, cols), BF16),
            jax.ShapeDtypeStruct((8, rows if before is None else 2 * rows), F32),
        ),
        in_specs=[VM] * len(operands),
        out_specs=(VM, VM),
        scratch_shapes=[pltpu.VMEM((2, rows, cols), BF16)],
        compiler_params=params(30),
        cost_estimate=cost(6e9 if own else 1),
        name="query_pass",
    )(*operands)


def key_step(scale, key, value, steps):
    c = scale * math.log2(math.e)
    key_sum = None
    value_sum = None
    for query, grad, total, delta in steps:
        weight = jnp.exp2(nt(key, query) * c - total)
        change = weight * (nt(value, grad) - delta)
        v = nn(weight.astype(BF16), grad)
        k = nn(change.astype(BF16), query)
        value_sum = v if value_sum is None else value_sum + v
        key_sum = k if key_sum is None else key_sum + k
    return key_sum, value_sum


def own_kernel(scale, keep, xr, dkeep, dxr, stats, sums):
    rows = keep.shape[1]
    heads = keep.shape[2] // HD
    for mine, keys in enumerate((keep, xr)):
        for head in range(heads):
            cols = slice(head * HD, (head + 1) * HD)
            steps = []
            for i, (q, d) in enumerate(((keep.at[2], dkeep), (xr.at[2], dxr))):
                span = slice(i * rows, (i + 1) * rows)
                steps.append((
                    q[:, cols],
                    d[:, cols],
                    stats[2 * head : 2 * head + 1, span],
                    stats[2 * head + 1 : 2 * head + 2, span],
                ))
            k, v = key_step(scale, keys[0, :, cols], keys[1, :, cols], steps)
            sums[mine, 0, :, cols] = k
            sums[mine, 1, :, cols] = v


def own_pass(*operands):
    _, rows, cols = operands[0].shape
    return pl.pallas_call(
        functools.partial(own_kernel, HD ** -0.5),
        out_shape=jax.ShapeDtypeStruct((2, 2, rows, cols), F32),
        in_specs=[VM] * 5,
        out_specs=VM,
        compiler_params=params(30),
        cost_estimate=cost(),
        name="own_pass",
    )(*operands)


def key_kernel(scale, own, heads, kv, e0, o0, e1, o1, de, do, se, so, sums, out, fifth_q, fifth_d):
    rows = kv.shape[1]
    even_ok, odd_ok, turned = place()
    from_even = turned if own else jnp.logical_not(turned)
    even_q = (e0.at[e0.shape[0] - 1], e1.at[e1.shape[0] - 1])
    odd_q = (o0.at[o0.shape[0] - 1], o1.at[o1.shape[0] - 1])
    same, other = (0, 1) if own else (1, 0)
    wanted = slice(heads[0] * HD, (heads[-1] + 1) * HD)

    @pl.when(from_even)
    def _():
        fifth_q[...] = even_q[other][:, wanted]
        fifth_d[...] = de[other, :, wanted]

    @pl.when(jnp.logical_not(from_even))
    def _():
        fifth_q[...] = odd_q[other][:, wanted]
        fifth_d[...] = do[other, :, wanted]

    row = lax.broadcasted_iota(jnp.int32, se.shape, 0)
    nothing = jnp.where(lax.rem(row, 2) == 0, jnp.float32(BIG), jnp.float32(0.0))
    even = jnp.where(even_ok, se[...], nothing)
    odd = jnp.where(odd_ok, so[...], nothing)
    span = slice(same * rows, (same + 1) * rows)
    across = slice(other * rows, (other + 1) * rows)
    fifth = jnp.where(from_even, even[:, across], odd[:, across])
    for i, head in enumerate(heads):
        cols = slice(head * HD, (head + 1) * HD)
        to = slice(i * HD, (i + 1) * HD)
        a, b = 2 * head, 2 * head + 1
        steps = (
            (even_q[same][:, cols], de[same, :, cols], even[a : a + 1, span], even[b : b + 1, span]),
            (odd_q[same][:, cols], do[same, :, cols], odd[a : a + 1, span], odd[b : b + 1, span]),
            (fifth_q[:, to], fifth_d[:, to], fifth[a : a + 1], fifth[b : b + 1]),
        )
        k, v = key_step(scale, kv[0, :, cols], kv[1, :, cols], steps)
        out[0, :, to] = ((k + sums[same, 0, :, cols]) * scale).astype(BF16)
        out[1, :, to] = (v + sums[same, 1, :, cols]).astype(BF16)


def key_pass(own, heads, kv, *operands):
    _, rows, _ = kv.shape
    wide = HD * len(heads)
    return pl.pallas_call(
        functools.partial(key_kernel, HD ** -0.5, own, heads),
        out_shape=jax.ShapeDtypeStruct((2, rows, wide), BF16),
        in_specs=[VM] * (1 + len(operands)),
        out_specs=VM,
        scratch_shapes=[pltpu.VMEM((rows, wide), BF16)] * 2,
        compiler_params=params(30),
        cost_estimate=cost(),
        name="key_pass",
    )(kv, *operands)


def unpack_kernel(q_keep, q_got, kv_keep, *refs):
    got, (dq, dk, dv) = refs[:-3], refs[-3:]
    half = q_keep.shape[1]
    x = lax.rem(lax.axis_index("ctx"), 2)
    mine = pl.multiple_of(x * half, half)
    theirs = pl.multiple_of((1 - x) * half, half)
    dq[:, pl.ds(mine, half)] = q_keep[...]
    dq[:, pl.ds(theirs, half)] = q_got[...]
    for i, out in enumerate((dk, dv)):
        out[:, pl.ds(mine, half)] = kv_keep[i]
        first = 0
        for piece in got:
            width = piece.shape[2]
            out[:, pl.ds(theirs + first, width)] = piece[i]
            first += width


def unpack(q_keep, q_got, kv_keep, *got):
    rows, half = q_keep.shape
    whole = jax.ShapeDtypeStruct((rows, 2 * half), BF16)
    return pl.pallas_call(
        unpack_kernel,
        out_shape=(whole,) * 3,
        in_specs=[VM] * (3 + len(got)),
        out_specs=(VM,) * 3,
        compiler_params=params(16),
        cost_estimate=cost(),
        name="unpack",
    )(q_keep, q_got, kv_keep, *got)


def body(queries, keys, values, out_grad, out_weight):
    length = lax.axis_size("ctx")
    lanes = lax.axis_size("mp")
    blocks = length // 2
    width = out_grad.shape[1]

    def over_mp(array, flip):
        return lax.ppermute(array, "mp", [(i, i ^ flip) for i in range(lanes)])

    def over_x(array):
        return lax.ppermute(array, "ctx", [(i, i ^ 1) for i in range(length)])

    def over_z(array, first):
        pairs = []
        for position in range(length):
            block = position // 2
            other = ((block - first) ^ 1) + first
            for lane in range(lanes):
                source = position * lanes + lane
                if block >= first and other < blocks:
                    target = (2 * other + position % 2) * lanes + lane
                else:
                    target = position * lanes + (lane ^ 1)
                pairs.append((source, target))
        return lax.ppermute(array, ("ctx", "mp"), pairs)

    y = over_mp(out_grad, 2)
    near = over_mp(out_grad, 1)
    keep, send = pack(queries, keys, values)
    xr = over_x(send)
    e0, o0 = over_z(keep, 0), over_z(keep, 1)
    acc, wy, wf = first_piece(out_grad, near, out_weight)
    e1, o1 = over_z(xr, 0), over_z(xr, 1)
    acc = after(acc, xr, flops=1e8)
    y, acc = lax.optimization_barrier((y, acc))
    far = over_mp(y, 1)
    acc = grad_piece(acc, y, wy, False)
    acc = after(acc, e0, o0, flops=3e9)
    dkeep, dsend = grad_piece(acc, far, wf, True)
    dxr = over_x(dsend)

    both_d = join(dkeep, dxr)
    de, do = over_z(both_d, 0), over_z(both_d, 1)
    dq_keep, stats = query_pass(True, keep, dkeep, keep, xr, e0, o0, e1, o1)
    dq_send, stats = query_pass(False, xr, dxr, keep, xr, e1, o1, e0, o0, stats)
    se, so = over_z(stats, 0), over_z(stats, 1)
    dq_got = over_x(dq_send)
    sums = own_pass(keep, xr, dkeep, dxr, stats)
    heads = dkeep.shape[1] // HD
    got = []
    for head in range(heads):
        if head == 1:
            sums, dq_got = lax.optimization_barrier((sums, dq_got))
        got.append(over_x(key_pass(False, (head,), xr, e0, o0, e1, o1, de, do, se, so, sums)))
    kv_keep = key_pass(True, tuple(range(heads)), keep, e0, o0, e1, o1, de, do, se, so, sums)
    return tuple(unpack(dq_keep, dq_got, kv_keep, *got))


def solution(mesh):
    placed = (P("ctx", "mp"), P("ctx", "mp"), P("ctx", "mp"), P("ctx", "mp"), P("mp", None))
    return jax.shard_map(
        body,
        mesh=mesh,
        in_specs=placed,
        out_specs=(P("ctx", "mp"), P("ctx", "mp"), P("ctx", "mp")),
        check_vma=False,
    )
```

```python
import functools
import math

import jax
import jax.numpy as jnp
from jax import lax
from jax.experimental import pallas as pl
from jax.experimental.pallas import tpu as pltpu
from jax.sharding import PartitionSpec as P

HD = 128
BF16 = jnp.bfloat16
F32 = jnp.float32
BIG = 1e30
ANY = pl.BlockSpec(memory_space=pl.ANY)
VM = pl.BlockSpec(memory_space=pltpu.VMEM)
HBM = pl.BlockSpec(memory_space=pltpu.HBM)


def params(mib=40):
    return pltpu.CompilerParams(vmem_limit_bytes=mib << 20)


def nt(a, b):
    return lax.dot_general(a, b, (((1,), (1,)), ((), ())), preferred_element_type=F32)


def nn(a, b):
    return lax.dot_general(a, b, (((1,), (0,)), ((), ())), preferred_element_type=F32)


def cost(flops=1):
    return pl.CostEstimate(flops=int(flops), bytes_accessed=1, transcendentals=0)


def pack_kernel(q, k, v, keep, send_kv, send_q, sem):
    half = q.shape[1] // 2
    x = lax.rem(lax.axis_index("ctx"), 2)
    mine = pl.ds(pl.multiple_of(x * half, half), half)
    theirs = pl.ds(pl.multiple_of((1 - x) * half, half), half)
    pairs = (
        (k.at[:, theirs], send_kv.at[0]),
        (v.at[:, theirs], send_kv.at[1]),
        (k.at[:, mine], keep.at[0]),
        (v.at[:, mine], keep.at[1]),
        (q.at[:, mine], keep.at[2]),
        (q.at[:, theirs], send_q),
    )
    copies = [pltpu.make_async_copy(a, b, sem.at[i]) for i, (a, b) in enumerate(pairs)]
    for copy in copies:
        copy.start()
    for copy in copies:
        copy.wait()


def pack(q, k, v):
    rows, cols = q.shape
    three, two = (jax.ShapeDtypeStruct((n, rows, cols // 2), BF16) for n in (3, 2))
    one = jax.ShapeDtypeStruct((rows, cols // 2), BF16)
    return pl.pallas_call(
        pack_kernel,
        out_shape=(three, two, one),
        in_specs=[ANY] * 3,
        out_specs=(VM,) * 3,
        scratch_shapes=[pltpu.SemaphoreType.DMA((6,))],
        compiler_params=params(60),
        cost_estimate=cost(),
        name="pack",
    )(q, k, v)


def join_kernel(first, second, out):
    out[0] = first[...]
    out[1] = second[...]


def join(first, second):
    return pl.pallas_call(
        join_kernel,
        out_shape=jax.ShapeDtypeStruct((2, *first.shape), BF16),
        in_specs=[VM] * 2,
        out_specs=VM,
        compiler_params=params(16),
        cost_estimate=cost(),
        name="join",
    )(first, second)


def first_kernel(og, near, w, acc, wy, wf, wbuf, sem):
    width = og.shape[1]
    me = lax.axis_index("mp")
    copies = []
    for flip, target in enumerate((wbuf.at[0], wbuf.at[1], wy, wf)):
        first = pl.multiple_of(jnp.bitwise_xor(me, flip) * width, width)
        copies.append(pltpu.make_async_copy(w.at[:, pl.ds(first, width)], target, sem.at[flip]))
    for copy in copies:
        copy.start()
    copies[0].wait()
    acc[...] = nt(og[...], wbuf[0])
    copies[1].wait()
    acc[...] += nt(near[...], wbuf[1])
    copies[2].wait()
    copies[3].wait()


def first_piece(og, near, w):
    rows, width = og.shape
    heads = w.shape[0]
    part = jax.ShapeDtypeStruct((heads, width), BF16)
    return pl.pallas_call(
        first_kernel,
        out_shape=(jax.ShapeDtypeStruct((rows, heads), F32), part, part),
        in_specs=[VM, VM, ANY],
        out_specs=(VM, VM, VM),
        scratch_shapes=[pltpu.VMEM((2, heads, width), BF16), pltpu.SemaphoreType.DMA((4,))],
        compiler_params=params(46),
        cost_estimate=cost(),
        name="head_grad_first",
    )(og, near, w)


def next_kernel(acc, piece, w, out):
    out[...] = acc[...] + nt(piece[...], w[...])


def last_kernel(acc, piece, w, keep, send):
    total = acc[...] + nt(piece[...], w[...])
    half = total.shape[1] // 2
    x = lax.rem(lax.axis_index("ctx"), 2)
    low = total[:, :half].astype(BF16)
    high = total[:, half:].astype(BF16)

    @pl.when(x == 0)
    def _():
        keep[...] = low
        send[...] = high

    @pl.when(x != 0)
    def _():
        keep[...] = high
        send[...] = low


def grad_piece(acc, piece, w, last):
    rows, heads = acc.shape
    half = jax.ShapeDtypeStruct((rows, heads // 2), BF16)
    return pl.pallas_call(
        last_kernel if last else next_kernel,
        out_shape=(half, half) if last else jax.ShapeDtypeStruct((rows, heads), F32),
        in_specs=[VM] * 3,
        out_specs=(VM, VM) if last else VM,
        compiler_params=params(30),
        cost_estimate=cost(),
        name="head_grad",
    )(acc, piece, w)


def after(value, *others, flops):
    return pl.pallas_call(
        lambda *refs: None,
        out_shape=jax.ShapeDtypeStruct(value.shape, value.dtype),
        in_specs=[ANY] * (1 + len(others)),
        out_specs=ANY,
        input_output_aliases={0: 0},
        compiler_params=params(16),
        cost_estimate=cost(flops),
        name="after",
    )(value, *others)


def place():
    position = lax.axis_index("ctx")
    block = position // 2
    low_ok = block > 0
    high_ok = block < lax.axis_size("ctx") // 2 - 1
    odd = lax.rem(block, 2) == 1
    even_ok = jnp.logical_or(jnp.logical_and(odd, low_ok), jnp.logical_and(jnp.logical_not(odd), high_ok))
    odd_ok = jnp.logical_or(jnp.logical_and(odd, high_ok), jnp.logical_and(jnp.logical_not(odd), low_ok))
    turned = lax.rem(position + block, 2) == 1
    return even_ok, odd_ok, turned


def off(ok):
    return jnp.where(ok, 0.0, BIG).astype(F32)


def query_kernel(scale, own, has_marks, *refs):
    refs = list(refs)
    q, d, keep, xr, e, o, e_other, o_other = refs[:8]
    q = q if len(q.shape) == 2 else q.at[2]
    before = refs[8] if has_marks else None
    out, stats, fifth = refs[-3:]
    rows = q.shape[0]
    heads = q.shape[1] // HD
    even_ok, odd_ok, turned = place()
    from_even = turned if own else jnp.logical_not(turned)

    @pl.when(from_even)
    def _():
        fifth[...] = e_other[0:2]

    @pl.when(jnp.logical_not(from_even))
    def _():
        fifth[...] = o_other[0:2]

    c = scale * math.log2(math.e)
    even_off, odd_off = off(even_ok), off(odd_ok)
    lane = lax.broadcasted_iota(jnp.int32, (rows, HD), 1)
    runs = (
        (keep, None),
        (xr, None),
        (e, even_off),
        (o, odd_off),
        (fifth, jnp.where(from_even, even_off, odd_off)),
    )
    mark = jnp.zeros((rows, HD), F32)
    for head in range(heads):
        cols = slice(head * HD, (head + 1) * HD)
        query = q[:, cols]
        grad = d[:, cols]
        scores = [nt(query, ref[0, :, cols]) for ref, _ in runs]
        top = None
        for s, (_, gone) in zip(scores, runs):
            m = jnp.max(s, -1, keepdims=True)
            m = m if gone is None else m - gone
            top = m if top is None else jnp.maximum(top, m)
        top = top * c
        weights = [
            jnp.exp2(s * c - (top if gone is None else top + gone))
            for s, (_, gone) in zip(scores, runs)
        ]
        total = jnp.sum(sum(weights), -1, keepdims=True)
        grads = [nt(grad, ref[1, :, cols]) for ref, _ in runs]
        inverse = 1.0 / total
        delta = jnp.sum(sum(w * g for w, g in zip(weights, grads)), -1, keepdims=True) * inverse
        result = sum(
            nn((w * (g - delta)).astype(BF16), ref[0, :, cols])
            for w, g, (ref, _) in zip(weights, grads, runs)
        )
        out[:, cols] = (result * (inverse * scale)).astype(BF16)
        mark = jnp.where(lane == 2 * head, top + jnp.log2(total), mark)
        mark = jnp.where(lane == 2 * head + 1, delta, mark)
    marks = jnp.transpose(mark)[: stats.shape[0], :]
    if has_marks:
        stats[:, :rows] = before[...]
        stats[:, rows:] = marks
    else:
        stats[...] = marks


def query_pass(own, q, d, keep, xr, e, o, e_other, o_other, before=None):
    rows, cols = d.shape
    operands = [q, d, keep, xr, e, o, e_other, o_other]
    if before is not None:
        operands.append(before)
    return pl.pallas_call(
        functools.partial(query_kernel, HD ** -0.5, own, before is not None),
        out_shape=(
            jax.ShapeDtypeStruct((rows, cols), BF16),
            jax.ShapeDtypeStruct((8, rows if before is None else 2 * rows), F32),
        ),
        in_specs=[VM] * len(operands),
        out_specs=(VM, VM),
        scratch_shapes=[pltpu.VMEM((2, rows, cols), BF16)],
        compiler_params=params(30),
        cost_estimate=cost(6e9 if own else 1),
        name="query_pass",
    )(*operands)


def key_step(scale, key, value, steps):
    c = scale * math.log2(math.e)
    key_sum = None
    value_sum = None
    for query, grad, total, delta in steps:
        weight = jnp.exp2(nt(key, query) * c - total)
        change = weight * (nt(value, grad) - delta)
        v = nn(weight.astype(BF16), grad)
        k = nn(change.astype(BF16), query)
        value_sum = v if value_sum is None else value_sum + v
        key_sum = k if key_sum is None else key_sum + k
    return key_sum, value_sum


def own_kernel(scale, keep, xkv, xq, dkeep, dxr, stats, sums):
    rows = keep.shape[1]
    heads = keep.shape[2] // HD
    for mine, keys in enumerate((keep, xkv)):
        for head in range(heads):
            cols = slice(head * HD, (head + 1) * HD)
            steps = []
            for i, (q, d) in enumerate(((keep.at[2], dkeep), (xq, dxr))):
                span = slice(i * rows, (i + 1) * rows)
                steps.append((
                    q[:, cols],
                    d[:, cols],
                    stats[2 * head : 2 * head + 1, span],
                    stats[2 * head + 1 : 2 * head + 2, span],
                ))
            k, v = key_step(scale, keys[0, :, cols], keys[1, :, cols], steps)
            sums[mine, 0, :, cols] = k
            sums[mine, 1, :, cols] = v


def own_pass(*operands):
    _, rows, cols = operands[0].shape
    return pl.pallas_call(
        functools.partial(own_kernel, HD ** -0.5),
        out_shape=jax.ShapeDtypeStruct((2, 2, rows, cols), F32),
        in_specs=[VM] * 6,
        out_specs=VM,
        compiler_params=params(30),
        cost_estimate=cost(),
        name="own_pass",
    )(*operands)


def key_kernel(scale, own, heads, kv, e0, o0, mixed_e, mixed_o, de1, do1, se, so, sums, out, fifth_q, fifth_d):
    rows = kv.shape[1]
    even_ok, odd_ok, turned = place()
    from_even = turned if own else jnp.logical_not(turned)
    even_q, odd_q = (e0.at[2], mixed_e.at[0]), (o0.at[2], mixed_o.at[0])
    even_d, odd_d = (mixed_e.at[1], de1), (mixed_o.at[1], do1)
    same, other = (0, 1) if own else (1, 0)
    wanted = slice(heads[0] * HD, (heads[-1] + 1) * HD)

    @pl.when(from_even)
    def _():
        fifth_q[...] = even_q[other][:, wanted]
        fifth_d[...] = even_d[other][:, wanted]

    @pl.when(jnp.logical_not(from_even))
    def _():
        fifth_q[...] = odd_q[other][:, wanted]
        fifth_d[...] = odd_d[other][:, wanted]

    row = lax.broadcasted_iota(jnp.int32, se.shape, 0)
    nothing = jnp.where(lax.rem(row, 2) == 0, jnp.float32(BIG), jnp.float32(0.0))
    even = jnp.where(even_ok, se[...], nothing)
    odd = jnp.where(odd_ok, so[...], nothing)
    span = slice(same * rows, (same + 1) * rows)
    across = slice(other * rows, (other + 1) * rows)
    fifth = jnp.where(from_even, even[:, across], odd[:, across])
    for i, head in enumerate(heads):
        cols = slice(head * HD, (head + 1) * HD)
        to = slice(i * HD, (i + 1) * HD)
        a, b = 2 * head, 2 * head + 1
        steps = (
            (even_q[same][:, cols], even_d[same][:, cols], even[a : a + 1, span], even[b : b + 1, span]),
            (odd_q[same][:, cols], odd_d[same][:, cols], odd[a : a + 1, span], odd[b : b + 1, span]),
            (fifth_q[:, to], fifth_d[:, to], fifth[a : a + 1], fifth[b : b + 1]),
        )
        k, v = key_step(scale, kv[0, :, cols], kv[1, :, cols], steps)
        out[0, :, to] = ((k + sums[same, 0, :, cols]) * scale).astype(BF16)
        out[1, :, to] = (v + sums[same, 1, :, cols]).astype(BF16)


def key_pass(own, heads, kv, *operands):
    _, rows, _ = kv.shape
    wide = HD * len(heads)
    return pl.pallas_call(
        functools.partial(key_kernel, HD ** -0.5, own, heads),
        out_shape=jax.ShapeDtypeStruct((2, rows, wide), BF16),
        in_specs=[VM] * (1 + len(operands)),
        out_specs=VM,
        scratch_shapes=[pltpu.VMEM((rows, wide), BF16)] * 2,
        compiler_params=params(30),
        cost_estimate=cost(1e9),
        name="key_pass",
    )(kv, *operands)


def unpack_kernel(q_keep, q_got, kv_keep, *refs):
    got, (dq, dk, dv) = refs[:-3], refs[-3:]
    half = q_keep.shape[1]
    x = lax.rem(lax.axis_index("ctx"), 2)
    mine = pl.multiple_of(x * half, half)
    theirs = pl.multiple_of((1 - x) * half, half)
    dq[:, pl.ds(mine, half)] = q_keep[...]
    dq[:, pl.ds(theirs, half)] = q_got[...]
    for i, out in enumerate((dk, dv)):
        out[:, pl.ds(mine, half)] = kv_keep[i]
        first = 0
        for piece in got:
            width = piece.shape[2]
            out[:, pl.ds(theirs + first, width)] = piece[i]
            first += width


def unpack(q_keep, q_got, kv_keep, *got):
    rows, half = q_keep.shape
    whole = jax.ShapeDtypeStruct((rows, 2 * half), BF16)
    return pl.pallas_call(
        unpack_kernel,
        out_shape=(whole,) * 3,
        in_specs=[VM] * (3 + len(got)),
        out_specs=(VM,) * 3,
        compiler_params=params(16),
        cost_estimate=cost(),
        name="unpack",
    )(q_keep, q_got, kv_keep, *got)


def body(queries, keys, values, out_grad, out_weight):
    length = lax.axis_size("ctx")
    lanes = lax.axis_size("mp")
    blocks = length // 2
    width = out_grad.shape[1]

    def over_mp(array, flip):
        return lax.ppermute(array, "mp", [(i, i ^ flip) for i in range(lanes)])

    def over_x(array):
        return lax.ppermute(array, "ctx", [(i, i ^ 1) for i in range(length)])

    def over_z(array, first):
        pairs = []
        for position in range(length):
            block = position // 2
            other = ((block - first) ^ 1) + first
            for lane in range(lanes):
                source = position * lanes + lane
                if block >= first and other < blocks:
                    target = (2 * other + position % 2) * lanes + lane
                else:
                    target = position * lanes + (lane ^ 1)
                pairs.append((source, target))
        return lax.ppermute(array, ("ctx", "mp"), pairs)

    y = over_mp(out_grad, 2)
    near = over_mp(out_grad, 1)
    keep, send_kv, send_q = pack(queries, keys, values)
    xkv, xq = over_x(send_kv), over_x(send_q)
    e0, o0 = over_z(keep, 0), over_z(keep, 1)
    acc, wy, wf = first_piece(out_grad, near, out_weight)
    e1, o1 = over_z(xkv, 0), over_z(xkv, 1)
    acc = after(acc, xkv, flops=1e8)
    y, acc = lax.optimization_barrier((y, acc))
    far = over_mp(y, 1)
    acc = grad_piece(acc, y, wy, False)
    acc = after(acc, e0, o0, flops=3e9)
    dkeep, dsend = grad_piece(acc, far, wf, True)
    dxr = after(over_x(dsend), flops=6e9)

    late_q, e1, o1 = lax.optimization_barrier((xq, e1, o1))
    mixed = join(late_q, dkeep)
    mixed_e, mixed_o = over_z(mixed, 0), over_z(mixed, 1)
    de1, do1 = over_z(dxr, 0), over_z(dxr, 1)
    dq_keep, stats = query_pass(True, keep, dkeep, keep, xkv, e0, o0, e1, o1)
    dq_send, stats = query_pass(False, xq, dxr, keep, xkv, e1, o1, e0, o0, stats)
    stats, mixed_e, mixed_o = lax.optimization_barrier((stats, mixed_e, mixed_o))
    se, so = over_z(stats, 0), over_z(stats, 1)
    dq_got = over_x(dq_send)
    sums = own_pass(keep, xkv, xq, dkeep, dxr, stats)
    sums = after(sums, de1, do1, flops=3e9)
    heads = dkeep.shape[1] // HD
    theirs = (e0, o0, mixed_e, mixed_o, de1, do1, se, so)
    got = []
    for head in range(heads):
        if head == 1:
            sums, dq_got = lax.optimization_barrier((sums, dq_got))
        got.append(over_x(key_pass(False, (head,), xkv, *theirs, sums)))
    kv_keep = key_pass(True, tuple(range(heads)), keep, *theirs, sums)
    return tuple(unpack(dq_keep, dq_got, kv_keep, *got))


def solution(mesh):
    placed = (P("ctx", "mp"), P("ctx", "mp"), P("ctx", "mp"), P("ctx", "mp"), P("mp", None))
    return jax.shard_map(
        body,
        mesh=mesh,
        in_specs=placed,
        out_specs=(P("ctx", "mp"), P("ctx", "mp"), P("ctx", "mp")),
        check_vma=False,
    )
```

```python
import functools
import math

import jax
import jax.numpy as jnp
from jax import lax
from jax.experimental import pallas as pl
from jax.experimental.pallas import tpu as pltpu
from jax.sharding import PartitionSpec as P

HD = 128
BF16 = jnp.bfloat16
F32 = jnp.float32
BIG = 1e30
ANY = pl.BlockSpec(memory_space=pl.ANY)
VM = pl.BlockSpec(memory_space=pltpu.VMEM)
HBM = pl.BlockSpec(memory_space=pltpu.HBM)


def params(mib=40):
    return pltpu.CompilerParams(vmem_limit_bytes=mib << 20)


def nt(a, b):
    return lax.dot_general(a, b, (((1,), (1,)), ((), ())), preferred_element_type=F32)


def nn(a, b):
    return lax.dot_general(a, b, (((1,), (0,)), ((), ())), preferred_element_type=F32)


def cost(flops=1):
    return pl.CostEstimate(flops=int(flops), bytes_accessed=1, transcendentals=0)


def pack_kernel(q, k, v, keep, send_kv, send_q, sem):
    half = q.shape[1] // 2
    x = lax.rem(lax.axis_index("ctx"), 2)
    mine = pl.ds(pl.multiple_of(x * half, half), half)
    theirs = pl.ds(pl.multiple_of((1 - x) * half, half), half)
    pairs = (
        (k.at[:, theirs], send_kv.at[0]),
        (v.at[:, theirs], send_kv.at[1]),
        (k.at[:, mine], keep.at[0]),
        (v.at[:, mine], keep.at[1]),
        (q.at[:, mine], keep.at[2]),
        (q.at[:, theirs], send_q),
    )
    copies = [pltpu.make_async_copy(a, b, sem.at[i]) for i, (a, b) in enumerate(pairs)]
    for copy in copies:
        copy.start()
    for copy in copies:
        copy.wait()


def pack(q, k, v):
    rows, cols = q.shape
    three, two = (jax.ShapeDtypeStruct((n, rows, cols // 2), BF16) for n in (3, 2))
    one = jax.ShapeDtypeStruct((rows, cols // 2), BF16)
    return pl.pallas_call(
        pack_kernel,
        out_shape=(three, two, one),
        in_specs=[ANY] * 3,
        out_specs=(VM,) * 3,
        scratch_shapes=[pltpu.SemaphoreType.DMA((6,))],
        compiler_params=params(60),
        cost_estimate=cost(),
        name="pack",
    )(q, k, v)


def join_kernel(*refs):
    for i, ref in enumerate(refs[:-1]):
        refs[-1][i] = ref[...]


def join(*pieces):
    return pl.pallas_call(
        join_kernel,
        out_shape=jax.ShapeDtypeStruct((len(pieces), *pieces[0].shape), BF16),
        in_specs=[VM] * len(pieces),
        out_specs=VM,
        compiler_params=params(16),
        cost_estimate=cost(),
        name="join",
    )(*pieces)


def first_kernel(og, near, w, acc, wy, wf, wbuf, sem):
    width = og.shape[1]
    me = lax.axis_index("mp")
    copies = []
    for flip, target in enumerate((wbuf.at[0], wbuf.at[1], wy, wf)):
        first = pl.multiple_of(jnp.bitwise_xor(me, flip) * width, width)
        copies.append(pltpu.make_async_copy(w.at[:, pl.ds(first, width)], target, sem.at[flip]))
    for copy in copies:
        copy.start()
    copies[0].wait()
    acc[...] = nt(og[...], wbuf[0])
    copies[1].wait()
    acc[...] += nt(near[...], wbuf[1])
    copies[2].wait()
    copies[3].wait()


def first_piece(og, near, w):
    rows, width = og.shape
    heads = w.shape[0]
    part = jax.ShapeDtypeStruct((heads, width), BF16)
    return pl.pallas_call(
        first_kernel,
        out_shape=(jax.ShapeDtypeStruct((rows, heads), F32), part, part),
        in_specs=[VM, VM, ANY],
        out_specs=(VM, VM, VM),
        scratch_shapes=[pltpu.VMEM((2, heads, width), BF16), pltpu.SemaphoreType.DMA((4,))],
        compiler_params=params(46),
        cost_estimate=cost(),
        name="head_grad_first",
    )(og, near, w)


def next_kernel(acc, piece, w, out):
    out[...] = acc[...] + nt(piece[...], w[...])


def last_kernel(acc, piece, w, keep, send):
    total = acc[...] + nt(piece[...], w[...])
    half = total.shape[1] // 2
    x = lax.rem(lax.axis_index("ctx"), 2)
    low = total[:, :half].astype(BF16)
    high = total[:, half:].astype(BF16)

    @pl.when(x == 0)
    def _():
        keep[...] = low
        send[...] = high

    @pl.when(x != 0)
    def _():
        keep[...] = high
        send[...] = low


def grad_piece(acc, piece, w, last):
    rows, heads = acc.shape
    half = jax.ShapeDtypeStruct((rows, heads // 2), BF16)
    return pl.pallas_call(
        last_kernel if last else next_kernel,
        out_shape=(half, half) if last else jax.ShapeDtypeStruct((rows, heads), F32),
        in_specs=[VM] * 3,
        out_specs=(VM, VM) if last else VM,
        compiler_params=params(30),
        cost_estimate=cost(),
        name="head_grad",
    )(acc, piece, w)


def after(value, *others, flops):
    return pl.pallas_call(
        lambda *refs: None,
        out_shape=jax.ShapeDtypeStruct(value.shape, value.dtype),
        in_specs=[ANY] * (1 + len(others)),
        out_specs=ANY,
        input_output_aliases={0: 0},
        compiler_params=params(16),
        cost_estimate=cost(flops),
        name="after",
    )(value, *others)


def place():
    position = lax.axis_index("ctx")
    block = position // 2
    low_ok = block > 0
    high_ok = block < lax.axis_size("ctx") // 2 - 1
    odd = lax.rem(block, 2) == 1
    even_ok = jnp.logical_or(jnp.logical_and(odd, low_ok), jnp.logical_and(jnp.logical_not(odd), high_ok))
    odd_ok = jnp.logical_or(jnp.logical_and(odd, high_ok), jnp.logical_and(jnp.logical_not(odd), low_ok))
    turned = lax.rem(position + block, 2) == 1
    return even_ok, odd_ok, turned


def off(ok):
    return jnp.where(ok, 0.0, BIG).astype(F32)


def query_kernel(scale, own, has_marks, *refs):
    refs = list(refs)
    q, d, keep, xr, e, o, e_other, o_other = refs[:8]
    q = q if len(q.shape) == 2 else q.at[2]
    before = refs[8] if has_marks else None
    out, stats, fifth = refs[-3:]
    rows = q.shape[0]
    heads = q.shape[1] // HD
    even_ok, odd_ok, turned = place()
    from_even = turned if own else jnp.logical_not(turned)

    @pl.when(from_even)
    def _():
        fifth[...] = e_other[0:2]

    @pl.when(jnp.logical_not(from_even))
    def _():
        fifth[...] = o_other[0:2]

    c = scale * math.log2(math.e)
    even_off, odd_off = off(even_ok), off(odd_ok)
    lane = lax.broadcasted_iota(jnp.int32, (rows, HD), 1)
    runs = (
        (keep, None),
        (xr, None),
        (e, even_off),
        (o, odd_off),
        (fifth, jnp.where(from_even, even_off, odd_off)),
    )
    mark = jnp.zeros((rows, HD), F32)
    for head in range(heads):
        cols = slice(head * HD, (head + 1) * HD)
        query = q[:, cols]
        grad = d[:, cols]
        scores = [nt(query, ref[0, :, cols]) for ref, _ in runs]
        top = None
        for s, (_, gone) in zip(scores, runs):
            m = jnp.max(s, -1, keepdims=True)
            m = m if gone is None else m - gone
            top = m if top is None else jnp.maximum(top, m)
        top = top * c
        weights = [
            jnp.exp2(s * c - (top if gone is None else top + gone))
            for s, (_, gone) in zip(scores, runs)
        ]
        total = jnp.sum(sum(weights), -1, keepdims=True)
        grads = [nt(grad, ref[1, :, cols]) for ref, _ in runs]
        inverse = 1.0 / total
        delta = jnp.sum(sum(w * g for w, g in zip(weights, grads)), -1, keepdims=True) * inverse
        result = sum(
            nn((w * (g - delta)).astype(BF16), ref[0, :, cols])
            for w, g, (ref, _) in zip(weights, grads, runs)
        )
        out[:, cols] = (result * (inverse * scale)).astype(BF16)
        mark = jnp.where(lane == 2 * head, top + jnp.log2(total), mark)
        mark = jnp.where(lane == 2 * head + 1, delta, mark)
    marks = jnp.transpose(mark)[: stats.shape[0], :]
    if has_marks:
        stats[:, :rows] = marks
        stats[:, rows:] = before[...]
    else:
        stats[...] = marks


def query_pass(own, q, d, keep, xr, e, o, e_other, o_other, before=None):
    rows, cols = d.shape
    operands = [q, d, keep, xr, e, o, e_other, o_other]
    if before is not None:
        operands.append(before)
    return pl.pallas_call(
        functools.partial(query_kernel, HD ** -0.5, own, before is not None),
        out_shape=(
            jax.ShapeDtypeStruct((rows, cols), BF16),
            jax.ShapeDtypeStruct((8, rows if before is None else 2 * rows), F32),
        ),
        in_specs=[VM] * len(operands),
        out_specs=(VM, VM),
        scratch_shapes=[pltpu.VMEM((2, rows, cols), BF16)],
        compiler_params=params(30),
        cost_estimate=cost(6e9 if own else 1),
        name="query_pass",
    )(*operands)


def key_step(scale, key, value, steps):
    c = scale * math.log2(math.e)
    key_sum = None
    value_sum = None
    for query, grad, total, delta in steps:
        weight = jnp.exp2(nt(key, query) * c - total)
        change = weight * (nt(value, grad) - delta)
        v = nn(weight.astype(BF16), grad)
        k = nn(change.astype(BF16), query)
        value_sum = v if value_sum is None else value_sum + v
        key_sum = k if key_sum is None else key_sum + k
    return key_sum, value_sum


def own_kernel(scale, keys, keep, xq, dkeep, dxr, stats, sums):
    rows = keep.shape[1]
    heads = keep.shape[2] // HD
    for head in range(heads):
        cols = slice(head * HD, (head + 1) * HD)
        steps = []
        for i, (q, d) in enumerate(((keep.at[2], dkeep), (xq, dxr))):
            span = slice(i * rows, (i + 1) * rows)
            steps.append((
                q[:, cols],
                d[:, cols],
                stats[2 * head : 2 * head + 1, span],
                stats[2 * head + 1 : 2 * head + 2, span],
            ))
        k, v = key_step(scale, keys[0, :, cols], keys[1, :, cols], steps)
        sums[0, :, cols] = k
        sums[1, :, cols] = v


def own_pass(*operands):
    _, rows, cols = operands[0].shape
    return pl.pallas_call(
        functools.partial(own_kernel, HD ** -0.5),
        out_shape=jax.ShapeDtypeStruct((2, rows, cols), F32),
        in_specs=[VM] * 6,
        out_specs=VM,
        compiler_params=params(30),
        cost_estimate=cost(),
        name="own_pass",
    )(*operands)


def key_kernel(scale, own, heads, kv, e0, o0, late_e, late_o, se, so, sums, out, fifth_q, fifth_d):
    rows = kv.shape[1]
    even_ok, odd_ok, turned = place()
    from_even = turned if own else jnp.logical_not(turned)
    even_q, odd_q = (e0.at[2], late_e.at[0]), (o0.at[2], late_o.at[0])
    even_d, odd_d = (late_e.at[1], late_e.at[2]), (late_o.at[1], late_o.at[2])
    same, other = (0, 1) if own else (1, 0)
    wanted = slice(heads[0] * HD, (heads[-1] + 1) * HD)

    @pl.when(from_even)
    def _():
        fifth_q[...] = even_q[other][:, wanted]
        fifth_d[...] = even_d[other][:, wanted]

    @pl.when(jnp.logical_not(from_even))
    def _():
        fifth_q[...] = odd_q[other][:, wanted]
        fifth_d[...] = odd_d[other][:, wanted]

    row = lax.broadcasted_iota(jnp.int32, se.shape, 0)
    nothing = jnp.where(lax.rem(row, 2) == 0, jnp.float32(BIG), jnp.float32(0.0))
    even = jnp.where(even_ok, se[...], nothing)
    odd = jnp.where(odd_ok, so[...], nothing)
    span = slice(same * rows, (same + 1) * rows)
    across = slice(other * rows, (other + 1) * rows)
    fifth = jnp.where(from_even, even[:, across], odd[:, across])
    for i, head in enumerate(heads):
        cols = slice(head * HD, (head + 1) * HD)
        to = slice(i * HD, (i + 1) * HD)
        a, b = 2 * head, 2 * head + 1
        steps = (
            (even_q[same][:, cols], even_d[same][:, cols], even[a : a + 1, span], even[b : b + 1, span]),
            (odd_q[same][:, cols], odd_d[same][:, cols], odd[a : a + 1, span], odd[b : b + 1, span]),
            (fifth_q[:, to], fifth_d[:, to], fifth[a : a + 1], fifth[b : b + 1]),
        )
        k, v = key_step(scale, kv[0, :, cols], kv[1, :, cols], steps)
        out[0, :, to] = ((k + sums[0, :, cols]) * scale).astype(BF16)
        out[1, :, to] = (v + sums[1, :, cols]).astype(BF16)


def key_pass(own, heads, kv, *operands):
    _, rows, _ = kv.shape
    wide = HD * len(heads)
    return pl.pallas_call(
        functools.partial(key_kernel, HD ** -0.5, own, heads),
        out_shape=jax.ShapeDtypeStruct((2, rows, wide), BF16),
        in_specs=[VM] * (1 + len(operands)),
        out_specs=VM,
        scratch_shapes=[pltpu.VMEM((rows, wide), BF16)] * 2,
        compiler_params=params(30),
        cost_estimate=cost(1e9),
        name="key_pass",
    )(kv, *operands)


def unpack_kernel(q_keep, q_got, kv_keep, *refs):
    got, (dq, dk, dv) = refs[:-3], refs[-3:]
    half = q_keep.shape[1]
    x = lax.rem(lax.axis_index("ctx"), 2)
    mine = pl.multiple_of(x * half, half)
    theirs = pl.multiple_of((1 - x) * half, half)
    dq[:, pl.ds(mine, half)] = q_keep[...]
    dq[:, pl.ds(theirs, half)] = q_got[...]
    for i, out in enumerate((dk, dv)):
        out[:, pl.ds(mine, half)] = kv_keep[i]
        first = 0
        for piece in got:
            width = piece.shape[2]
            out[:, pl.ds(theirs + first, width)] = piece[i]
            first += width


def unpack(q_keep, q_got, kv_keep, *got):
    rows, half = q_keep.shape
    whole = jax.ShapeDtypeStruct((rows, 2 * half), BF16)
    return pl.pallas_call(
        unpack_kernel,
        out_shape=(whole,) * 3,
        in_specs=[VM] * (3 + len(got)),
        out_specs=(VM,) * 3,
        compiler_params=params(16),
        cost_estimate=cost(),
        name="unpack",
    )(q_keep, q_got, kv_keep, *got)


def body(queries, keys, values, out_grad, out_weight):
    length = lax.axis_size("ctx")
    lanes = lax.axis_size("mp")
    blocks = length // 2
    width = out_grad.shape[1]

    def over_mp(array, flip):
        return lax.ppermute(array, "mp", [(i, i ^ flip) for i in range(lanes)])

    def over_x(array):
        return lax.ppermute(array, "ctx", [(i, i ^ 1) for i in range(length)])

    def over_z(array, first):
        pairs = []
        for position in range(length):
            block = position // 2
            other = ((block - first) ^ 1) + first
            for lane in range(lanes):
                source = position * lanes + lane
                if block >= first and other < blocks:
                    target = (2 * other + position % 2) * lanes + lane
                else:
                    target = position * lanes + (lane ^ 1)
                pairs.append((source, target))
        return lax.ppermute(array, ("ctx", "mp"), pairs)

    y = over_mp(out_grad, 2)
    near = over_mp(out_grad, 1)
    keep, send_kv, send_q = pack(queries, keys, values)
    xkv, xq = over_x(send_kv), over_x(send_q)
    e0, o0 = over_z(keep, 0), over_z(keep, 1)
    acc, wy, wf = first_piece(out_grad, near, out_weight)
    e1, o1 = over_z(xkv, 0), over_z(xkv, 1)
    acc = after(acc, xkv, xq, flops=1e8)
    y, acc = lax.optimization_barrier((y, acc))
    far = over_mp(y, 1)
    acc = grad_piece(acc, y, wy, False)
    acc = after(acc, e0, o0, flops=3e9)
    dkeep, dsend = grad_piece(acc, far, wf, True)
    dxr = after(over_x(dsend), flops=6e9)

    xq, e1, o1 = lax.optimization_barrier((xq, e1, o1))
    late = join(xq, dkeep, dxr)
    late_e, late_o = over_z(late, 0), over_z(late, 1)
    dq_send, marks = query_pass(False, xq, dxr, keep, xkv, e1, o1, e0, o0)
    dq_keep, stats = query_pass(True, keep, dkeep, keep, xkv, e0, o0, e1, o1, marks)
    dq_got = after(over_x(dq_send), flops=6e9)
    se, so = over_z(stats, 0), over_z(stats, 1)
    sums = own_pass(xkv, keep, xq, dkeep, dxr, stats)
    sums = after(sums, late_e, late_o, flops=3e9)
    own_sums = own_pass(keep, keep, xq, dkeep, dxr, stats)
    heads = dkeep.shape[1] // HD
    theirs = (e0, o0, late_e, late_o, se, so)
    got = []
    for head in range(heads):
        if head == 1:
            sums, dq_got = lax.optimization_barrier((sums, dq_got))
        got.append(over_x(key_pass(False, (head,), xkv, *theirs, sums)))
    kv_keep = key_pass(True, tuple(range(heads)), keep, *theirs, own_sums)
    return tuple(unpack(dq_keep, dq_got, kv_keep, *got))


def solution(mesh):
    placed = (P("ctx", "mp"), P("ctx", "mp"), P("ctx", "mp"), P("ctx", "mp"), P("mp", None))
    return jax.shard_map(
        body,
        mesh=mesh,
        in_specs=placed,
        out_specs=(P("ctx", "mp"), P("ctx", "mp"), P("ctx", "mp")),
        check_vma=False,
    )
```

```python
import functools
import math

import jax
import jax.numpy as jnp
from jax import lax
from jax.experimental import pallas as pl
from jax.experimental.pallas import tpu as pltpu
from jax.sharding import PartitionSpec as P

HD = 128
BF16 = jnp.bfloat16
F32 = jnp.float32
BIG = 1e30
ANY = pl.BlockSpec(memory_space=pl.ANY)
VM = pl.BlockSpec(memory_space=pltpu.VMEM)
HBM = pl.BlockSpec(memory_space=pltpu.HBM)


def params(mib=40):
    return pltpu.CompilerParams(vmem_limit_bytes=mib << 20)


def nt(a, b):
    return lax.dot_general(a, b, (((1,), (1,)), ((), ())), preferred_element_type=F32)


def nn(a, b):
    return lax.dot_general(a, b, (((1,), (0,)), ((), ())), preferred_element_type=F32)


def cost(flops=1):
    return pl.CostEstimate(flops=int(flops), bytes_accessed=1, transcendentals=0)


def pack_kernel(q, k, v, keep, send_kv, send_q, sem):
    half = q.shape[1] // 2
    x = lax.rem(lax.axis_index("ctx"), 2)
    mine = pl.ds(pl.multiple_of(x * half, half), half)
    theirs = pl.ds(pl.multiple_of((1 - x) * half, half), half)
    pairs = (
        (k.at[:, theirs], send_kv.at[0]),
        (v.at[:, theirs], send_kv.at[1]),
        (k.at[:, mine], keep.at[0]),
        (v.at[:, mine], keep.at[1]),
        (q.at[:, mine], keep.at[2]),
        (q.at[:, theirs], send_q),
    )
    copies = [pltpu.make_async_copy(a, b, sem.at[i]) for i, (a, b) in enumerate(pairs)]
    for copy in copies:
        copy.start()
    for copy in copies:
        copy.wait()


def pack(q, k, v):
    rows, cols = q.shape
    three, two = (jax.ShapeDtypeStruct((n, rows, cols // 2), BF16) for n in (3, 2))
    one = jax.ShapeDtypeStruct((rows, cols // 2), BF16)
    return pl.pallas_call(
        pack_kernel,
        out_shape=(three, two, one),
        in_specs=[ANY] * 3,
        out_specs=(VM,) * 3,
        scratch_shapes=[pltpu.SemaphoreType.DMA((6,))],
        compiler_params=params(60),
        cost_estimate=cost(),
        name="pack",
    )(q, k, v)


def join_kernel(*refs):
    for i, ref in enumerate(refs[:-1]):
        refs[-1][i] = ref[...]


def join(*pieces):
    return pl.pallas_call(
        join_kernel,
        out_shape=jax.ShapeDtypeStruct((len(pieces), *pieces[0].shape), BF16),
        in_specs=[VM] * len(pieces),
        out_specs=VM,
        compiler_params=params(16),
        cost_estimate=cost(),
        name="join",
    )(*pieces)


def first_kernel(og, near, w, acc, wy, wf, wbuf, sem):
    width = og.shape[1]
    me = lax.axis_index("mp")
    copies = []
    for flip, target in enumerate((wbuf.at[0], wbuf.at[1], wy, wf)):
        first = pl.multiple_of(jnp.bitwise_xor(me, flip) * width, width)
        copies.append(pltpu.make_async_copy(w.at[:, pl.ds(first, width)], target, sem.at[flip]))
    for copy in copies:
        copy.start()
    copies[0].wait()
    acc[...] = nt(og[...], wbuf[0])
    copies[1].wait()
    acc[...] += nt(near[...], wbuf[1])
    copies[2].wait()
    copies[3].wait()


def first_piece(og, near, w):
    rows, width = og.shape
    heads = w.shape[0]
    part = jax.ShapeDtypeStruct((heads, width), BF16)
    return pl.pallas_call(
        first_kernel,
        out_shape=(jax.ShapeDtypeStruct((rows, heads), F32), part, part),
        in_specs=[VM, VM, ANY],
        out_specs=(VM, VM, VM),
        scratch_shapes=[pltpu.VMEM((2, heads, width), BF16), pltpu.SemaphoreType.DMA((4,))],
        compiler_params=params(46),
        cost_estimate=cost(),
        name="head_grad_first",
    )(og, near, w)


def next_kernel(acc, piece, w, out):
    out[...] = acc[...] + nt(piece[...], w[...])


def last_kernel(acc, piece, w, keep, send):
    total = acc[...] + nt(piece[...], w[...])
    half = total.shape[1] // 2
    x = lax.rem(lax.axis_index("ctx"), 2)
    low = total[:, :half].astype(BF16)
    high = total[:, half:].astype(BF16)

    @pl.when(x == 0)
    def _():
        keep[...] = low
        send[...] = high

    @pl.when(x != 0)
    def _():
        keep[...] = high
        send[...] = low


def grad_piece(acc, piece, w, last):
    rows, heads = acc.shape
    half = jax.ShapeDtypeStruct((rows, heads // 2), BF16)
    return pl.pallas_call(
        last_kernel if last else next_kernel,
        out_shape=(half, half) if last else jax.ShapeDtypeStruct((rows, heads), F32),
        in_specs=[VM] * 3,
        out_specs=(VM, VM) if last else VM,
        compiler_params=params(30),
        cost_estimate=cost(),
        name="head_grad",
    )(acc, piece, w)


def after(value, *others, flops):
    return pl.pallas_call(
        lambda *refs: None,
        out_shape=jax.ShapeDtypeStruct(value.shape, value.dtype),
        in_specs=[ANY] * (1 + len(others)),
        out_specs=ANY,
        input_output_aliases={0: 0},
        compiler_params=params(16),
        cost_estimate=cost(flops),
        name="after",
    )(value, *others)


def place():
    position = lax.axis_index("ctx")
    block = position // 2
    low_ok = block > 0
    high_ok = block < lax.axis_size("ctx") // 2 - 1
    odd = lax.rem(block, 2) == 1
    even_ok = jnp.logical_or(jnp.logical_and(odd, low_ok), jnp.logical_and(jnp.logical_not(odd), high_ok))
    odd_ok = jnp.logical_or(jnp.logical_and(odd, high_ok), jnp.logical_and(jnp.logical_not(odd), low_ok))
    turned = lax.rem(position + block, 2) == 1
    return even_ok, odd_ok, turned


def off(ok):
    return jnp.where(ok, 0.0, BIG).astype(F32)


def query_kernel(scale, own, has_marks, *refs):
    refs = list(refs)
    q, d, keep, xr, e, o, e_other, o_other = refs[:8]
    q = q if len(q.shape) == 2 else q.at[2]
    before = refs[8] if has_marks else None
    out, stats, fifth = refs[-3:]
    rows = q.shape[0]
    heads = q.shape[1] // HD
    even_ok, odd_ok, turned = place()
    from_even = turned if own else jnp.logical_not(turned)

    @pl.when(from_even)
    def _():
        fifth[...] = e_other[0:2]

    @pl.when(jnp.logical_not(from_even))
    def _():
        fifth[...] = o_other[0:2]

    c = scale * math.log2(math.e)
    even_off, odd_off = off(even_ok), off(odd_ok)
    lane = lax.broadcasted_iota(jnp.int32, (rows, HD), 1)
    runs = (
        (keep, None),
        (xr, None),
        (e, even_off),
        (o, odd_off),
        (fifth, jnp.where(from_even, even_off, odd_off)),
    )
    mark = jnp.zeros((rows, HD), F32)
    for head in range(heads):
        cols = slice(head * HD, (head + 1) * HD)
        query = q[:, cols]
        grad = d[:, cols]
        scores = [nt(query, ref[0, :, cols]) for ref, _ in runs]
        top = None
        for s, (_, gone) in zip(scores, runs):
            m = jnp.max(s, -1, keepdims=True)
            m = m if gone is None else m - gone
            top = m if top is None else jnp.maximum(top, m)
        top = top * c
        weights = [
            jnp.exp2(s * c - (top if gone is None else top + gone))
            for s, (_, gone) in zip(scores, runs)
        ]
        total = jnp.sum(sum(weights), -1, keepdims=True)
        grads = [nt(grad, ref[1, :, cols]) for ref, _ in runs]
        inverse = 1.0 / total
        delta = jnp.sum(sum(w * g for w, g in zip(weights, grads)), -1, keepdims=True) * inverse
        result = sum(
            nn((w * (g - delta)).astype(BF16), ref[0, :, cols])
            for w, g, (ref, _) in zip(weights, grads, runs)
        )
        out[0, :, cols] = (result * (inverse * scale)).astype(BF16)
        mark = jnp.where(lane == 2 * head, top + jnp.log2(total), mark)
        mark = jnp.where(lane == 2 * head + 1, delta, mark)
    marks = jnp.transpose(mark)[: stats.shape[0], :]
    if has_marks:
        stats[:, :rows] = marks
        stats[:, rows:] = before[...]
    else:
        stats[...] = marks


def query_pass(own, q, d, keep, xr, e, o, e_other, o_other, before=None):
    rows, cols = d.shape
    operands = [q, d, keep, xr, e, o, e_other, o_other]
    if before is not None:
        operands.append(before)
    return pl.pallas_call(
        functools.partial(query_kernel, HD ** -0.5, own, before is not None),
        out_shape=(
            jax.ShapeDtypeStruct((1, rows, cols), BF16),
            jax.ShapeDtypeStruct((8, rows if before is None else 2 * rows), F32),
        ),
        in_specs=[VM] * len(operands),
        out_specs=(VM, VM),
        scratch_shapes=[pltpu.VMEM((2, rows, cols), BF16)],
        compiler_params=params(30),
        cost_estimate=cost(6e9 if own else 1),
        name="query_pass",
    )(*operands)


def key_step(scale, key, value, steps):
    c = scale * math.log2(math.e)
    key_sum = None
    value_sum = None
    for query, grad, total, delta in steps:
        weight = jnp.exp2(nt(key, query) * c - total)
        change = weight * (nt(value, grad) - delta)
        v = nn(weight.astype(BF16), grad)
        k = nn(change.astype(BF16), query)
        value_sum = v if value_sum is None else value_sum + v
        key_sum = k if key_sum is None else key_sum + k
    return key_sum, value_sum


def own_kernel(scale, keys, keep, xq, dkeep, dxr, stats, sums):
    rows = keep.shape[1]
    heads = keep.shape[2] // HD
    for head in range(heads):
        cols = slice(head * HD, (head + 1) * HD)
        steps = []
        for i, (q, d) in enumerate(((keep.at[2], dkeep), (xq, dxr))):
            span = slice(i * rows, (i + 1) * rows)
            steps.append((
                q[:, cols],
                d[:, cols],
                stats[2 * head : 2 * head + 1, span],
                stats[2 * head + 1 : 2 * head + 2, span],
            ))
        k, v = key_step(scale, keys[0, :, cols], keys[1, :, cols], steps)
        sums[0, :, cols] = k
        sums[1, :, cols] = v


def own_pass(*operands):
    _, rows, cols = operands[0].shape
    return pl.pallas_call(
        functools.partial(own_kernel, HD ** -0.5),
        out_shape=jax.ShapeDtypeStruct((2, rows, cols), F32),
        in_specs=[VM] * 6,
        out_specs=VM,
        compiler_params=params(30),
        cost_estimate=cost(),
        name="own_pass",
    )(*operands)


def key_kernel(scale, own, heads, kv, e0, o0, late_e, late_o, se, so, sums, out, fifth_q, fifth_d):
    rows = kv.shape[1]
    even_ok, odd_ok, turned = place()
    from_even = turned if own else jnp.logical_not(turned)
    even_q, odd_q = (e0.at[2], late_e.at[0]), (o0.at[2], late_o.at[0])
    even_d, odd_d = (late_e.at[1], late_e.at[2]), (late_o.at[1], late_o.at[2])
    same, other = (0, 1) if own else (1, 0)
    wanted = slice(heads[0] * HD, (heads[-1] + 1) * HD)

    @pl.when(from_even)
    def _():
        fifth_q[...] = even_q[other][:, wanted]
        fifth_d[...] = even_d[other][:, wanted]

    @pl.when(jnp.logical_not(from_even))
    def _():
        fifth_q[...] = odd_q[other][:, wanted]
        fifth_d[...] = odd_d[other][:, wanted]

    row = lax.broadcasted_iota(jnp.int32, se.shape, 0)
    nothing = jnp.where(lax.rem(row, 2) == 0, jnp.float32(BIG), jnp.float32(0.0))
    even = jnp.where(even_ok, se[...], nothing)
    odd = jnp.where(odd_ok, so[...], nothing)
    span = slice(same * rows, (same + 1) * rows)
    across = slice(other * rows, (other + 1) * rows)
    fifth = jnp.where(from_even, even[:, across], odd[:, across])
    for i, head in enumerate(heads):
        cols = slice(head * HD, (head + 1) * HD)
        to = slice(i * HD, (i + 1) * HD)
        a, b = 2 * head, 2 * head + 1
        steps = (
            (even_q[same][:, cols], even_d[same][:, cols], even[a : a + 1, span], even[b : b + 1, span]),
            (odd_q[same][:, cols], odd_d[same][:, cols], odd[a : a + 1, span], odd[b : b + 1, span]),
            (fifth_q[:, to], fifth_d[:, to], fifth[a : a + 1], fifth[b : b + 1]),
        )
        k, v = key_step(scale, kv[0, :, cols], kv[1, :, cols], steps)
        out[0, :, to] = ((k + sums[0, :, cols]) * scale).astype(BF16)
        out[1, :, to] = (v + sums[1, :, cols]).astype(BF16)


def key_pass(own, heads, kv, *operands):
    _, rows, _ = kv.shape
    wide = HD * len(heads)
    return pl.pallas_call(
        functools.partial(key_kernel, HD ** -0.5, own, heads),
        out_shape=jax.ShapeDtypeStruct((2, rows, wide), BF16),
        in_specs=[VM] * (1 + len(operands)),
        out_specs=VM,
        scratch_shapes=[pltpu.VMEM((rows, wide), BF16)] * 2,
        compiler_params=params(30),
        cost_estimate=cost(1e9),
        name="key_pass",
    )(kv, *operands)


def unpack_kernel(n_out, kept, *refs):
    got, outs, sem = refs[: -1 - n_out], refs[-1 - n_out : -1], refs[-1]
    half = kept.shape[2]
    x = lax.rem(lax.axis_index("ctx"), 2)
    mine = pl.multiple_of(x * half, half)
    theirs = pl.multiple_of((1 - x) * half, half)
    copies = []
    for i, out in enumerate(outs):
        pairs = [(kept.at[i], out.at[:, pl.ds(mine, half)])]
        first = 0
        for piece in got:
            width = piece.shape[2]
            pairs.append((piece.at[i], out.at[:, pl.ds(theirs + first, width)]))
            first += width
        for a, b in pairs:
            copies.append(pltpu.make_async_copy(a, b, sem.at[len(copies)]))
    for copy in copies:
        copy.start()
    for copy in copies:
        copy.wait()


def unpack(kept, *got):
    n, rows, half = kept.shape
    return pl.pallas_call(
        functools.partial(unpack_kernel, n),
        out_shape=(jax.ShapeDtypeStruct((rows, 2 * half), BF16),) * n,
        in_specs=[VM] * (1 + len(got)),
        out_specs=(ANY,) * n,
        scratch_shapes=[pltpu.SemaphoreType.DMA((n * (1 + len(got)),))],
        compiler_params=params(16),
        cost_estimate=cost(),
        name="unpack",
    )(kept, *got)


def body(queries, keys, values, out_grad, out_weight):
    length = lax.axis_size("ctx")
    lanes = lax.axis_size("mp")
    blocks = length // 2
    width = out_grad.shape[1]

    def over_mp(array, flip):
        return lax.ppermute(array, "mp", [(i, i ^ flip) for i in range(lanes)])

    def over_x(array):
        return lax.ppermute(array, "ctx", [(i, i ^ 1) for i in range(length)])

    def over_z(array, first):
        pairs = []
        for position in range(length):
            block = position // 2
            other = ((block - first) ^ 1) + first
            for lane in range(lanes):
                source = position * lanes + lane
                if block >= first and other < blocks:
                    target = (2 * other + position % 2) * lanes + lane
                else:
                    target = position * lanes + (lane ^ 1)
                pairs.append((source, target))
        return lax.ppermute(array, ("ctx", "mp"), pairs)

    y = over_mp(out_grad, 2)
    near = over_mp(out_grad, 1)
    keep, send_kv, send_q = pack(queries, keys, values)
    xkv, xq = over_x(send_kv), over_x(send_q)
    e0, o0 = over_z(keep, 0), over_z(keep, 1)
    acc, wy, wf = first_piece(out_grad, near, out_weight)
    e1, o1 = over_z(xkv, 0), over_z(xkv, 1)
    acc = after(acc, xkv, xq, flops=1e8)
    y, acc = lax.optimization_barrier((y, acc))
    far = over_mp(y, 1)
    acc = grad_piece(acc, y, wy, False)
    acc = after(acc, e0, o0, flops=3e9)
    dkeep, dsend = grad_piece(acc, far, wf, True)
    dxr = after(over_x(dsend), flops=6e9)

    xq, e1, o1 = lax.optimization_barrier((xq, e1, o1))
    late = join(xq, dkeep, dxr)
    late_e, late_o = over_z(late, 0), over_z(late, 1)
    dq_send, marks = query_pass(False, xq, dxr, keep, xkv, e1, o1, e0, o0)
    dq_keep, stats = query_pass(True, keep, dkeep, keep, xkv, e0, o0, e1, o1, marks)
    dq_got = after(over_x(dq_send), flops=6e9)
    se, so = over_z(stats, 0), over_z(stats, 1)
    sums = own_pass(xkv, keep, xq, dkeep, dxr, stats)
    sums = after(sums, late_e, late_o, flops=3e9)
    own_sums = own_pass(keep, keep, xq, dkeep, dxr, stats)
    heads = dkeep.shape[1] // HD
    theirs = (e0, o0, late_e, late_o, se, so)
    got = []
    for head in range(heads):
        if head == 1:
            dq, = unpack(dq_keep, dq_got)
            sums, dq = lax.optimization_barrier((sums, dq))
        got.append(over_x(key_pass(False, (head,), xkv, *theirs, sums)))
    kv_keep = key_pass(True, tuple(range(heads)), keep, *theirs, own_sums)
    return (dq, *unpack(kv_keep, *got))


def solution(mesh):
    placed = (P("ctx", "mp"), P("ctx", "mp"), P("ctx", "mp"), P("ctx", "mp"), P("mp", None))
    return jax.shard_map(
        body,
        mesh=mesh,
        in_specs=placed,
        out_specs=(P("ctx", "mp"), P("ctx", "mp"), P("ctx", "mp")),
        check_vma=False,
    )
```

```python
import functools
import math

import jax
import jax.numpy as jnp
from jax import lax
from jax.experimental import pallas as pl
from jax.experimental.pallas import tpu as pltpu
from jax.sharding import PartitionSpec as P

HD = 128
BF16 = jnp.bfloat16
F32 = jnp.float32
BIG = 1e30
ANY = pl.BlockSpec(memory_space=pl.ANY)
VM = pl.BlockSpec(memory_space=pltpu.VMEM)
HBM = pl.BlockSpec(memory_space=pltpu.HBM)


def params(mib=40):
    return pltpu.CompilerParams(vmem_limit_bytes=mib << 20)


def nt(a, b):
    return lax.dot_general(a, b, (((1,), (1,)), ((), ())), preferred_element_type=F32)


def nn(a, b):
    return lax.dot_general(a, b, (((1,), (0,)), ((), ())), preferred_element_type=F32)


def cost(flops=1):
    return pl.CostEstimate(flops=int(flops), bytes_accessed=1, transcendentals=0)


def pack_kernel(q, k, v, keep, send_kv, send_q, sem):
    half = q.shape[1] // 2
    x = lax.rem(lax.axis_index("ctx"), 2)
    mine = pl.ds(pl.multiple_of(x * half, half), half)
    theirs = pl.ds(pl.multiple_of((1 - x) * half, half), half)
    pairs = (
        (k.at[:, theirs], send_kv.at[0]),
        (v.at[:, theirs], send_kv.at[1]),
        (k.at[:, mine], keep.at[0]),
        (v.at[:, mine], keep.at[1]),
        (q.at[:, mine], keep.at[2]),
        (q.at[:, theirs], send_q),
    )
    copies = [pltpu.make_async_copy(a, b, sem.at[i]) for i, (a, b) in enumerate(pairs)]
    for copy in copies:
        copy.start()
    for copy in copies:
        copy.wait()


def pack(q, k, v):
    rows, cols = q.shape
    three, two = (jax.ShapeDtypeStruct((n, rows, cols // 2), BF16) for n in (3, 2))
    one = jax.ShapeDtypeStruct((rows, cols // 2), BF16)
    return pl.pallas_call(
        pack_kernel,
        out_shape=(three, two, one),
        in_specs=[ANY] * 3,
        out_specs=(VM,) * 3,
        scratch_shapes=[pltpu.SemaphoreType.DMA((6,))],
        compiler_params=params(60),
        cost_estimate=cost(),
        name="pack",
    )(q, k, v)


def join_kernel(*refs):
    for i, ref in enumerate(refs[:-1]):
        refs[-1][i] = ref[...]


def join(*pieces):
    return pl.pallas_call(
        join_kernel,
        out_shape=jax.ShapeDtypeStruct((len(pieces), *pieces[0].shape), BF16),
        in_specs=[VM] * len(pieces),
        out_specs=VM,
        compiler_params=params(16),
        cost_estimate=cost(),
        name="join",
    )(*pieces)


def first_kernel(og, near, w, acc, wy, wf, wbuf, sem):
    width = og.shape[1]
    me = lax.axis_index("mp")
    copies = []
    for flip, target in enumerate((wbuf.at[0], wbuf.at[1], wy, wf)):
        first = pl.multiple_of(jnp.bitwise_xor(me, flip) * width, width)
        copies.append(pltpu.make_async_copy(w.at[:, pl.ds(first, width)], target, sem.at[flip]))
    for copy in copies:
        copy.start()
    copies[0].wait()
    acc[...] = nt(og[...], wbuf[0])
    copies[1].wait()
    acc[...] += nt(near[...], wbuf[1])
    copies[2].wait()
    copies[3].wait()


def first_piece(og, near, w):
    rows, width = og.shape
    heads = w.shape[0]
    part = jax.ShapeDtypeStruct((heads, width), BF16)
    return pl.pallas_call(
        first_kernel,
        out_shape=(jax.ShapeDtypeStruct((rows, heads), F32), part, part),
        in_specs=[VM, VM, ANY],
        out_specs=(VM, VM, VM),
        scratch_shapes=[pltpu.VMEM((2, heads, width), BF16), pltpu.SemaphoreType.DMA((4,))],
        compiler_params=params(46),
        cost_estimate=cost(),
        name="head_grad_first",
    )(og, near, w)


def next_kernel(acc, piece, w, out):
    out[...] = acc[...] + nt(piece[...], w[...])


def last_kernel(acc, piece, w, keep, send):
    total = acc[...] + nt(piece[...], w[...])
    half = total.shape[1] // 2
    x = lax.rem(lax.axis_index("ctx"), 2)
    low = total[:, :half].astype(BF16)
    high = total[:, half:].astype(BF16)

    @pl.when(x == 0)
    def _():
        keep[...] = low
        send[...] = high

    @pl.when(x != 0)
    def _():
        keep[...] = high
        send[...] = low


def grad_piece(acc, piece, w, last):
    rows, heads = acc.shape
    half = jax.ShapeDtypeStruct((rows, heads // 2), BF16)
    return pl.pallas_call(
        last_kernel if last else next_kernel,
        out_shape=(half, half) if last else jax.ShapeDtypeStruct((rows, heads), F32),
        in_specs=[VM] * 3,
        out_specs=(VM, VM) if last else VM,
        compiler_params=params(30),
        cost_estimate=cost(),
        name="head_grad",
    )(acc, piece, w)


def after(value, *others, flops):
    return pl.pallas_call(
        lambda *refs: None,
        out_shape=jax.ShapeDtypeStruct(value.shape, value.dtype),
        in_specs=[ANY] * (1 + len(others)),
        out_specs=ANY,
        input_output_aliases={0: 0},
        compiler_params=params(16),
        cost_estimate=cost(flops),
        name="after",
    )(value, *others)


def place():
    position = lax.axis_index("ctx")
    block = position // 2
    low_ok = block > 0
    high_ok = block < lax.axis_size("ctx") // 2 - 1
    odd = lax.rem(block, 2) == 1
    even_ok = jnp.logical_or(jnp.logical_and(odd, low_ok), jnp.logical_and(jnp.logical_not(odd), high_ok))
    odd_ok = jnp.logical_or(jnp.logical_and(odd, high_ok), jnp.logical_and(jnp.logical_not(odd), low_ok))
    turned = lax.rem(position + block, 2) == 1
    return even_ok, odd_ok, turned


def off(ok):
    return jnp.where(ok, 0.0, BIG).astype(F32)


def query_kernel(scale, own, has_marks, *refs):
    refs = list(refs)
    q, d, keep, xr, e, o, e_other, o_other = refs[:8]
    q = q if len(q.shape) == 2 else q.at[2]
    before = refs[8] if has_marks else None
    out, stats, fifth = refs[-3:]
    rows = q.shape[0]
    heads = q.shape[1] // HD
    even_ok, odd_ok, turned = place()
    from_even = turned if own else jnp.logical_not(turned)

    @pl.when(from_even)
    def _():
        fifth[...] = e_other[0:2]

    @pl.when(jnp.logical_not(from_even))
    def _():
        fifth[...] = o_other[0:2]

    c = scale * math.log2(math.e)
    even_off, odd_off = off(even_ok), off(odd_ok)
    lane = lax.broadcasted_iota(jnp.int32, (rows, HD), 1)
    runs = (
        (keep, None),
        (xr, None),
        (e, even_off),
        (o, odd_off),
        (fifth, jnp.where(from_even, even_off, odd_off)),
    )
    mark = jnp.zeros((rows, HD), F32)
    for head in range(heads):
        cols = slice(head * HD, (head + 1) * HD)
        query = q[:, cols]
        grad = d[:, cols]
        scores = [nt(query, ref[0, :, cols]) for ref, _ in runs]
        top = None
        for s, (_, gone) in zip(scores, runs):
            m = jnp.max(s, -1, keepdims=True)
            m = m if gone is None else m - gone
            top = m if top is None else jnp.maximum(top, m)
        top = top * c
        weights = [
            jnp.exp2(s * c - (top if gone is None else top + gone))
            for s, (_, gone) in zip(scores, runs)
        ]
        total = jnp.sum(sum(weights), -1, keepdims=True)
        grads = [nt(grad, ref[1, :, cols]) for ref, _ in runs]
        inverse = 1.0 / total
        delta = jnp.sum(sum(w * g for w, g in zip(weights, grads)), -1, keepdims=True) * inverse
        result = sum(
            nn((w * (g - delta)).astype(BF16), ref[0, :, cols])
            for w, g, (ref, _) in zip(weights, grads, runs)
        )
        out[0, :, cols] = (result * (inverse * scale)).astype(BF16)
        mark = jnp.where(lane == 2 * head, top + jnp.log2(total), mark)
        mark = jnp.where(lane == 2 * head + 1, delta, mark)
    marks = jnp.transpose(mark)[: stats.shape[0], :]
    if has_marks:
        stats[:, :rows] = marks
        stats[:, rows:] = before[...]
    else:
        stats[...] = marks


def query_pass(own, q, d, keep, xr, e, o, e_other, o_other, before=None):
    rows, cols = d.shape
    operands = [q, d, keep, xr, e, o, e_other, o_other]
    if before is not None:
        operands.append(before)
    return pl.pallas_call(
        functools.partial(query_kernel, HD ** -0.5, own, before is not None),
        out_shape=(
            jax.ShapeDtypeStruct((1, rows, cols), BF16),
            jax.ShapeDtypeStruct((8, rows if before is None else 2 * rows), F32),
        ),
        in_specs=[VM] * len(operands),
        out_specs=(VM, VM),
        scratch_shapes=[pltpu.VMEM((2, rows, cols), BF16)],
        compiler_params=params(30),
        cost_estimate=cost(6e9 if own else 1),
        name="query_pass",
    )(*operands)


def key_step(scale, key, value, steps):
    c = scale * math.log2(math.e)
    key_sum = None
    value_sum = None
    for query, grad, total, delta in steps:
        weight = jnp.exp2(nt(key, query) * c - total)
        change = weight * (nt(value, grad) - delta)
        v = nn(weight.astype(BF16), grad)
        k = nn(change.astype(BF16), query)
        value_sum = v if value_sum is None else value_sum + v
        key_sum = k if key_sum is None else key_sum + k
    return key_sum, value_sum


def own_kernel(scale, keys, keep, xq, dkeep, dxr, stats, sums):
    rows = keep.shape[1]
    heads = keep.shape[2] // HD
    for head in range(heads):
        cols = slice(head * HD, (head + 1) * HD)
        steps = []
        for i, (q, d) in enumerate(((keep.at[2], dkeep), (xq, dxr))):
            span = slice(i * rows, (i + 1) * rows)
            steps.append((
                q[:, cols],
                d[:, cols],
                stats[2 * head : 2 * head + 1, span],
                stats[2 * head + 1 : 2 * head + 2, span],
            ))
        k, v = key_step(scale, keys[0, :, cols], keys[1, :, cols], steps)
        sums[0, :, cols] = k
        sums[1, :, cols] = v


def own_pass(*operands):
    _, rows, cols = operands[0].shape
    return pl.pallas_call(
        functools.partial(own_kernel, HD ** -0.5),
        out_shape=jax.ShapeDtypeStruct((2, rows, cols), F32),
        in_specs=[VM] * 6,
        out_specs=VM,
        compiler_params=params(30),
        cost_estimate=cost(),
        name="own_pass",
    )(*operands)


def key_kernel(scale, own, heads, kv, e0, o0, late_e, late_o, so, se, sums, out, fifth_q, fifth_d):
    rows = kv.shape[1]
    even_ok, odd_ok, turned = place()
    from_even = turned if own else jnp.logical_not(turned)
    even_q, odd_q = (e0.at[2], late_e.at[0]), (o0.at[2], late_o.at[0])
    even_d, odd_d = (late_e.at[1], late_e.at[2]), (late_o.at[1], late_o.at[2])
    same, other = (0, 1) if own else (1, 0)
    wanted = slice(heads[0] * HD, (heads[-1] + 1) * HD)

    @pl.when(from_even)
    def _():
        fifth_q[...] = even_q[other][:, wanted]
        fifth_d[...] = even_d[other][:, wanted]

    @pl.when(jnp.logical_not(from_even))
    def _():
        fifth_q[...] = odd_q[other][:, wanted]
        fifth_d[...] = odd_d[other][:, wanted]

    row = lax.broadcasted_iota(jnp.int32, se.shape, 0)
    nothing = jnp.where(lax.rem(row, 2) == 0, jnp.float32(BIG), jnp.float32(0.0))
    even = jnp.where(even_ok, se[...], nothing)
    odd = jnp.where(odd_ok, so[...], nothing)
    span = slice(same * rows, (same + 1) * rows)
    across = slice(other * rows, (other + 1) * rows)
    fifth = jnp.where(from_even, even[:, across], odd[:, across])
    for i, head in enumerate(heads):
        cols = slice(head * HD, (head + 1) * HD)
        to = slice(i * HD, (i + 1) * HD)
        a, b = 2 * head, 2 * head + 1
        steps = (
            (even_q[same][:, cols], even_d[same][:, cols], even[a : a + 1, span], even[b : b + 1, span]),
            (odd_q[same][:, cols], odd_d[same][:, cols], odd[a : a + 1, span], odd[b : b + 1, span]),
            (fifth_q[:, to], fifth_d[:, to], fifth[a : a + 1], fifth[b : b + 1]),
        )
        k, v = key_step(scale, kv[0, :, cols], kv[1, :, cols], steps)
        out[0, :, to] = ((k + sums[0, :, cols]) * scale).astype(BF16)
        out[1, :, to] = (v + sums[1, :, cols]).astype(BF16)


def key_pass(own, heads, kv, *operands):
    _, rows, _ = kv.shape
    wide = HD * len(heads)
    return pl.pallas_call(
        functools.partial(key_kernel, HD ** -0.5, own, heads),
        out_shape=jax.ShapeDtypeStruct((2, rows, wide), BF16),
        in_specs=[VM] * (1 + len(operands)),
        out_specs=VM,
        scratch_shapes=[pltpu.VMEM((rows, wide), BF16)] * 2,
        compiler_params=params(30),
        cost_estimate=cost(1e9),
        name="key_pass",
    )(kv, *operands)


def unpack_kernel(n_out, kept, *refs):
    got, outs, sem = refs[: -1 - n_out], refs[-1 - n_out : -1], refs[-1]
    half = kept.shape[2]
    x = lax.rem(lax.axis_index("ctx"), 2)
    mine = pl.multiple_of(x * half, half)
    theirs = pl.multiple_of((1 - x) * half, half)
    copies = []
    for i, out in enumerate(outs):
        pairs = [(kept.at[i], out.at[:, pl.ds(mine, half)])]
        first = 0
        for piece in got:
            width = piece.shape[2]
            pairs.append((piece.at[i], out.at[:, pl.ds(theirs + first, width)]))
            first += width
        for a, b in pairs:
            copies.append(pltpu.make_async_copy(a, b, sem.at[len(copies)]))
    for copy in copies:
        copy.start()
    for copy in copies:
        copy.wait()


def unpack(kept, *got):
    n, rows, half = kept.shape
    return pl.pallas_call(
        functools.partial(unpack_kernel, n),
        out_shape=(jax.ShapeDtypeStruct((rows, 2 * half), BF16),) * n,
        in_specs=[VM] * (1 + len(got)),
        out_specs=(ANY,) * n,
        scratch_shapes=[pltpu.SemaphoreType.DMA((n * (1 + len(got)),))],
        compiler_params=params(16),
        cost_estimate=cost(),
        name="unpack",
    )(kept, *got)


def body(queries, keys, values, out_grad, out_weight):
    length = lax.axis_size("ctx")
    lanes = lax.axis_size("mp")
    blocks = length // 2
    width = out_grad.shape[1]

    def over_mp(array, flip):
        return lax.ppermute(array, "mp", [(i, i ^ flip) for i in range(lanes)])

    def over_x(array):
        return lax.ppermute(array, "ctx", [(i, i ^ 1) for i in range(length)])

    def over_z(array, first):
        pairs = []
        for position in range(length):
            block = position // 2
            other = ((block - first) ^ 1) + first
            for lane in range(lanes):
                source = position * lanes + lane
                if block >= first and other < blocks:
                    target = (2 * other + position % 2) * lanes + lane
                else:
                    target = position * lanes + (lane ^ 1)
                pairs.append((source, target))
        return lax.ppermute(array, ("ctx", "mp"), pairs)

    y = over_mp(out_grad, 2)
    near = over_mp(out_grad, 1)
    keep, send_kv, send_q = pack(queries, keys, values)
    xkv, xq = over_x(send_kv), over_x(send_q)
    o0, e0 = over_z(keep, 1), over_z(keep, 0)
    acc, wy, wf = first_piece(out_grad, near, out_weight)
    o1, e1 = over_z(xkv, 1), over_z(xkv, 0)
    acc = after(acc, xkv, xq, flops=1e8)
    y, acc = lax.optimization_barrier((y, acc))
    far = over_mp(y, 1)
    acc = grad_piece(acc, y, wy, False)
    acc = after(acc, o0, e0, flops=3e9)
    dkeep, dsend = grad_piece(acc, far, wf, True)
    dxr = after(over_x(dsend), flops=6e9)

    xq, o1, e1 = lax.optimization_barrier((xq, o1, e1))
    late = join(xq, dkeep, dxr)
    late_o, late_e = over_z(late, 1), over_z(late, 0)
    dq_send, marks = query_pass(False, xq, dxr, keep, xkv, e1, o1, e0, o0)
    dq_keep, stats = query_pass(True, keep, dkeep, keep, xkv, e0, o0, e1, o1, marks)
    dq_got = after(over_x(dq_send), flops=1)
    so, se = over_z(stats, 1), over_z(stats, 0)
    sums = own_pass(xkv, keep, xq, dkeep, dxr, stats)
    sums = after(sums, late_o, late_e, flops=3e9)
    own_sums = own_pass(keep, keep, xq, dkeep, dxr, stats)
    heads = dkeep.shape[1] // HD
    theirs = (e0, o0, late_e, late_o, so, se)
    got = []
    for head in range(heads):
        if head == 1:
            dq, = unpack(dq_keep, dq_got)
            sums, dq = lax.optimization_barrier((sums, dq))
        got.append(over_x(key_pass(False, (head,), xkv, *theirs, sums)))
    kv_keep = key_pass(True, tuple(range(heads)), keep, *theirs, own_sums)
    return (dq, *unpack(kv_keep, *got))


def solution(mesh):
    placed = (P("ctx", "mp"), P("ctx", "mp"), P("ctx", "mp"), P("ctx", "mp"), P("mp", None))
    return jax.shard_map(
        body,
        mesh=mesh,
        in_specs=placed,
        out_specs=(P("ctx", "mp"), P("ctx", "mp"), P("ctx", "mp")),
        check_vma=False,
    )
```

```python
import functools
import math

import jax
import jax.numpy as jnp
from jax import lax
from jax.experimental import pallas as pl
from jax.experimental.pallas import tpu as pltpu
from jax.sharding import PartitionSpec as P

HD = 128
BF16 = jnp.bfloat16
F32 = jnp.float32
BIG = 1e30
ANY = pl.BlockSpec(memory_space=pl.ANY)
VM = pl.BlockSpec(memory_space=pltpu.VMEM)
HBM = pl.BlockSpec(memory_space=pltpu.HBM)


def params(mib=40):
    return pltpu.CompilerParams(vmem_limit_bytes=mib << 20)


def nt(a, b):
    return lax.dot_general(a, b, (((1,), (1,)), ((), ())), preferred_element_type=F32)


def nn(a, b):
    return lax.dot_general(a, b, (((1,), (0,)), ((), ())), preferred_element_type=F32)


def cost(flops=1):
    return pl.CostEstimate(flops=int(flops), bytes_accessed=1, transcendentals=0)


def pack_kernel(q, k, v, keep, send_kv, send_q, sem):
    half = q.shape[1] // 2
    x = lax.rem(lax.axis_index("ctx"), 2)
    mine = pl.ds(pl.multiple_of(x * half, half), half)
    theirs = pl.ds(pl.multiple_of((1 - x) * half, half), half)
    pairs = (
        (k.at[:, theirs], send_kv.at[0]),
        (v.at[:, theirs], send_kv.at[1]),
        (k.at[:, mine], keep.at[0]),
        (v.at[:, mine], keep.at[1]),
        (q.at[:, mine], keep.at[2]),
        (q.at[:, theirs], send_q),
    )
    copies = [pltpu.make_async_copy(a, b, sem.at[i]) for i, (a, b) in enumerate(pairs)]
    for copy in copies:
        copy.start()
    for copy in copies:
        copy.wait()


def pack(q, k, v):
    rows, cols = q.shape
    three, two = (jax.ShapeDtypeStruct((n, rows, cols // 2), BF16) for n in (3, 2))
    one = jax.ShapeDtypeStruct((rows, cols // 2), BF16)
    return pl.pallas_call(
        pack_kernel,
        out_shape=(three, two, one),
        in_specs=[ANY] * 3,
        out_specs=(VM,) * 3,
        scratch_shapes=[pltpu.SemaphoreType.DMA((6,))],
        compiler_params=params(60),
        cost_estimate=cost(),
        name="pack",
    )(q, k, v)


def join_kernel(pieces, *refs):
    first = 0
    for out in refs[pieces:]:
        width = out.shape[2]
        for i, ref in enumerate(refs[:pieces]):
            out[i] = ref[:, first : first + width]
        first += width


def join(widths, *pieces):
    rows = pieces[0].shape[0]
    return pl.pallas_call(
        functools.partial(join_kernel, len(pieces)),
        out_shape=tuple(jax.ShapeDtypeStruct((len(pieces), rows, w), BF16) for w in widths),
        in_specs=[VM] * len(pieces),
        out_specs=(VM,) * len(widths),
        compiler_params=params(16),
        cost_estimate=cost(),
        name="join",
    )(*pieces)


def first_kernel(og, near, w, acc, wy, wf, wbuf, sem):
    width = og.shape[1]
    me = lax.axis_index("mp")
    copies = []
    for flip, target in enumerate((wbuf.at[0], wbuf.at[1], wy, wf)):
        first = pl.multiple_of(jnp.bitwise_xor(me, flip) * width, width)
        copies.append(pltpu.make_async_copy(w.at[:, pl.ds(first, width)], target, sem.at[flip]))
    for copy in copies:
        copy.start()
    copies[0].wait()
    acc[...] = nt(og[...], wbuf[0])
    copies[1].wait()
    acc[...] += nt(near[...], wbuf[1])
    copies[2].wait()
    copies[3].wait()


def first_piece(og, near, w):
    rows, width = og.shape
    heads = w.shape[0]
    part = jax.ShapeDtypeStruct((heads, width), BF16)
    return pl.pallas_call(
        first_kernel,
        out_shape=(jax.ShapeDtypeStruct((rows, heads), F32), part, part),
        in_specs=[VM, VM, ANY],
        out_specs=(VM, VM, VM),
        scratch_shapes=[pltpu.VMEM((2, heads, width), BF16), pltpu.SemaphoreType.DMA((4,))],
        compiler_params=params(46),
        cost_estimate=cost(),
        name="head_grad_first",
    )(og, near, w)


def next_kernel(acc, piece, w, out):
    out[...] = acc[...] + nt(piece[...], w[...])


def last_kernel(acc, piece, w, keep, send):
    total = acc[...] + nt(piece[...], w[...])
    half = total.shape[1] // 2
    x = lax.rem(lax.axis_index("ctx"), 2)
    low = total[:, :half].astype(BF16)
    high = total[:, half:].astype(BF16)

    @pl.when(x == 0)
    def _():
        keep[...] = low
        send[...] = high

    @pl.when(x != 0)
    def _():
        keep[...] = high
        send[...] = low


def grad_piece(acc, piece, w, last):
    rows, heads = acc.shape
    half = jax.ShapeDtypeStruct((rows, heads // 2), BF16)
    return pl.pallas_call(
        last_kernel if last else next_kernel,
        out_shape=(half, half) if last else jax.ShapeDtypeStruct((rows, heads), F32),
        in_specs=[VM] * 3,
        out_specs=(VM, VM) if last else VM,
        compiler_params=params(30),
        cost_estimate=cost(),
        name="head_grad",
    )(acc, piece, w)


def after(value, *others, flops):
    return pl.pallas_call(
        lambda *refs: None,
        out_shape=jax.ShapeDtypeStruct(value.shape, value.dtype),
        in_specs=[ANY] * (1 + len(others)),
        out_specs=ANY,
        input_output_aliases={0: 0},
        compiler_params=params(16),
        cost_estimate=cost(flops),
        name="after",
    )(value, *others)


def place():
    position = lax.axis_index("ctx")
    block = position // 2
    low_ok = block > 0
    high_ok = block < lax.axis_size("ctx") // 2 - 1
    odd = lax.rem(block, 2) == 1
    even_ok = jnp.logical_or(jnp.logical_and(odd, low_ok), jnp.logical_and(jnp.logical_not(odd), high_ok))
    odd_ok = jnp.logical_or(jnp.logical_and(odd, high_ok), jnp.logical_and(jnp.logical_not(odd), low_ok))
    turned = lax.rem(position + block, 2) == 1
    return even_ok, odd_ok, turned


def off(ok):
    return jnp.where(ok, 0.0, BIG).astype(F32)


def query_kernel(scale, own, has_marks, *refs):
    refs = list(refs)
    q, d, keep, xr, e, o, e_other, o_other = refs[:8]
    q = q if len(q.shape) == 2 else q.at[2]
    before = refs[8] if has_marks else None
    out, stats, fifth = refs[-3:]
    rows = q.shape[0]
    heads = q.shape[1] // HD
    even_ok, odd_ok, turned = place()
    from_even = turned if own else jnp.logical_not(turned)

    @pl.when(from_even)
    def _():
        fifth[...] = e_other[0:2]

    @pl.when(jnp.logical_not(from_even))
    def _():
        fifth[...] = o_other[0:2]

    c = scale * math.log2(math.e)
    even_off, odd_off = off(even_ok), off(odd_ok)
    lane = lax.broadcasted_iota(jnp.int32, (rows, HD), 1)
    runs = (
        (keep, None),
        (xr, None),
        (e, even_off),
        (o, odd_off),
        (fifth, jnp.where(from_even, even_off, odd_off)),
    )
    mark = jnp.zeros((rows, HD), F32)
    for head in range(heads):
        cols = slice(head * HD, (head + 1) * HD)
        query = q[:, cols]
        grad = d[:, cols]
        scores = [nt(query, ref[0, :, cols]) for ref, _ in runs]
        top = None
        for s, (_, gone) in zip(scores, runs):
            m = jnp.max(s, -1, keepdims=True)
            m = m if gone is None else m - gone
            top = m if top is None else jnp.maximum(top, m)
        top = top * c
        weights = [
            jnp.exp2(s * c - (top if gone is None else top + gone))
            for s, (_, gone) in zip(scores, runs)
        ]
        total = jnp.sum(sum(weights), -1, keepdims=True)
        grads = [nt(grad, ref[1, :, cols]) for ref, _ in runs]
        inverse = 1.0 / total
        delta = jnp.sum(sum(w * g for w, g in zip(weights, grads)), -1, keepdims=True) * inverse
        result = sum(
            nn((w * (g - delta)).astype(BF16), ref[0, :, cols])
            for w, g, (ref, _) in zip(weights, grads, runs)
        )
        out[0, :, cols] = (result * (inverse * scale)).astype(BF16)
        mark = jnp.where(lane == 2 * head, top + jnp.log2(total), mark)
        mark = jnp.where(lane == 2 * head + 1, delta, mark)
    marks = jnp.transpose(mark)[: stats.shape[0], :]
    if has_marks:
        stats[:, :rows] = marks
        stats[:, rows:] = before[...]
    else:
        stats[...] = marks


def query_pass(own, q, d, keep, xr, e, o, e_other, o_other, before=None):
    rows, cols = d.shape
    operands = [q, d, keep, xr, e, o, e_other, o_other]
    if before is not None:
        operands.append(before)
    return pl.pallas_call(
        functools.partial(query_kernel, HD ** -0.5, own, before is not None),
        out_shape=(
            jax.ShapeDtypeStruct((1, rows, cols), BF16),
            jax.ShapeDtypeStruct((8, rows if before is None else 2 * rows), F32),
        ),
        in_specs=[VM] * len(operands),
        out_specs=(VM, VM),
        scratch_shapes=[pltpu.VMEM((2, rows, cols), BF16)],
        compiler_params=params(30),
        cost_estimate=cost(1e9 if own else 6e9),
        name="query_pass",
    )(*operands)


def key_step(scale, key, value, steps):
    c = scale * math.log2(math.e)
    key_sum = None
    value_sum = None
    for query, grad, total, delta in steps:
        weight = jnp.exp2(nt(key, query) * c - total)
        change = weight * (nt(value, grad) - delta)
        v = nn(weight.astype(BF16), grad)
        k = nn(change.astype(BF16), query)
        value_sum = v if value_sum is None else value_sum + v
        key_sum = k if key_sum is None else key_sum + k
    return key_sum, value_sum


def own_kernel(scale, keys, keep, xq, dkeep, dxr, stats, sums):
    rows = keep.shape[1]
    heads = keep.shape[2] // HD
    for head in range(heads):
        cols = slice(head * HD, (head + 1) * HD)
        steps = []
        for i, (q, d) in enumerate(((keep.at[2], dkeep), (xq, dxr))):
            span = slice(i * rows, (i + 1) * rows)
            steps.append((
                q[:, cols],
                d[:, cols],
                stats[2 * head : 2 * head + 1, span],
                stats[2 * head + 1 : 2 * head + 2, span],
            ))
        k, v = key_step(scale, keys[0, :, cols], keys[1, :, cols], steps)
        sums[0, :, cols] = k
        sums[1, :, cols] = v


def own_pass(*operands):
    _, rows, cols = operands[0].shape
    return pl.pallas_call(
        functools.partial(own_kernel, HD ** -0.5),
        out_shape=jax.ShapeDtypeStruct((2, rows, cols), F32),
        in_specs=[VM] * 6,
        out_specs=VM,
        compiler_params=params(30),
        cost_estimate=cost(),
        name="own_pass",
    )(*operands)


def key_kernel(scale, own, heads, runs, kv, e0, o0, se, so, sums, *refs):
    late, (out, fifth_q, fifth_d) = refs[:-3], refs[-3:]
    rows = kv.shape[1]
    even_ok, odd_ok, turned = place()
    from_even = turned if own else jnp.logical_not(turned)
    same, other = (0, 1) if own else (1, 0)
    where = {}
    for i, run in enumerate(runs):
        for at, head in enumerate(run):
            where[head] = (late[2 * i], late[2 * i + 1], slice(at * HD, (at + 1) * HD))

    def theirs(head, odd, half):
        ref, cols = where[head][odd], where[head][2]
        whole = slice(head * HD, (head + 1) * HD)
        first = (o0 if odd else e0)[2, :, whole] if half == 0 else ref[0, :, cols]
        return first, ref[1 + half, :, cols]

    def fill(odd):
        for i, head in enumerate(heads):
            to = slice(i * HD, (i + 1) * HD)
            fifth_q[:, to], fifth_d[:, to] = theirs(head, odd, other)

    @pl.when(from_even)
    def _():
        fill(0)

    @pl.when(jnp.logical_not(from_even))
    def _():
        fill(1)

    row = lax.broadcasted_iota(jnp.int32, se.shape, 0)
    nothing = jnp.where(lax.rem(row, 2) == 0, jnp.float32(BIG), jnp.float32(0.0))
    even = jnp.where(even_ok, se[...], nothing)
    odd = jnp.where(odd_ok, so[...], nothing)
    span = slice(same * rows, (same + 1) * rows)
    across = slice(other * rows, (other + 1) * rows)
    fifth = jnp.where(from_even, even[:, across], odd[:, across])
    for i, head in enumerate(heads):
        cols = slice(head * HD, (head + 1) * HD)
        to = slice(i * HD, (i + 1) * HD)
        a, b = 2 * head, 2 * head + 1
        steps = (
            (*theirs(head, 0, same), even[a : a + 1, span], even[b : b + 1, span]),
            (*theirs(head, 1, same), odd[a : a + 1, span], odd[b : b + 1, span]),
            (fifth_q[:, to], fifth_d[:, to], fifth[a : a + 1], fifth[b : b + 1]),
        )
        k, v = key_step(scale, kv[0, :, cols], kv[1, :, cols], steps)
        out[0, :, to] = ((k + sums[0, :, cols]) * scale).astype(BF16)
        out[1, :, to] = (v + sums[1, :, cols]).astype(BF16)


def key_pass(own, heads, runs, kv, *operands):
    _, rows, _ = kv.shape
    wide = HD * len(heads)
    return pl.pallas_call(
        functools.partial(key_kernel, HD ** -0.5, own, heads, runs),
        out_shape=jax.ShapeDtypeStruct((2, rows, wide), BF16),
        in_specs=[VM] * (1 + len(operands)),
        out_specs=VM,
        scratch_shapes=[pltpu.VMEM((rows, wide), BF16)] * 2,
        compiler_params=params(30),
        cost_estimate=cost(1e9),
        name="key_pass",
    )(kv, *operands)


def unpack_kernel(n_out, kept, *refs):
    got, outs, sem = refs[: -1 - n_out], refs[-1 - n_out : -1], refs[-1]
    half = kept.shape[2]
    x = lax.rem(lax.axis_index("ctx"), 2)
    mine = pl.multiple_of(x * half, half)
    theirs = pl.multiple_of((1 - x) * half, half)
    copies = []
    for i, out in enumerate(outs):
        pairs = [(kept.at[i], out.at[:, pl.ds(mine, half)])]
        first = 0
        for piece in got:
            width = piece.shape[2]
            pairs.append((piece.at[i], out.at[:, pl.ds(theirs + first, width)]))
            first += width
        for a, b in pairs:
            copies.append(pltpu.make_async_copy(a, b, sem.at[len(copies)]))
    for copy in copies:
        copy.start()
    for copy in copies:
        copy.wait()


def unpack(kept, *got):
    n, rows, half = kept.shape
    return pl.pallas_call(
        functools.partial(unpack_kernel, n),
        out_shape=(jax.ShapeDtypeStruct((rows, 2 * half), BF16),) * n,
        in_specs=[VM] * (1 + len(got)),
        out_specs=(ANY,) * n,
        scratch_shapes=[pltpu.SemaphoreType.DMA((n * (1 + len(got)),))],
        compiler_params=params(16),
        cost_estimate=cost(),
        name="unpack",
    )(kept, *got)


def body(queries, keys, values, out_grad, out_weight):
    length = lax.axis_size("ctx")
    lanes = lax.axis_size("mp")
    blocks = length // 2
    width = out_grad.shape[1]

    def over_mp(array, flip):
        return lax.ppermute(array, "mp", [(i, i ^ flip) for i in range(lanes)])

    def over_x(array):
        return lax.ppermute(array, "ctx", [(i, i ^ 1) for i in range(length)])

    def over_z(array, first):
        pairs = []
        for position in range(length):
            block = position // 2
            other = ((block - first) ^ 1) + first
            for lane in range(lanes):
                source = position * lanes + lane
                if block >= first and other < blocks:
                    target = (2 * other + position % 2) * lanes + lane
                else:
                    target = position * lanes + (lane ^ 1)
                pairs.append((source, target))
        return lax.ppermute(array, ("ctx", "mp"), pairs)

    y = over_mp(out_grad, 2)
    near = over_mp(out_grad, 1)
    keep, send_kv, send_q = pack(queries, keys, values)
    xkv, xq = over_x(send_kv), over_x(send_q)
    e0, o0 = over_z(keep, 0), over_z(keep, 1)
    acc, wy, wf = first_piece(out_grad, near, out_weight)
    e1, o1 = over_z(xkv, 0), over_z(xkv, 1)
    acc = after(acc, xkv, xq, flops=1e8)
    y, acc = lax.optimization_barrier((y, acc))
    far = over_mp(y, 1)
    acc = grad_piece(acc, y, wy, False)
    acc = after(acc, e0, o0, flops=3e9)
    dkeep, dsend = grad_piece(acc, far, wf, True)
    dxr = after(over_x(dsend), flops=6e9)

    xq, e1, o1 = lax.optimization_barrier((xq, e1, o1))
    heads = dkeep.shape[1] // HD
    runs = ((0,), tuple(range(1, heads))) if heads > 1 else ((0,),)
    late = [
        (over_z(piece, 0), over_z(piece, 1))
        for piece in join(tuple(HD * len(run) for run in runs), xq, dkeep, dxr)
    ]
    dq_send, marks = query_pass(False, xq, dxr, keep, xkv, e1, o1, e0, o0)
    dq_keep, stats = query_pass(True, keep, dkeep, keep, xkv, e0, o0, e1, o1, marks)
    dq_got = after(over_x(dq_send), flops=4e9)
    stats, first_e, first_o = lax.optimization_barrier((stats, *late[0]))
    late[0] = (first_e, first_o)
    se, so = over_z(stats, 0), over_z(stats, 1)
    sums = own_pass(xkv, keep, xq, dkeep, dxr, stats)
    own_sums = own_pass(keep, keep, xq, dkeep, dxr, stats)
    dq, = unpack(dq_keep, dq_got)
    got = []
    for i, (run, pair) in enumerate(zip(runs, late)):
        if i > 0:
            sums = after(sums, *pair, flops=6e9)
        if i == len(runs) - 1:
            sums, dq = lax.optimization_barrier((sums, dq))
        for head in run:
            piece = key_pass(False, (head,), (run,), xkv, e0, o0, se, so, sums, *pair)
            got.append(over_x(piece))
    every = [array for pair in late for array in pair]
    kv_keep = key_pass(True, tuple(range(heads)), runs, keep, e0, o0, se, so, own_sums, *every)
    return (dq, *unpack(kv_keep, *got))


def solution(mesh):
    placed = (P("ctx", "mp"), P("ctx", "mp"), P("ctx", "mp"), P("ctx", "mp"), P("mp", None))
    return jax.shard_map(
        body,
        mesh=mesh,
        in_specs=placed,
        out_specs=(P("ctx", "mp"), P("ctx", "mp"), P("ctx", "mp")),
        check_vma=False,
    )
```

```python
import functools
import math

import jax
import jax.numpy as jnp
from jax import lax
from jax.experimental import pallas as pl
from jax.experimental.pallas import tpu as pltpu
from jax.sharding import PartitionSpec as P

HD = 128
BF16 = jnp.bfloat16
F32 = jnp.float32
BIG = 1e30
ANY = pl.BlockSpec(memory_space=pl.ANY)
VM = pl.BlockSpec(memory_space=pltpu.VMEM)
HBM = pl.BlockSpec(memory_space=pltpu.HBM)


def params(mib=40):
    return pltpu.CompilerParams(vmem_limit_bytes=mib << 20)


def nt(a, b):
    return lax.dot_general(a, b, (((1,), (1,)), ((), ())), preferred_element_type=F32)


def nn(a, b):
    return lax.dot_general(a, b, (((1,), (0,)), ((), ())), preferred_element_type=F32)


def cost(flops=1):
    return pl.CostEstimate(flops=int(flops), bytes_accessed=1, transcendentals=0)


def pack_kernel(q, k, v, keep, send_kv, send_q, sem):
    half = q.shape[1] // 2
    x = lax.rem(lax.axis_index("ctx"), 2)
    mine = pl.ds(pl.multiple_of(x * half, half), half)
    theirs = pl.ds(pl.multiple_of((1 - x) * half, half), half)
    pairs = (
        (k.at[:, theirs], send_kv.at[0]),
        (v.at[:, theirs], send_kv.at[1]),
        (k.at[:, mine], keep.at[0]),
        (v.at[:, mine], keep.at[1]),
        (q.at[:, mine], keep.at[2]),
        (q.at[:, theirs], send_q),
    )
    copies = [pltpu.make_async_copy(a, b, sem.at[i]) for i, (a, b) in enumerate(pairs)]
    for copy in copies:
        copy.start()
    for copy in copies:
        copy.wait()


def pack(q, k, v):
    rows, cols = q.shape
    three, two = (jax.ShapeDtypeStruct((n, rows, cols // 2), BF16) for n in (3, 2))
    one = jax.ShapeDtypeStruct((rows, cols // 2), BF16)
    return pl.pallas_call(
        pack_kernel,
        out_shape=(three, two, one),
        in_specs=[ANY] * 3,
        out_specs=(VM,) * 3,
        scratch_shapes=[pltpu.SemaphoreType.DMA((6,))],
        compiler_params=params(60),
        cost_estimate=cost(),
        name="pack",
    )(q, k, v)


def join_kernel(*refs):
    for i, ref in enumerate(refs[:-1]):
        refs[-1][i] = ref[...]


def join(*pieces):
    return pl.pallas_call(
        join_kernel,
        out_shape=jax.ShapeDtypeStruct((len(pieces), *pieces[0].shape), BF16),
        in_specs=[VM] * len(pieces),
        out_specs=VM,
        compiler_params=params(16),
        cost_estimate=cost(),
        name="join",
    )(*pieces)


def first_kernel(og, near, w, acc, wy, wf, wbuf, sem):
    width = og.shape[1]
    me = lax.axis_index("mp")
    copies = []
    for flip, target in enumerate((wbuf.at[0], wbuf.at[1], wy, wf)):
        first = pl.multiple_of(jnp.bitwise_xor(me, flip) * width, width)
        copies.append(pltpu.make_async_copy(w.at[:, pl.ds(first, width)], target, sem.at[flip]))
    for copy in copies:
        copy.start()
    copies[0].wait()
    acc[...] = nt(og[...], wbuf[0])
    copies[1].wait()
    acc[...] += nt(near[...], wbuf[1])
    copies[2].wait()
    copies[3].wait()


def first_piece(og, near, w):
    rows, width = og.shape
    heads = w.shape[0]
    part = jax.ShapeDtypeStruct((heads, width), BF16)
    return pl.pallas_call(
        first_kernel,
        out_shape=(jax.ShapeDtypeStruct((rows, heads), F32), part, part),
        in_specs=[VM, VM, ANY],
        out_specs=(VM, VM, VM),
        scratch_shapes=[pltpu.VMEM((2, heads, width), BF16), pltpu.SemaphoreType.DMA((4,))],
        compiler_params=params(46),
        cost_estimate=cost(),
        name="head_grad_first",
    )(og, near, w)


def next_kernel(acc, piece, w, out):
    out[...] = acc[...] + nt(piece[...], w[...])


def last_kernel(acc, piece, w, keep, send):
    total = acc[...] + nt(piece[...], w[...])
    half = total.shape[1] // 2
    x = lax.rem(lax.axis_index("ctx"), 2)
    low = total[:, :half].astype(BF16)
    high = total[:, half:].astype(BF16)

    @pl.when(x == 0)
    def _():
        keep[...] = low
        send[...] = high

    @pl.when(x != 0)
    def _():
        keep[...] = high
        send[...] = low


def grad_piece(acc, piece, w, last):
    rows, heads = acc.shape
    half = jax.ShapeDtypeStruct((rows, heads // 2), BF16)
    return pl.pallas_call(
        last_kernel if last else next_kernel,
        out_shape=(half, half) if last else jax.ShapeDtypeStruct((rows, heads), F32),
        in_specs=[VM] * 3,
        out_specs=(VM, VM) if last else VM,
        compiler_params=params(30),
        cost_estimate=cost(),
        name="head_grad",
    )(acc, piece, w)


def after(value, *others, flops):
    return pl.pallas_call(
        lambda *refs: None,
        out_shape=jax.ShapeDtypeStruct(value.shape, value.dtype),
        in_specs=[ANY] * (1 + len(others)),
        out_specs=ANY,
        input_output_aliases={0: 0},
        compiler_params=params(16),
        cost_estimate=cost(flops),
        name="after",
    )(value, *others)


def place():
    position = lax.axis_index("ctx")
    block = position // 2
    low_ok = block > 0
    high_ok = block < lax.axis_size("ctx") // 2 - 1
    odd = lax.rem(block, 2) == 1
    even_ok = jnp.logical_or(jnp.logical_and(odd, low_ok), jnp.logical_and(jnp.logical_not(odd), high_ok))
    odd_ok = jnp.logical_or(jnp.logical_and(odd, high_ok), jnp.logical_and(jnp.logical_not(odd), low_ok))
    turned = lax.rem(position + block, 2) == 1
    return even_ok, odd_ok, turned


def off(ok):
    return jnp.where(ok, 0.0, BIG).astype(F32)


def query_kernel(scale, own, has_marks, *refs):
    refs = list(refs)
    q, d, keep, xr, e, o, e_other, o_other = refs[:8]
    q = q if len(q.shape) == 2 else q.at[2]
    before = refs[8] if has_marks else None
    out, stats, fifth = refs[-3:]
    rows = q.shape[0]
    heads = q.shape[1] // HD
    even_ok, odd_ok, turned = place()
    from_even = turned if own else jnp.logical_not(turned)

    @pl.when(from_even)
    def _():
        fifth[...] = e_other[0:2]

    @pl.when(jnp.logical_not(from_even))
    def _():
        fifth[...] = o_other[0:2]

    c = scale * math.log2(math.e)
    even_off, odd_off = off(even_ok), off(odd_ok)
    lane = lax.broadcasted_iota(jnp.int32, (rows, HD), 1)
    runs = (
        (keep, None),
        (xr, None),
        (e, even_off),
        (o, odd_off),
        (fifth, jnp.where(from_even, even_off, odd_off)),
    )
    mark = jnp.zeros((rows, HD), F32)
    for head in range(heads):
        cols = slice(head * HD, (head + 1) * HD)
        query = q[:, cols]
        grad = d[:, cols]
        scores = [nt(query, ref[0, :, cols]) for ref, _ in runs]
        top = None
        for s, (_, gone) in zip(scores, runs):
            m = jnp.max(s, -1, keepdims=True)
            m = m if gone is None else m - gone
            top = m if top is None else jnp.maximum(top, m)
        top = top * c
        weights = [
            jnp.exp2(s * c - (top if gone is None else top + gone))
            for s, (_, gone) in zip(scores, runs)
        ]
        total = jnp.sum(sum(weights), -1, keepdims=True)
        grads = [nt(grad, ref[1, :, cols]) for ref, _ in runs]
        inverse = 1.0 / total
        delta = jnp.sum(sum(w * g for w, g in zip(weights, grads)), -1, keepdims=True) * inverse
        result = sum(
            nn((w * (g - delta)).astype(BF16), ref[0, :, cols])
            for w, g, (ref, _) in zip(weights, grads, runs)
        )
        out[0, :, cols] = (result * (inverse * scale)).astype(BF16)
        mark = jnp.where(lane == 2 * head, top + jnp.log2(total), mark)
        mark = jnp.where(lane == 2 * head + 1, delta, mark)
    marks = jnp.transpose(mark)[: stats.shape[0], :]
    if has_marks:
        stats[:, :rows] = marks
        stats[:, rows:] = before[...]
    else:
        stats[...] = marks


def query_pass(own, q, d, keep, xr, e, o, e_other, o_other, before=None):
    rows, cols = d.shape
    operands = [q, d, keep, xr, e, o, e_other, o_other]
    if before is not None:
        operands.append(before)
    return pl.pallas_call(
        functools.partial(query_kernel, HD ** -0.5, own, before is not None),
        out_shape=(
            jax.ShapeDtypeStruct((1, rows, cols), BF16),
            jax.ShapeDtypeStruct((8, rows if before is None else 2 * rows), F32),
        ),
        in_specs=[VM] * len(operands),
        out_specs=(VM, VM),
        scratch_shapes=[pltpu.VMEM((2, rows, cols), BF16)],
        compiler_params=params(30),
        cost_estimate=cost(6e9 if own else 1),
        name="query_pass",
    )(*operands)


def key_step(scale, key, value, steps):
    c = scale * math.log2(math.e)
    key_sum = None
    value_sum = None
    for query, grad, total, delta in steps:
        weight = jnp.exp2(nt(key, query) * c - total)
        change = weight * (nt(value, grad) - delta)
        v = nn(weight.astype(BF16), grad)
        k = nn(change.astype(BF16), query)
        value_sum = v if value_sum is None else value_sum + v
        key_sum = k if key_sum is None else key_sum + k
    return key_sum, value_sum


def own_kernel(scale, keys, keep, xq, dkeep, dxr, stats, sums):
    rows = keep.shape[1]
    heads = keep.shape[2] // HD
    for head in range(heads):
        cols = slice(head * HD, (head + 1) * HD)
        steps = []
        for i, (q, d) in enumerate(((keep.at[2], dkeep), (xq, dxr))):
            span = slice(i * rows, (i + 1) * rows)
            steps.append((
                q[:, cols],
                d[:, cols],
                stats[2 * head : 2 * head + 1, span],
                stats[2 * head + 1 : 2 * head + 2, span],
            ))
        k, v = key_step(scale, keys[0, :, cols], keys[1, :, cols], steps)
        sums[0, :, cols] = k
        sums[1, :, cols] = v


def own_pass(*operands):
    _, rows, cols = operands[0].shape
    return pl.pallas_call(
        functools.partial(own_kernel, HD ** -0.5),
        out_shape=jax.ShapeDtypeStruct((2, rows, cols), F32),
        in_specs=[VM] * 6,
        out_specs=VM,
        compiler_params=params(30),
        cost_estimate=cost(),
        name="own_pass",
    )(*operands)


def key_kernel(scale, own, heads, kv, e0, o0, late_e, late_o, se, so, sums, out, fifth_q, fifth_d):
    rows = kv.shape[1]
    even_ok, odd_ok, turned = place()
    from_even = turned if own else jnp.logical_not(turned)
    even_q, odd_q = (e0.at[2], late_e.at[0]), (o0.at[2], late_o.at[0])
    even_d, odd_d = (late_e.at[1], late_e.at[2]), (late_o.at[1], late_o.at[2])
    same, other = (0, 1) if own else (1, 0)
    wanted = slice(heads[0] * HD, (heads[-1] + 1) * HD)

    @pl.when(from_even)
    def _():
        fifth_q[...] = even_q[other][:, wanted]
        fifth_d[...] = even_d[other][:, wanted]

    @pl.when(jnp.logical_not(from_even))
    def _():
        fifth_q[...] = odd_q[other][:, wanted]
        fifth_d[...] = odd_d[other][:, wanted]

    row = lax.broadcasted_iota(jnp.int32, se.shape, 0)
    nothing = jnp.where(lax.rem(row, 2) == 0, jnp.float32(BIG), jnp.float32(0.0))
    even = jnp.where(even_ok, se[...], nothing)
    odd = jnp.where(odd_ok, so[...], nothing)
    span = slice(same * rows, (same + 1) * rows)
    across = slice(other * rows, (other + 1) * rows)
    fifth = jnp.where(from_even, even[:, across], odd[:, across])
    for i, head in enumerate(heads):
        cols = slice(head * HD, (head + 1) * HD)
        to = slice(i * HD, (i + 1) * HD)
        a, b = 2 * head, 2 * head + 1
        steps = (
            (even_q[same][:, cols], even_d[same][:, cols], even[a : a + 1, span], even[b : b + 1, span]),
            (odd_q[same][:, cols], odd_d[same][:, cols], odd[a : a + 1, span], odd[b : b + 1, span]),
            (fifth_q[:, to], fifth_d[:, to], fifth[a : a + 1], fifth[b : b + 1]),
        )
        k, v = key_step(scale, kv[0, :, cols], kv[1, :, cols], steps)
        out[0, :, to] = ((k + sums[0, :, cols]) * scale).astype(BF16)
        out[1, :, to] = (v + sums[1, :, cols]).astype(BF16)


def key_pass(own, heads, kv, *operands):
    _, rows, _ = kv.shape
    wide = HD * len(heads)
    return pl.pallas_call(
        functools.partial(key_kernel, HD ** -0.5, own, heads),
        out_shape=jax.ShapeDtypeStruct((2, rows, wide), BF16),
        in_specs=[VM] * (1 + len(operands)),
        out_specs=VM,
        scratch_shapes=[pltpu.VMEM((rows, wide), BF16)] * 2,
        compiler_params=params(30),
        cost_estimate=cost(1e9),
        name="key_pass",
    )(kv, *operands)


def unpack_kernel(n_out, kept, *refs):
    got, outs, sem = refs[: -1 - n_out], refs[-1 - n_out : -1], refs[-1]
    half = kept.shape[2]
    x = lax.rem(lax.axis_index("ctx"), 2)
    mine = pl.multiple_of(x * half, half)
    theirs = pl.multiple_of((1 - x) * half, half)
    copies = []
    for i, out in enumerate(outs):
        pairs = [(kept.at[i], out.at[:, pl.ds(mine, half)])]
        first = 0
        for piece in got:
            width = piece.shape[2]
            pairs.append((piece.at[i], out.at[:, pl.ds(theirs + first, width)]))
            first += width
        for a, b in pairs:
            copies.append(pltpu.make_async_copy(a, b, sem.at[len(copies)]))
    for copy in copies:
        copy.start()
    for copy in copies:
        copy.wait()


def unpack(kept, *got):
    n, rows, half = kept.shape
    return pl.pallas_call(
        functools.partial(unpack_kernel, n),
        out_shape=(jax.ShapeDtypeStruct((rows, 2 * half), BF16),) * n,
        in_specs=[VM] * (1 + len(got)),
        out_specs=(ANY,) * n,
        scratch_shapes=[pltpu.SemaphoreType.DMA((n * (1 + len(got)),))],
        compiler_params=params(16),
        cost_estimate=cost(),
        name="unpack",
    )(kept, *got)


def finish_kernel(dk_in, dv_in, last, dk, dv, sem):
    del dk_in, dv_in
    width = last.shape[2]
    half = dk.shape[1] // 2
    x = lax.rem(lax.axis_index("ctx"), 2)
    columns = pl.ds(pl.multiple_of((1 - x) * half + half - width, width), width)
    copies = [
        pltpu.make_async_copy(last.at[i], out.at[:, columns], sem.at[i])
        for i, out in enumerate((dk, dv))
    ]
    for copy in copies:
        copy.start()
    for copy in copies:
        copy.wait()


def finish(dk, dv, last):
    return pl.pallas_call(
        finish_kernel,
        out_shape=(jax.ShapeDtypeStruct(dk.shape, dk.dtype),) * 2,
        in_specs=[ANY, ANY, VM],
        out_specs=(ANY, ANY),
        input_output_aliases={0: 0, 1: 1},
        scratch_shapes=[pltpu.SemaphoreType.DMA((2,))],
        compiler_params=params(16),
        cost_estimate=cost(),
        name="finish",
    )(dk, dv, last)


def body(queries, keys, values, out_grad, out_weight):
    length = lax.axis_size("ctx")
    lanes = lax.axis_size("mp")
    blocks = length // 2
    width = out_grad.shape[1]

    def over_mp(array, flip):
        return lax.ppermute(array, "mp", [(i, i ^ flip) for i in range(lanes)])

    def over_x(array):
        return lax.ppermute(array, "ctx", [(i, i ^ 1) for i in range(length)])

    def over_z(array, first):
        pairs = []
        for position in range(length):
            block = position // 2
            other = ((block - first) ^ 1) + first
            for lane in range(lanes):
                source = position * lanes + lane
                if block >= first and other < blocks:
                    target = (2 * other + position % 2) * lanes + lane
                else:
                    target = position * lanes + (lane ^ 1)
                pairs.append((source, target))
        return lax.ppermute(array, ("ctx", "mp"), pairs)

    y = over_mp(out_grad, 2)
    near = over_mp(out_grad, 1)
    keep, send_kv, send_q = pack(queries, keys, values)
    xkv, xq = over_x(send_kv), over_x(send_q)
    e0, o0 = over_z(keep, 0), over_z(keep, 1)
    acc, wy, wf = first_piece(out_grad, near, out_weight)
    e1, o1 = over_z(xkv, 0), over_z(xkv, 1)
    acc = after(acc, xkv, xq, flops=1e8)
    y, acc = lax.optimization_barrier((y, acc))
    far = over_mp(y, 1)
    acc = grad_piece(acc, y, wy, False)
    acc = after(acc, e0, o0, flops=3e9)
    dkeep, dsend = grad_piece(acc, far, wf, True)
    dxr = after(over_x(dsend), flops=6e9)

    xq, e1, o1 = lax.optimization_barrier((xq, e1, o1))
    late = join(xq, dkeep, dxr)
    late_e, late_o = over_z(late, 0), over_z(late, 1)
    dq_send, marks = query_pass(False, xq, dxr, keep, xkv, e1, o1, e0, o0)
    dq_keep, stats = query_pass(True, keep, dkeep, keep, xkv, e0, o0, e1, o1, marks)
    dq_got = after(over_x(dq_send), flops=6e9)
    se, so = over_z(stats, 0), over_z(stats, 1)
    sums = own_pass(xkv, keep, xq, dkeep, dxr, stats)
    sums = after(sums, late_e, late_o, flops=3e9)
    own_sums = own_pass(keep, keep, xq, dkeep, dxr, stats)
    heads = dkeep.shape[1] // HD
    theirs = (e0, o0, late_e, late_o, se, so)
    got = []
    for head in range(heads):
        if head == 1:
            dq, = unpack(dq_keep, dq_got)
            sums, dq = lax.optimization_barrier((sums, dq))
        got.append(over_x(key_pass(False, (head,), xkv, *theirs, sums)))
    kv_keep = key_pass(True, tuple(range(heads)), keep, *theirs, own_sums)
    *early, last = got
    dk, dv = unpack(kv_keep, *early)
    return (dq, *finish(dk, dv, last))


def solution(mesh):
    placed = (P("ctx", "mp"), P("ctx", "mp"), P("ctx", "mp"), P("ctx", "mp"), P("mp", None))
    return jax.shard_map(
        body,
        mesh=mesh,
        in_specs=placed,
        out_specs=(P("ctx", "mp"), P("ctx", "mp"), P("ctx", "mp")),
        check_vma=False,
    )
```

```python
import functools
import math

import jax
import jax.numpy as jnp
from jax import lax
from jax.experimental import pallas as pl
from jax.experimental.pallas import tpu as pltpu
from jax.sharding import PartitionSpec as P

HD = 128
BF16 = jnp.bfloat16
F32 = jnp.float32
BIG = 1e30
ANY = pl.BlockSpec(memory_space=pl.ANY)
VM = pl.BlockSpec(memory_space=pltpu.VMEM)
HBM = pl.BlockSpec(memory_space=pltpu.HBM)


def params(mib=40):
    return pltpu.CompilerParams(vmem_limit_bytes=mib << 20)


def nt(a, b):
    return lax.dot_general(a, b, (((1,), (1,)), ((), ())), preferred_element_type=F32)


def nn(a, b):
    return lax.dot_general(a, b, (((1,), (0,)), ((), ())), preferred_element_type=F32)


def cost(flops=1):
    return pl.CostEstimate(flops=int(flops), bytes_accessed=1, transcendentals=0)


def pack_kernel(q, k, v, keep, send_kv, send_q, sem):
    half = q.shape[1] // 2
    x = lax.rem(lax.axis_index("ctx"), 2)
    mine = pl.ds(pl.multiple_of(x * half, half), half)
    theirs = pl.ds(pl.multiple_of((1 - x) * half, half), half)
    pairs = (
        (k.at[:, theirs], send_kv.at[0]),
        (v.at[:, theirs], send_kv.at[1]),
        (k.at[:, mine], keep.at[0]),
        (v.at[:, mine], keep.at[1]),
        (q.at[:, mine], keep.at[2]),
        (q.at[:, theirs], send_q),
    )
    copies = [pltpu.make_async_copy(a, b, sem.at[i]) for i, (a, b) in enumerate(pairs)]
    for copy in copies:
        copy.start()
    for copy in copies:
        copy.wait()


def pack(q, k, v):
    rows, cols = q.shape
    three, two = (jax.ShapeDtypeStruct((n, rows, cols // 2), BF16) for n in (3, 2))
    one = jax.ShapeDtypeStruct((rows, cols // 2), BF16)
    return pl.pallas_call(
        pack_kernel,
        out_shape=(three, two, one),
        in_specs=[ANY] * 3,
        out_specs=(VM,) * 3,
        scratch_shapes=[pltpu.SemaphoreType.DMA((6,))],
        compiler_params=params(60),
        cost_estimate=cost(),
        name="pack",
    )(q, k, v)


def join_kernel(*refs):
    for i, ref in enumerate(refs[:-1]):
        refs[-1][i] = ref[...]


def join(*pieces):
    return pl.pallas_call(
        join_kernel,
        out_shape=jax.ShapeDtypeStruct((len(pieces), *pieces[0].shape), BF16),
        in_specs=[VM] * len(pieces),
        out_specs=VM,
        compiler_params=params(16),
        cost_estimate=cost(),
        name="join",
    )(*pieces)


def first_kernel(og, near, w, acc, wy, wf, wbuf, sem):
    width = og.shape[1]
    me = lax.axis_index("mp")
    copies = []
    for flip, target in enumerate((wbuf.at[0], wbuf.at[1], wy, wf)):
        first = pl.multiple_of(jnp.bitwise_xor(me, flip) * width, width)
        copies.append(pltpu.make_async_copy(w.at[:, pl.ds(first, width)], target, sem.at[flip]))
    for copy in copies:
        copy.start()
    copies[0].wait()
    acc[...] = nt(og[...], wbuf[0])
    copies[1].wait()
    acc[...] += nt(near[...], wbuf[1])
    copies[2].wait()
    copies[3].wait()


def first_piece(og, near, w):
    rows, width = og.shape
    heads = w.shape[0]
    part = jax.ShapeDtypeStruct((heads, width), BF16)
    return pl.pallas_call(
        first_kernel,
        out_shape=(jax.ShapeDtypeStruct((rows, heads), F32), part, part),
        in_specs=[VM, VM, ANY],
        out_specs=(VM, VM, VM),
        scratch_shapes=[pltpu.VMEM((2, heads, width), BF16), pltpu.SemaphoreType.DMA((4,))],
        compiler_params=params(46),
        cost_estimate=cost(),
        name="head_grad_first",
    )(og, near, w)


def next_kernel(acc, piece, w, out):
    out[...] = acc[...] + nt(piece[...], w[...])


def last_kernel(acc, piece, w, keep, send):
    total = acc[...] + nt(piece[...], w[...])
    half = total.shape[1] // 2
    x = lax.rem(lax.axis_index("ctx"), 2)
    low = total[:, :half].astype(BF16)
    high = total[:, half:].astype(BF16)

    @pl.when(x == 0)
    def _():
        keep[...] = low
        send[...] = high

    @pl.when(x != 0)
    def _():
        keep[...] = high
        send[...] = low


def grad_piece(acc, piece, w, last):
    rows, heads = acc.shape
    half = jax.ShapeDtypeStruct((rows, heads // 2), BF16)
    return pl.pallas_call(
        last_kernel if last else next_kernel,
        out_shape=(half, half) if last else jax.ShapeDtypeStruct((rows, heads), F32),
        in_specs=[VM] * 3,
        out_specs=(VM, VM) if last else VM,
        compiler_params=params(30),
        cost_estimate=cost(),
        name="head_grad",
    )(acc, piece, w)


def after(value, *others, flops):
    return pl.pallas_call(
        lambda *refs: None,
        out_shape=jax.ShapeDtypeStruct(value.shape, value.dtype),
        in_specs=[ANY] * (1 + len(others)),
        out_specs=ANY,
        input_output_aliases={0: 0},
        compiler_params=params(16),
        cost_estimate=cost(flops),
        name="after",
    )(value, *others)


def place():
    position = lax.axis_index("ctx")
    block = position // 2
    low_ok = block > 0
    high_ok = block < lax.axis_size("ctx") // 2 - 1
    odd = lax.rem(block, 2) == 1
    even_ok = jnp.logical_or(jnp.logical_and(odd, low_ok), jnp.logical_and(jnp.logical_not(odd), high_ok))
    odd_ok = jnp.logical_or(jnp.logical_and(odd, high_ok), jnp.logical_and(jnp.logical_not(odd), low_ok))
    turned = lax.rem(position + block, 2) == 1
    return even_ok, odd_ok, turned


def off(ok):
    return jnp.where(ok, 0.0, BIG).astype(F32)


def query_kernel(scale, own, has_marks, *refs):
    refs = list(refs)
    q, d, keep, xr, e, o, e_other, o_other = refs[:8]
    q = q if len(q.shape) == 2 else q.at[2]
    before = refs[8] if has_marks else None
    out, stats, fifth = refs[-3:]
    rows = q.shape[0]
    heads = q.shape[1] // HD
    even_ok, odd_ok, turned = place()
    from_even = turned if own else jnp.logical_not(turned)

    @pl.when(from_even)
    def _():
        fifth[...] = e_other[0:2]

    @pl.when(jnp.logical_not(from_even))
    def _():
        fifth[...] = o_other[0:2]

    c = scale * math.log2(math.e)
    even_off, odd_off = off(even_ok), off(odd_ok)
    lane = lax.broadcasted_iota(jnp.int32, (rows, HD), 1)
    runs = (
        (keep, None),
        (xr, None),
        (e, even_off),
        (o, odd_off),
        (fifth, jnp.where(from_even, even_off, odd_off)),
    )
    mark = jnp.zeros((rows, HD), F32)
    for head in range(heads):
        cols = slice(head * HD, (head + 1) * HD)
        query = q[:, cols]
        grad = d[:, cols]
        scores = [nt(query, ref[0, :, cols]) for ref, _ in runs]
        top = None
        for s, (_, gone) in zip(scores, runs):
            m = jnp.max(s, -1, keepdims=True)
            m = m if gone is None else m - gone
            top = m if top is None else jnp.maximum(top, m)
        top = top * c
        weights = [
            jnp.exp2(s * c - (top if gone is None else top + gone))
            for s, (_, gone) in zip(scores, runs)
        ]
        total = jnp.sum(sum(weights), -1, keepdims=True)
        grads = [nt(grad, ref[1, :, cols]) for ref, _ in runs]
        inverse = 1.0 / total
        delta = jnp.sum(sum(w * g for w, g in zip(weights, grads)), -1, keepdims=True) * inverse
        result = sum(
            nn((w * (g - delta)).astype(BF16), ref[0, :, cols])
            for w, g, (ref, _) in zip(weights, grads, runs)
        )
        out[0, :, cols] = (result * (inverse * scale)).astype(BF16)
        mark = jnp.where(lane == 2 * head, top + jnp.log2(total), mark)
        mark = jnp.where(lane == 2 * head + 1, delta, mark)
    marks = jnp.transpose(mark)[: stats.shape[0], :]
    if has_marks:
        stats[:, :rows] = marks
        stats[:, rows:] = before[...]
    else:
        stats[...] = marks


def query_pass(own, q, d, keep, xr, e, o, e_other, o_other, before=None):
    rows, cols = d.shape
    operands = [q, d, keep, xr, e, o, e_other, o_other]
    if before is not None:
        operands.append(before)
    return pl.pallas_call(
        functools.partial(query_kernel, HD ** -0.5, own, before is not None),
        out_shape=(
            jax.ShapeDtypeStruct((1, rows, cols), BF16),
            jax.ShapeDtypeStruct((8, rows if before is None else 2 * rows), F32),
        ),
        in_specs=[VM] * len(operands),
        out_specs=(VM, VM),
        scratch_shapes=[pltpu.VMEM((2, rows, cols), BF16)],
        compiler_params=params(30),
        cost_estimate=cost(6e9 if own else 1),
        name="query_pass",
    )(*operands)


def key_step(scale, key, value, steps):
    c = scale * math.log2(math.e)
    key_sum = None
    value_sum = None
    for query, grad, total, delta in steps:
        weight = jnp.exp2(nt(key, query) * c - total)
        change = weight * (nt(value, grad) - delta)
        v = nn(weight.astype(BF16), grad)
        k = nn(change.astype(BF16), query)
        value_sum = v if value_sum is None else value_sum + v
        key_sum = k if key_sum is None else key_sum + k
    return key_sum, value_sum


def own_kernel(scale, keys, keep, xq, dkeep, dxr, stats, sums):
    rows = keep.shape[1]
    heads = keep.shape[2] // HD
    for head in range(heads):
        cols = slice(head * HD, (head + 1) * HD)
        steps = []
        for i, (q, d) in enumerate(((keep.at[2], dkeep), (xq, dxr))):
            span = slice(i * rows, (i + 1) * rows)
            steps.append((
                q[:, cols],
                d[:, cols],
                stats[2 * head : 2 * head + 1, span],
                stats[2 * head + 1 : 2 * head + 2, span],
            ))
        k, v = key_step(scale, keys[0, :, cols], keys[1, :, cols], steps)
        sums[0, :, cols] = k
        sums[1, :, cols] = v


def own_pass(*operands):
    _, rows, cols = operands[0].shape
    return pl.pallas_call(
        functools.partial(own_kernel, HD ** -0.5),
        out_shape=jax.ShapeDtypeStruct((2, rows, cols), F32),
        in_specs=[VM] * 6,
        out_specs=VM,
        compiler_params=params(30),
        cost_estimate=cost(),
        name="own_pass",
    )(*operands)


def key_kernel(scale, own, heads, kv, e0, o0, qe, qo, late_e, late_o, se, so, sums, out, fifth_q, fifth_d):
    rows = kv.shape[1]
    even_ok, odd_ok, turned = place()
    from_even = turned if own else jnp.logical_not(turned)
    even_q, odd_q = (e0.at[2], qe), (o0.at[2], qo)
    even_d, odd_d = (late_e.at[0], late_e.at[1]), (late_o.at[0], late_o.at[1])
    same, other = (0, 1) if own else (1, 0)
    wanted = slice(heads[0] * HD, (heads[-1] + 1) * HD)

    @pl.when(from_even)
    def _():
        fifth_q[...] = even_q[other][:, wanted]
        fifth_d[...] = even_d[other][:, wanted]

    @pl.when(jnp.logical_not(from_even))
    def _():
        fifth_q[...] = odd_q[other][:, wanted]
        fifth_d[...] = odd_d[other][:, wanted]

    row = lax.broadcasted_iota(jnp.int32, se.shape, 0)
    nothing = jnp.where(lax.rem(row, 2) == 0, jnp.float32(BIG), jnp.float32(0.0))
    even = jnp.where(even_ok, se[...], nothing)
    odd = jnp.where(odd_ok, so[...], nothing)
    span = slice(same * rows, (same + 1) * rows)
    across = slice(other * rows, (other + 1) * rows)
    fifth = jnp.where(from_even, even[:, across], odd[:, across])
    for i, head in enumerate(heads):
        cols = slice(head * HD, (head + 1) * HD)
        to = slice(i * HD, (i + 1) * HD)
        a, b = 2 * head, 2 * head + 1
        steps = (
            (even_q[same][:, cols], even_d[same][:, cols], even[a : a + 1, span], even[b : b + 1, span]),
            (odd_q[same][:, cols], odd_d[same][:, cols], odd[a : a + 1, span], odd[b : b + 1, span]),
            (fifth_q[:, to], fifth_d[:, to], fifth[a : a + 1], fifth[b : b + 1]),
        )
        k, v = key_step(scale, kv[0, :, cols], kv[1, :, cols], steps)
        out[0, :, to] = ((k + sums[0, :, cols]) * scale).astype(BF16)
        out[1, :, to] = (v + sums[1, :, cols]).astype(BF16)


def key_pass(own, heads, kv, *operands):
    _, rows, _ = kv.shape
    wide = HD * len(heads)
    return pl.pallas_call(
        functools.partial(key_kernel, HD ** -0.5, own, heads),
        out_shape=jax.ShapeDtypeStruct((2, rows, wide), BF16),
        in_specs=[VM] * (1 + len(operands)),
        out_specs=VM,
        scratch_shapes=[pltpu.VMEM((rows, wide), BF16)] * 2,
        compiler_params=params(30),
        cost_estimate=cost(1e9),
        name="key_pass",
    )(kv, *operands)


def unpack_kernel(n_out, kept, *refs):
    got, outs, sem = refs[: -1 - n_out], refs[-1 - n_out : -1], refs[-1]
    half = kept.shape[2]
    x = lax.rem(lax.axis_index("ctx"), 2)
    mine = pl.multiple_of(x * half, half)
    theirs = pl.multiple_of((1 - x) * half, half)
    copies = []
    for i, out in enumerate(outs):
        pairs = [(kept.at[i], out.at[:, pl.ds(mine, half)])]
        first = 0
        for piece in got:
            width = piece.shape[2]
            pairs.append((piece.at[i], out.at[:, pl.ds(theirs + first, width)]))
            first += width
        for a, b in pairs:
            copies.append(pltpu.make_async_copy(a, b, sem.at[len(copies)]))
    for copy in copies:
        copy.start()
    for copy in copies:
        copy.wait()


def unpack(kept, *got):
    n, rows, half = kept.shape
    return pl.pallas_call(
        functools.partial(unpack_kernel, n),
        out_shape=(jax.ShapeDtypeStruct((rows, 2 * half), BF16),) * n,
        in_specs=[VM] * (1 + len(got)),
        out_specs=(ANY,) * n,
        scratch_shapes=[pltpu.SemaphoreType.DMA((n * (1 + len(got)),))],
        compiler_params=params(16),
        cost_estimate=cost(),
        name="unpack",
    )(kept, *got)


def finish_kernel(dk_in, dv_in, last, dk, dv, sem):
    del dk_in, dv_in
    width = last.shape[2]
    half = dk.shape[1] // 2
    x = lax.rem(lax.axis_index("ctx"), 2)
    columns = pl.ds(pl.multiple_of((1 - x) * half + half - width, width), width)
    copies = [
        pltpu.make_async_copy(last.at[i], out.at[:, columns], sem.at[i])
        for i, out in enumerate((dk, dv))
    ]
    for copy in copies:
        copy.start()
    for copy in copies:
        copy.wait()


def finish(dk, dv, last):
    return pl.pallas_call(
        finish_kernel,
        out_shape=(jax.ShapeDtypeStruct(dk.shape, dk.dtype),) * 2,
        in_specs=[ANY, ANY, VM],
        out_specs=(ANY, ANY),
        input_output_aliases={0: 0, 1: 1},
        scratch_shapes=[pltpu.SemaphoreType.DMA((2,))],
        compiler_params=params(16),
        cost_estimate=cost(),
        name="finish",
    )(dk, dv, last)


def body(queries, keys, values, out_grad, out_weight):
    length = lax.axis_size("ctx")
    lanes = lax.axis_size("mp")
    blocks = length // 2
    width = out_grad.shape[1]

    def over_mp(array, flip):
        return lax.ppermute(array, "mp", [(i, i ^ flip) for i in range(lanes)])

    def over_x(array):
        return lax.ppermute(array, "ctx", [(i, i ^ 1) for i in range(length)])

    def over_z(array, first):
        pairs = []
        for position in range(length):
            block = position // 2
            other = ((block - first) ^ 1) + first
            for lane in range(lanes):
                source = position * lanes + lane
                if block >= first and other < blocks:
                    target = (2 * other + position % 2) * lanes + lane
                else:
                    target = position * lanes + (lane ^ 1)
                pairs.append((source, target))
        return lax.ppermute(array, ("ctx", "mp"), pairs)

    y = over_mp(out_grad, 2)
    near = over_mp(out_grad, 1)
    keep, send_kv, send_q = pack(queries, keys, values)
    xkv, xq = over_x(send_kv), over_x(send_q)
    e0, o0 = over_z(keep, 0), over_z(keep, 1)
    acc, wy, wf = first_piece(out_grad, near, out_weight)
    e1, o1 = over_z(xkv, 0), over_z(xkv, 1)
    acc = after(acc, xkv, xq, flops=1e8)
    y, acc = lax.optimization_barrier((y, acc))
    far = over_mp(y, 1)
    acc = grad_piece(acc, y, wy, False)
    acc = after(acc, e0, o0, flops=3e9)
    dkeep, dsend = grad_piece(acc, far, wf, True)
    dxr = after(over_x(dsend), flops=6e9)

    late_q, dxr = lax.optimization_barrier((xq, dxr))
    qe, qo = over_z(late_q, 0), over_z(late_q, 1)
    own_d, e1, o1 = lax.optimization_barrier((dkeep, e1, o1))
    late = join(own_d, dxr)
    late_e, late_o = over_z(late, 0), over_z(late, 1)
    dq_send, marks = query_pass(False, xq, dxr, keep, xkv, e1, o1, e0, o0)
    dq_keep, stats = query_pass(True, keep, dkeep, keep, xkv, e0, o0, e1, o1, marks)
    dq_got = after(over_x(dq_send), flops=6e9)
    stats, qe, qo = lax.optimization_barrier((stats, qe, qo))
    se, so = over_z(stats, 0), over_z(stats, 1)
    sums = own_pass(xkv, keep, xq, dkeep, dxr, stats)
    sums = after(sums, late_e, late_o, flops=3e9)
    own_sums = own_pass(keep, keep, xq, dkeep, dxr, stats)
    heads = dkeep.shape[1] // HD
    theirs = (e0, o0, qe, qo, late_e, late_o, se, so)
    got = []
    for head in range(heads):
        if head == 1:
            dq, = unpack(dq_keep, dq_got)
            sums, dq = lax.optimization_barrier((sums, dq))
        got.append(over_x(key_pass(False, (head,), xkv, *theirs, sums)))
    kv_keep = key_pass(True, tuple(range(heads)), keep, *theirs, own_sums)
    *early, last = got
    dk, dv = unpack(kv_keep, *early)
    return (dq, *finish(dk, dv, last))


def solution(mesh):
    placed = (P("ctx", "mp"), P("ctx", "mp"), P("ctx", "mp"), P("ctx", "mp"), P("mp", None))
    return jax.shard_map(
        body,
        mesh=mesh,
        in_specs=placed,
        out_specs=(P("ctx", "mp"), P("ctx", "mp"), P("ctx", "mp")),
        check_vma=False,
    )
```

```python
import functools
import math

import jax
import jax.numpy as jnp
from jax import lax
from jax.experimental import pallas as pl
from jax.experimental.pallas import tpu as pltpu
from jax.sharding import PartitionSpec as P

HD = 128
BF16 = jnp.bfloat16
F32 = jnp.float32
BIG = 1e30
ANY = pl.BlockSpec(memory_space=pl.ANY)
VM = pl.BlockSpec(memory_space=pltpu.VMEM)
HBM = pl.BlockSpec(memory_space=pltpu.HBM)


def params(mib=40):
    return pltpu.CompilerParams(vmem_limit_bytes=mib << 20)


def nt(a, b):
    return lax.dot_general(a, b, (((1,), (1,)), ((), ())), preferred_element_type=F32)


def nn(a, b):
    return lax.dot_general(a, b, (((1,), (0,)), ((), ())), preferred_element_type=F32)


def cost(flops=1):
    return pl.CostEstimate(flops=int(flops), bytes_accessed=1, transcendentals=0)


def pack_kernel(q, k, v, keep, send_kv, send_q, sem):
    half = q.shape[1] // 2
    x = lax.rem(lax.axis_index("ctx"), 2)
    mine = pl.ds(pl.multiple_of(x * half, half), half)
    theirs = pl.ds(pl.multiple_of((1 - x) * half, half), half)
    pairs = (
        (k.at[:, theirs], send_kv.at[0]),
        (v.at[:, theirs], send_kv.at[1]),
        (k.at[:, mine], keep.at[0]),
        (v.at[:, mine], keep.at[1]),
        (q.at[:, mine], keep.at[2]),
        (q.at[:, theirs], send_q),
    )
    copies = [pltpu.make_async_copy(a, b, sem.at[i]) for i, (a, b) in enumerate(pairs)]
    for copy in copies:
        copy.start()
    for copy in copies:
        copy.wait()


def pack(q, k, v):
    rows, cols = q.shape
    three, two = (jax.ShapeDtypeStruct((n, rows, cols // 2), BF16) for n in (3, 2))
    one = jax.ShapeDtypeStruct((rows, cols // 2), BF16)
    return pl.pallas_call(
        pack_kernel,
        out_shape=(three, two, one),
        in_specs=[ANY] * 3,
        out_specs=(VM,) * 3,
        scratch_shapes=[pltpu.SemaphoreType.DMA((6,))],
        compiler_params=params(60),
        cost_estimate=cost(),
        name="pack",
    )(q, k, v)


def join_kernel(*refs):
    for i, ref in enumerate(refs[:-1]):
        refs[-1][i] = ref[...]


def join(*pieces):
    return pl.pallas_call(
        join_kernel,
        out_shape=jax.ShapeDtypeStruct((len(pieces), *pieces[0].shape), BF16),
        in_specs=[VM] * len(pieces),
        out_specs=VM,
        compiler_params=params(16),
        cost_estimate=cost(),
        name="join",
    )(*pieces)


def first_kernel(og, near, w, acc, wy, wf, wbuf, sem):
    width = og.shape[1]
    me = lax.axis_index("mp")
    copies = []
    for flip, target in enumerate((wbuf.at[0], wbuf.at[1], wy, wf)):
        first = pl.multiple_of(jnp.bitwise_xor(me, flip) * width, width)
        copies.append(pltpu.make_async_copy(w.at[:, pl.ds(first, width)], target, sem.at[flip]))
    for copy in copies:
        copy.start()
    copies[0].wait()
    acc[...] = nt(og[...], wbuf[0])
    copies[1].wait()
    acc[...] += nt(near[...], wbuf[1])
    copies[2].wait()
    copies[3].wait()


def first_piece(og, near, w):
    rows, width = og.shape
    heads = w.shape[0]
    part = jax.ShapeDtypeStruct((heads, width), BF16)
    return pl.pallas_call(
        first_kernel,
        out_shape=(jax.ShapeDtypeStruct((rows, heads), F32), part, part),
        in_specs=[VM, VM, ANY],
        out_specs=(VM, VM, VM),
        scratch_shapes=[pltpu.VMEM((2, heads, width), BF16), pltpu.SemaphoreType.DMA((4,))],
        compiler_params=params(46),
        cost_estimate=cost(),
        name="head_grad_first",
    )(og, near, w)


def next_kernel(acc, piece, w, out):
    out[...] = acc[...] + nt(piece[...], w[...])


def last_kernel(acc, piece, w, keep, send):
    total = acc[...] + nt(piece[...], w[...])
    half = total.shape[1] // 2
    x = lax.rem(lax.axis_index("ctx"), 2)
    low = total[:, :half].astype(BF16)
    high = total[:, half:].astype(BF16)

    @pl.when(x == 0)
    def _():
        keep[...] = low
        send[...] = high

    @pl.when(x != 0)
    def _():
        keep[...] = high
        send[...] = low


def grad_piece(acc, piece, w, last):
    rows, heads = acc.shape
    half = jax.ShapeDtypeStruct((rows, heads // 2), BF16)
    return pl.pallas_call(
        last_kernel if last else next_kernel,
        out_shape=(half, half) if last else jax.ShapeDtypeStruct((rows, heads), F32),
        in_specs=[VM] * 3,
        out_specs=(VM, VM) if last else VM,
        compiler_params=params(30),
        cost_estimate=cost(),
        name="head_grad",
    )(acc, piece, w)


def after(value, *others, flops):
    return pl.pallas_call(
        lambda *refs: None,
        out_shape=jax.ShapeDtypeStruct(value.shape, value.dtype),
        in_specs=[ANY] * (1 + len(others)),
        out_specs=ANY,
        input_output_aliases={0: 0},
        compiler_params=params(16),
        cost_estimate=cost(flops),
        name="after",
    )(value, *others)


def place():
    position = lax.axis_index("ctx")
    block = position // 2
    low_ok = block > 0
    high_ok = block < lax.axis_size("ctx") // 2 - 1
    odd = lax.rem(block, 2) == 1
    even_ok = jnp.logical_or(jnp.logical_and(odd, low_ok), jnp.logical_and(jnp.logical_not(odd), high_ok))
    odd_ok = jnp.logical_or(jnp.logical_and(odd, high_ok), jnp.logical_and(jnp.logical_not(odd), low_ok))
    turned = lax.rem(position + block, 2) == 1
    return even_ok, odd_ok, turned


def off(ok):
    return jnp.where(ok, 0.0, BIG).astype(F32)


def query_kernel(scale, own, has_marks, *refs):
    refs = list(refs)
    q, d, keep, xr, e, o, e_other, o_other = refs[:8]
    q = q if len(q.shape) == 2 else q.at[2]
    before = refs[8] if has_marks else None
    out, stats, fifth = refs[-3:]
    rows = q.shape[0]
    heads = q.shape[1] // HD
    even_ok, odd_ok, turned = place()
    from_even = turned if own else jnp.logical_not(turned)

    @pl.when(from_even)
    def _():
        fifth[...] = e_other[0:2]

    @pl.when(jnp.logical_not(from_even))
    def _():
        fifth[...] = o_other[0:2]

    c = scale * math.log2(math.e)
    even_off, odd_off = off(even_ok), off(odd_ok)
    lane = lax.broadcasted_iota(jnp.int32, (rows, HD), 1)
    runs = (
        (keep, None),
        (xr, None),
        (e, even_off),
        (o, odd_off),
        (fifth, jnp.where(from_even, even_off, odd_off)),
    )
    mark = jnp.zeros((rows, HD), F32)
    for head in range(heads):
        cols = slice(head * HD, (head + 1) * HD)
        query = q[:, cols]
        grad = d[:, cols]
        scores = [nt(query, ref[0, :, cols]) for ref, _ in runs]
        top = None
        for s, (_, gone) in zip(scores, runs):
            m = jnp.max(s, -1, keepdims=True)
            m = m if gone is None else m - gone
            top = m if top is None else jnp.maximum(top, m)
        top = top * c
        weights = [
            jnp.exp2(s * c - (top if gone is None else top + gone))
            for s, (_, gone) in zip(scores, runs)
        ]
        total = jnp.sum(sum(weights), -1, keepdims=True)
        grads = [nt(grad, ref[1, :, cols]) for ref, _ in runs]
        inverse = 1.0 / total
        delta = jnp.sum(sum(w * g for w, g in zip(weights, grads)), -1, keepdims=True) * inverse
        result = sum(
            nn((w * (g - delta)).astype(BF16), ref[0, :, cols])
            for w, g, (ref, _) in zip(weights, grads, runs)
        )
        out[0, :, cols] = (result * (inverse * scale)).astype(BF16)
        mark = jnp.where(lane == 2 * head, top + jnp.log2(total), mark)
        mark = jnp.where(lane == 2 * head + 1, delta, mark)
    marks = jnp.transpose(mark)[: stats.shape[0], :]
    if has_marks:
        stats[:, :rows] = marks
        stats[:, rows:] = before[...]
    else:
        stats[...] = marks


def query_pass(own, q, d, keep, xr, e, o, e_other, o_other, before=None):
    rows, cols = d.shape
    operands = [q, d, keep, xr, e, o, e_other, o_other]
    if before is not None:
        operands.append(before)
    return pl.pallas_call(
        functools.partial(query_kernel, HD ** -0.5, own, before is not None),
        out_shape=(
            jax.ShapeDtypeStruct((1, rows, cols), BF16),
            jax.ShapeDtypeStruct((8, rows if before is None else 2 * rows), F32),
        ),
        in_specs=[VM] * len(operands),
        out_specs=(VM, VM),
        scratch_shapes=[pltpu.VMEM((2, rows, cols), BF16)],
        compiler_params=params(30),
        cost_estimate=cost(6e9 if own else 1),
        name="query_pass",
    )(*operands)


def key_step(scale, key, value, steps):
    c = scale * math.log2(math.e)
    key_sum = None
    value_sum = None
    for query, grad, total, delta in steps:
        weight = jnp.exp2(nt(key, query) * c - total)
        change = weight * (nt(value, grad) - delta)
        v = nn(weight.astype(BF16), grad)
        k = nn(change.astype(BF16), query)
        value_sum = v if value_sum is None else value_sum + v
        key_sum = k if key_sum is None else key_sum + k
    return key_sum, value_sum


def own_kernel(scale, keys, keep, xq, dkeep, dxr, stats, sums):
    rows = keep.shape[1]
    heads = keep.shape[2] // HD
    for head in range(heads):
        cols = slice(head * HD, (head + 1) * HD)
        steps = []
        for i, (q, d) in enumerate(((keep.at[2], dkeep), (xq, dxr))):
            span = slice(i * rows, (i + 1) * rows)
            steps.append((
                q[:, cols],
                d[:, cols],
                stats[2 * head : 2 * head + 1, span],
                stats[2 * head + 1 : 2 * head + 2, span],
            ))
        k, v = key_step(scale, keys[0, :, cols], keys[1, :, cols], steps)
        sums[0, :, cols] = k
        sums[1, :, cols] = v


def own_pass(*operands):
    _, rows, cols = operands[0].shape
    return pl.pallas_call(
        functools.partial(own_kernel, HD ** -0.5),
        out_shape=jax.ShapeDtypeStruct((2, rows, cols), F32),
        in_specs=[VM] * 6,
        out_specs=VM,
        compiler_params=params(30),
        cost_estimate=cost(),
        name="own_pass",
    )(*operands)


def key_kernel(scale, own, heads, kv, e0, o0, late_e, late_o, se, so, sums, out, fifth_q, fifth_d):
    rows = kv.shape[1]
    even_ok, odd_ok, turned = place()
    from_even = turned if own else jnp.logical_not(turned)
    even_q, odd_q = (e0.at[2], late_e.at[0]), (o0.at[2], late_o.at[0])
    even_d, odd_d = (late_e.at[1], late_e.at[2]), (late_o.at[1], late_o.at[2])
    same, other = (0, 1) if own else (1, 0)
    wanted = slice(heads[0] * HD, (heads[-1] + 1) * HD)

    @pl.when(from_even)
    def _():
        fifth_q[...] = even_q[other][:, wanted]
        fifth_d[...] = even_d[other][:, wanted]

    @pl.when(jnp.logical_not(from_even))
    def _():
        fifth_q[...] = odd_q[other][:, wanted]
        fifth_d[...] = odd_d[other][:, wanted]

    row = lax.broadcasted_iota(jnp.int32, se.shape, 0)
    nothing = jnp.where(lax.rem(row, 2) == 0, jnp.float32(BIG), jnp.float32(0.0))
    even = jnp.where(even_ok, se[...], nothing)
    odd = jnp.where(odd_ok, so[...], nothing)
    span = slice(same * rows, (same + 1) * rows)
    across = slice(other * rows, (other + 1) * rows)
    fifth = jnp.where(from_even, even[:, across], odd[:, across])
    for i, head in enumerate(heads):
        cols = slice(head * HD, (head + 1) * HD)
        to = slice(i * HD, (i + 1) * HD)
        a, b = 2 * head, 2 * head + 1
        steps = (
            (even_q[same][:, cols], even_d[same][:, cols], even[a : a + 1, span], even[b : b + 1, span]),
            (odd_q[same][:, cols], odd_d[same][:, cols], odd[a : a + 1, span], odd[b : b + 1, span]),
            (fifth_q[:, to], fifth_d[:, to], fifth[a : a + 1], fifth[b : b + 1]),
        )
        k, v = key_step(scale, kv[0, :, cols], kv[1, :, cols], steps)
        out[0, :, to] = ((k + sums[0, :, cols]) * scale).astype(BF16)
        out[1, :, to] = (v + sums[1, :, cols]).astype(BF16)


def key_pass(own, heads, kv, *operands):
    _, rows, _ = kv.shape
    wide = HD * len(heads)
    return pl.pallas_call(
        functools.partial(key_kernel, HD ** -0.5, own, heads),
        out_shape=jax.ShapeDtypeStruct((2, rows, wide), BF16),
        in_specs=[VM] * (1 + len(operands)),
        out_specs=VM,
        scratch_shapes=[pltpu.VMEM((rows, wide), BF16)] * 2,
        compiler_params=params(30),
        cost_estimate=cost(1e9),
        name="key_pass",
    )(kv, *operands)


def unpack_kernel(n_out, kept, *refs):
    got, outs, sem = refs[: -1 - n_out], refs[-1 - n_out : -1], refs[-1]
    half = kept.shape[2]
    x = lax.rem(lax.axis_index("ctx"), 2)
    mine = pl.multiple_of(x * half, half)
    theirs = pl.multiple_of((1 - x) * half, half)
    copies = []
    for i, out in enumerate(outs):
        pairs = [(kept.at[i], out.at[:, pl.ds(mine, half)])]
        first = 0
        for piece in got:
            width = piece.shape[2]
            pairs.append((piece.at[i], out.at[:, pl.ds(theirs + first, width)]))
            first += width
        for a, b in pairs:
            copies.append(pltpu.make_async_copy(a, b, sem.at[len(copies)]))
    for copy in copies:
        copy.start()
    for copy in copies:
        copy.wait()


def unpack(kept, *got):
    n, rows, half = kept.shape
    return pl.pallas_call(
        functools.partial(unpack_kernel, n),
        out_shape=(jax.ShapeDtypeStruct((rows, 2 * half), BF16),) * n,
        in_specs=[VM] * (1 + len(got)),
        out_specs=(ANY,) * n,
        scratch_shapes=[pltpu.SemaphoreType.DMA((n * (1 + len(got)),))],
        compiler_params=params(16),
        cost_estimate=cost(),
        name="unpack",
    )(kept, *got)


def finish_kernel(dk_in, dv_in, last, dk, dv, sem):
    del dk_in, dv_in
    width = last.shape[2]
    half = dk.shape[1] // 2
    x = lax.rem(lax.axis_index("ctx"), 2)
    columns = pl.ds(pl.multiple_of((1 - x) * half + half - width, HD), width)
    copies = [
        pltpu.make_async_copy(last.at[i], out.at[:, columns], sem.at[i])
        for i, out in enumerate((dk, dv))
    ]
    for copy in copies:
        copy.start()
    for copy in copies:
        copy.wait()


def finish(dk, dv, last):
    return pl.pallas_call(
        finish_kernel,
        out_shape=(jax.ShapeDtypeStruct(dk.shape, dk.dtype),) * 2,
        in_specs=[ANY, ANY, VM],
        out_specs=(ANY, ANY),
        input_output_aliases={0: 0, 1: 1},
        scratch_shapes=[pltpu.SemaphoreType.DMA((2,))],
        compiler_params=params(16),
        cost_estimate=cost(),
        name="finish",
    )(dk, dv, last)


def body(queries, keys, values, out_grad, out_weight):
    length = lax.axis_size("ctx")
    lanes = lax.axis_size("mp")
    blocks = length // 2
    width = out_grad.shape[1]

    def over_mp(array, flip):
        return lax.ppermute(array, "mp", [(i, i ^ flip) for i in range(lanes)])

    def over_x(array):
        return lax.ppermute(array, "ctx", [(i, i ^ 1) for i in range(length)])

    def over_z(array, first):
        pairs = []
        for position in range(length):
            block = position // 2
            other = ((block - first) ^ 1) + first
            for lane in range(lanes):
                source = position * lanes + lane
                if block >= first and other < blocks:
                    target = (2 * other + position % 2) * lanes + lane
                else:
                    target = position * lanes + (lane ^ 1)
                pairs.append((source, target))
        return lax.ppermute(array, ("ctx", "mp"), pairs)

    y = over_mp(out_grad, 2)
    near = over_mp(out_grad, 1)
    keep, send_kv, send_q = pack(queries, keys, values)
    xkv, xq = over_x(send_kv), over_x(send_q)
    e0, o0 = over_z(keep, 0), over_z(keep, 1)
    acc, wy, wf = first_piece(out_grad, near, out_weight)
    e1, o1 = over_z(xkv, 0), over_z(xkv, 1)
    acc = after(acc, xkv, xq, flops=1e8)
    y, acc = lax.optimization_barrier((y, acc))
    far = over_mp(y, 1)
    acc = grad_piece(acc, y, wy, False)
    acc = after(acc, e0, o0, flops=3e9)
    dkeep, dsend = grad_piece(acc, far, wf, True)
    dxr = after(over_x(dsend), flops=6e9)

    xq, e1, o1 = lax.optimization_barrier((xq, e1, o1))
    late = join(xq, dkeep, dxr)
    late_e, late_o = over_z(late, 0), over_z(late, 1)
    dq_send, marks = query_pass(False, xq, dxr, keep, xkv, e1, o1, e0, o0)
    dq_keep, stats = query_pass(True, keep, dkeep, keep, xkv, e0, o0, e1, o1, marks)
    dq_got = after(over_x(dq_send), flops=6e9)
    se, so = over_z(stats, 0), over_z(stats, 1)
    sums = own_pass(xkv, keep, xq, dkeep, dxr, stats)
    sums = after(sums, late_e, late_o, flops=3e9)
    own_sums = own_pass(keep, keep, xq, dkeep, dxr, stats)
    heads = dkeep.shape[1] // HD
    theirs = (e0, o0, late_e, late_o, se, so)
    got = []
    for group in ((0,), tuple(range(1, heads))):
        if group[0] == 1:
            dq, = unpack(dq_keep, dq_got)
            sums, dq = lax.optimization_barrier((sums, dq))
        got.append(over_x(key_pass(False, group, xkv, *theirs, sums)))
    kv_keep = key_pass(True, tuple(range(heads)), keep, *theirs, own_sums)
    *early, last = got
    dk, dv = unpack(kv_keep, *early)
    return (dq, *finish(dk, dv, last))


def solution(mesh):
    placed = (P("ctx", "mp"), P("ctx", "mp"), P("ctx", "mp"), P("ctx", "mp"), P("mp", None))
    return jax.shard_map(
        body,
        mesh=mesh,
        in_specs=placed,
        out_specs=(P("ctx", "mp"), P("ctx", "mp"), P("ctx", "mp")),
        check_vma=False,
    )
```
